256 devices in a mesh: tm: 64 (over y_hi, x, z), rows: 4 (over y_lo, core).
Axes of the slice: x: 4, y: 4 (y_hi: 2, y_lo: 2; y = y_hi * 2 + y_lo), z: 8, core: 2. Of those that a mesh axis runs over, the one named last changes fastest.
Arguments:
- frames: bfloat16 [64, 32, 32, 640], P('tm', 'rows'), may hold values from -24 to 24
- conv_weight: bfloat16 [3, 3, 640, 640], replicated, may hold values from -0.078125 to 0.078125
- conv_bias: float32 [640], replicated, may hold values from -1.5 to 1.5
- ref_features: bfloat16 [1024, 640], P('tm'), may hold values from -6 to 6
- w_query: bfloat16 [640, 640], replicated, may hold values from -0.25 to 0.25
- w_key: bfloat16 [640, 640], replicated, may hold values from -0.25 to 0.25
- w_value: bfloat16 [640, 640], replicated, may hold values from -0.25 to 0.25
- w_out: bfloat16 [640, 640], replicated, may hold values from -0.25 to 0.25
- out_bias: float32 [640], replicated, may hold values from -1.5 to 1.5
Outputs:
- hidden: bfloat16 [64, 32, 32, 640], P('tm', 'rows')
- attended: bfloat16 [64, 32, 32, 640], P('tm', 'rows')
The draws below stay inside these ranges and needn't reach their ends.
All inputs are finite; a program needn't handle non-finite values.
Results may differ from the reference program's by a relative error of at most 0.025.
Values may be sent and summed in bfloat16 or wider, within the bound.
A program may use at most 128 MiB of HBM per device.

```python
import math
import jax
import jax.numpy as jnp
from jax import lax

H = 32
W = 32
HEADS = 8
HD = 80
C = 640
FRAMES = 64


def draw_frames(key, part):
    shape = (FRAMES, H, W, C)
    values = jnp.clip(jax.random.normal(jax.random.fold_in(key, 15), shape, jnp.float32), -6.0, 6.0)
    return values.astype(jnp.bfloat16)


def projection_parts(key):
    spread = 1.7 / math.sqrt(C)
    first = jnp.clip(jax.random.normal(jax.random.fold_in(key, 21), (C, C), jnp.float32), -6.0, 6.0) * spread
    second = jnp.clip(jax.random.normal(jax.random.fold_in(key, 22), (C, C), jnp.float32), -6.0, 6.0) * spread
    return (first, second)


def draw_w_query(key, part):
    first, second = projection_parts(key)
    return jnp.clip(first, -0.25, 0.25).astype(jnp.bfloat16)


def draw_w_key(key, part):
    first, second = projection_parts(key)
    values = second
    return jnp.clip(values, -0.25, 0.25).astype(jnp.bfloat16)


def shard_levels(rng, extent, pieces, smallest, largest):
    def one(position, shards_of):
        draws = jax.random.uniform(jax.random.fold_in(jax.random.fold_in(rng, 6), position), (shards_of,), jnp.float32, smallest / len(pieces), largest / len(pieces))
        return jnp.repeat(jnp.exp(draws), extent[position] // shards_of).reshape((-1,) + (1,) * (len(extent) - position - 1))

    loudness = one(*pieces[0])
    for cut in pieces[1:]:
        loudness = loudness * one(*cut)
    return loudness


def gaussian(key, dims, width, limit, pieces=(), held_as=jnp.bfloat16):
    level = shard_levels(key, dims, pieces, -0.22, 0.18) if pieces else 1.0
    entries = jax.random.normal(key, dims, jnp.float32) * width * level
    return jnp.minimum(jnp.maximum(entries, -limit), limit).astype(held_as)


def setup_inputs(seed: int = 0) -> dict:
    key_of = jax.random.split(jax.random.key(seed), 10)
    frames = draw_frames(jax.random.fold_in(key_of[9], 71), 0)
    conv_weight = gaussian(key_of[1], (3, 3, C, C), (9 * C) ** -0.5, 0.078125)
    conv_bias = gaussian(key_of[2], (C,), 0.3, 1.5, (), jnp.float32)
    ref_features = gaussian(key_of[3], (H * W, C), 1.0, 6.0, ((0, 64),))
    w_query = draw_w_query(jax.random.fold_in(key_of[9], 71), 0)
    w_key = draw_w_key(jax.random.fold_in(key_of[9], 71), 0)
    w_value = gaussian(key_of[6], (C, C), C ** -0.5, 0.25)
    w_out = gaussian(key_of[7], (C, C), C ** -0.5, 0.25)
    out_bias = gaussian(key_of[8], (C,), 0.3, 1.5, (), jnp.float32)
    return {"frames": frames, "conv_weight": conv_weight, "conv_bias": conv_bias, "ref_features": ref_features, "w_query": w_query, "w_key": w_key, "w_value": w_value, "w_out": w_out, "out_bias": out_bias}


def attend_head(query_head, key_head, value_head):
    scores = jnp.dot(query_head, key_head.T, preferred_element_type=jnp.float32) * (HD ** -0.5)
    top = jnp.max(scores, axis=1, keepdims=True)
    weights = jnp.exp(scores - top)
    total = jnp.sum(weights, axis=1, keepdims=True)
    summed = jnp.dot(weights.astype(jnp.bfloat16), value_head, preferred_element_type=jnp.float32)
    return summed / total


def reference(frames, conv_weight, conv_bias, ref_features, w_query, w_key, w_value, w_out, out_bias):
    ref_key = jnp.dot(ref_features, w_key, preferred_element_type=jnp.float32).astype(jnp.bfloat16)
    ref_value = jnp.dot(ref_features, w_value, preferred_element_type=jnp.float32).astype(jnp.bfloat16)

    def one_frame(latent):
        activated = jax.nn.silu(latent.astype(jnp.float32)).astype(jnp.bfloat16)
        padded = jnp.pad(activated, ((1, 1), (1, 1), (0, 0)))
        total = jnp.zeros((H * W, C), jnp.float32)
        for row_tap in range(3):
            for col_tap in range(3):
                window = padded[row_tap:row_tap + H, col_tap:col_tap + W].reshape(H * W, C)
                total = total + jnp.dot(window, conv_weight[row_tap, col_tap], preferred_element_type=jnp.float32)
        hidden = (latent.reshape(H * W, C).astype(jnp.float32) + total + conv_bias).astype(jnp.bfloat16)
        query = jnp.dot(hidden, w_query, preferred_element_type=jnp.float32).astype(jnp.bfloat16)
        key = jnp.dot(hidden, w_key, preferred_element_type=jnp.float32).astype(jnp.bfloat16)
        value = jnp.dot(hidden, w_value, preferred_element_type=jnp.float32).astype(jnp.bfloat16)
        keys = jnp.concatenate([key, ref_key], axis=0)
        values = jnp.concatenate([value, ref_value], axis=0)
        query_heads = query.reshape(H * W, HEADS, HD).transpose(1, 0, 2)
        key_heads = keys.reshape(2 * H * W, HEADS, HD).transpose(1, 0, 2)
        value_heads = values.reshape(2 * H * W, HEADS, HD).transpose(1, 0, 2)
        mixed = lax.map(lambda trio: attend_head(trio[0], trio[1], trio[2]), (query_heads, key_heads, value_heads))
        mixed = mixed.transpose(1, 0, 2).reshape(H * W, C).astype(jnp.bfloat16)
        attended = (jnp.dot(mixed, w_out, preferred_element_type=jnp.float32) + out_bias).astype(jnp.bfloat16)
        return hidden.reshape(H, W, C), attended.reshape(H, W, C)

    hidden, attended = lax.map(one_frame, frames)
    return hidden, attended
```

```python
import jax
import jax.numpy as jnp
import numpy as np
from jax import lax
from jax.sharding import Mesh
from jax.sharding import PartitionSpec as P

HD = 80

TM_PARTS = ("y_hi", "x", "z")
ROW_PARTS = ("y_lo", "core")


def distinct(values):
    return len(set(values))


def fine_mesh(mesh):
    devices = np.asarray(mesh.devices)
    tm, rows = devices.shape
    try:
        column = devices[:, 0]
        nx = distinct(d.coords[0] for d in column)
        nz = distinct(d.coords[2] for d in column)
        cores = distinct(d.core_on_chip for d in devices[0])
    except (AttributeError, IndexError, TypeError):
        nx, nz, cores = tm, 1, rows
    if tm % (nx * nz) or rows % cores:
        nx, nz, cores = tm, 1, rows
    shape = (tm // (nx * nz), nx, nz, rows // cores, cores)
    return Mesh(devices.reshape(shape), TM_PARTS + ROW_PARTS)


def gather_in_steps(value, axes, dim):
    for axis in reversed(axes):
        value = lax.all_gather(value, axis, axis=dim, tiled=True)
    return value


def extended(value, axes, dim, width):
    size = 1
    for axis in axes:
        size *= lax.axis_size(axis)
    length = value.shape[dim]
    up = [(i, i + 1) for i in range(size - 1)]
    down = [(j, i) for i, j in up]
    last = lax.slice_in_dim(value, length - width, length, axis=dim)
    initial = lax.slice_in_dim(value, 0, width, axis=dim)
    before = lax.ppermute(last, axes, up)
    after = lax.ppermute(initial, axes, down)
    return jnp.concatenate([before, value, after], axis=dim)


def attend(query, keys, values, heads):
    tokens = query.shape[0]
    length = keys.shape[0]
    query_heads = query.reshape(tokens, heads, HD)
    key_heads = keys.reshape(length, heads, HD)
    value_heads = values.reshape(length, heads, HD)
    scores = jnp.einsum(
        "qhd,khd->hqk", query_heads, key_heads, preferred_element_type=jnp.float32
    )
    scores = scores * HD ** (-0.5)
    top = jnp.max(scores, axis=2, keepdims=True)
    weights = jnp.exp(scores - top)
    total = jnp.sum(weights, axis=2)
    summed = jnp.einsum(
        "hqk,khd->qhd",
        weights.astype(jnp.bfloat16),
        value_heads,
        preferred_element_type=jnp.float32,
    )
    mixed = summed / jnp.transpose(total)[..., None]
    return mixed.reshape(tokens, heads * HD).astype(jnp.bfloat16)


def shards(frames, conv_weight, conv_bias, ref_features, w_query, w_key, w_value, w_out, out_bias):
    count, band_rows, width, channels = frames.shape
    heads = channels // HD
    band = band_rows * width
    w_pair = jnp.concatenate([w_key, w_value], axis=1)
    ref_pair = jnp.dot(ref_features, w_pair, preferred_element_type=jnp.float32).astype(
        jnp.bfloat16
    )
    every_pair = gather_in_steps(ref_pair, TM_PARTS, 0)
    activated = jax.nn.silu(frames.astype(jnp.float32)).astype(jnp.bfloat16)
    padded = extended(activated, ROW_PARTS, 1, 1)
    padded = jnp.pad(padded, ((0, 0), (0, 0), (1, 1), (0, 0)))
    convolved = jnp.zeros((count * band, channels), jnp.float32)
    for row_tap in range(3):
        for col_tap in range(3):
            window = padded[:, row_tap : row_tap + band_rows, col_tap : col_tap + width].reshape(
                count * band, channels
            )
            convolved = convolved + jnp.dot(
                window, conv_weight[row_tap, col_tap], preferred_element_type=jnp.float32
            )
    hidden = (
        frames.reshape(count * band, channels).astype(jnp.float32) + convolved + conv_bias
    ).astype(jnp.bfloat16)
    whole = gather_in_steps(hidden, ROW_PARTS, 0)
    query = jnp.dot(hidden, w_query, preferred_element_type=jnp.float32).astype(jnp.bfloat16)
    pair = jnp.dot(whole, w_pair, preferred_element_type=jnp.float32).astype(jnp.bfloat16)
    keys = jnp.concatenate([pair[:, :channels], every_pair[:, :channels]], axis=0)
    values = jnp.concatenate([pair[:, channels:], every_pair[:, channels:]], axis=0)
    mixed = attend(query, keys, values, heads)
    attended = (jnp.dot(mixed, w_out, preferred_element_type=jnp.float32) + out_bias).astype(
        jnp.bfloat16
    )
    return (
        hidden.reshape(count, band_rows, width, channels),
        attended.reshape(count, band_rows, width, channels),
    )


def solution(mesh):
    fine = fine_mesh(mesh)
    blocks = P(TM_PARTS, ROW_PARTS, None, None)
    return jax.shard_map(
        shards,
        mesh=fine,
        in_specs=(blocks, P(), P(), P(TM_PARTS, None), P(), P(), P(), P(), P()),
        out_specs=(blocks, blocks),
        check_vma=False,
    )
```

```python
import functools

import jax
import jax.numpy as jnp
from jax import lax
from jax.experimental import pallas as pl
from jax.experimental.pallas import tpu as pltpu
from jax.sharding import PartitionSpec as P

HD = 80


MESH = pl.DeviceIdType.MESH


def gather_kernel(axis, other, size, x_ref, out_ref, local_sem, send_sem, recv_sem):
    me = lax.axis_index(axis)
    there = lax.axis_index(other)

    def device(peer):
        return {axis: peer, other: there}

    barrier = pltpu.get_barrier_semaphore()

    def greet(step, carry):
        peer = lax.rem(me + step, size)
        pl.semaphore_signal(barrier, inc=1, device_id=device(peer), device_id_type=MESH)
        return carry

    lax.fori_loop(1, size, greet, 0)
    pl.semaphore_wait(barrier, size - 1)

    def remote(step):
        return pltpu.make_async_remote_copy(
            src_ref=x_ref,
            dst_ref=out_ref.at[me],
            send_sem=send_sem.at[step],
            recv_sem=recv_sem.at[step],
            device_id=device(lax.rem(me + step, size)),
            device_id_type=MESH,
        )

    def launch(step, carry):
        remote(step).start()
        return carry

    lax.fori_loop(1, size, launch, 0)
    local = pltpu.make_async_copy(x_ref, out_ref.at[me], local_sem)
    local.start()
    local.wait()

    def finish(step, carry):
        remote(step).wait()
        return carry

    lax.fori_loop(1, size, finish, 0)


def gather_all(value, axis, other, collective):
    size = lax.axis_size(axis)
    return pl.pallas_call(
        functools.partial(gather_kernel, axis, other, size),
        out_shape=jax.ShapeDtypeStruct((size,) + value.shape, value.dtype),
        in_specs=[pl.BlockSpec(memory_space=pl.ANY)],
        out_specs=pl.BlockSpec(memory_space=pl.ANY),
        scratch_shapes=[
            pltpu.SemaphoreType.DMA,
            pltpu.SemaphoreType.DMA((size,)),
            pltpu.SemaphoreType.DMA((size,)),
        ],
        compiler_params=pltpu.CompilerParams(collective_id=collective, has_side_effects=True),
    )(value)


def extended(value, axis, dim, width):
    size = lax.axis_size(axis)
    length = value.shape[dim]
    up = [(i, i + 1) for i in range(size - 1)]
    down = [(j, i) for i, j in up]
    last = lax.slice_in_dim(value, length - width, length, axis=dim)
    initial = lax.slice_in_dim(value, 0, width, axis=dim)
    before = lax.ppermute(last, axis, up)
    after = lax.ppermute(initial, axis, down)
    return jnp.concatenate([before, value, after], axis=dim)


def attend(query, keys, values, heads):
    tokens = query.shape[0]
    length = keys.shape[0]
    query_heads = query.reshape(tokens, heads, HD)
    key_heads = keys.reshape(length, heads, HD)
    value_heads = values.reshape(length, heads, HD)
    scores = jnp.einsum(
        "qhd,khd->hqk", query_heads, key_heads, preferred_element_type=jnp.float32
    )
    scores = scores * HD ** (-0.5)
    top = jnp.max(scores, axis=2, keepdims=True)
    weights = jnp.exp(scores - top)
    total = jnp.sum(weights, axis=2)
    summed = jnp.einsum(
        "hqk,khd->qhd",
        weights.astype(jnp.bfloat16),
        value_heads,
        preferred_element_type=jnp.float32,
    )
    mixed = summed / jnp.transpose(total)[..., None]
    return mixed.reshape(tokens, heads * HD).astype(jnp.bfloat16)


def shards(frames, conv_weight, conv_bias, ref_features, w_query, w_key, w_value, w_out, out_bias):
    count, band_rows, width, channels = frames.shape
    heads = channels // HD
    band = band_rows * width
    w_pair = jnp.concatenate([w_key, w_value], axis=1)
    every_feature = gather_all(ref_features, "tm", "rows", 0)
    every_feature = every_feature.reshape(-1, channels)
    every_pair = jnp.dot(every_feature, w_pair, preferred_element_type=jnp.float32).astype(
        jnp.bfloat16
    )
    activated = jax.nn.silu(frames.astype(jnp.float32)).astype(jnp.bfloat16)
    padded = extended(activated, "rows", 1, 1)
    padded = jnp.pad(padded, ((0, 0), (0, 0), (1, 1), (0, 0)))
    convolved = jnp.zeros((count * band, channels), jnp.float32)
    for row_tap in range(3):
        for col_tap in range(3):
            window = padded[:, row_tap : row_tap + band_rows, col_tap : col_tap + width].reshape(
                count * band, channels
            )
            convolved = convolved + jnp.dot(
                window, conv_weight[row_tap, col_tap], preferred_element_type=jnp.float32
            )
    hidden = (
        frames.reshape(count * band, channels).astype(jnp.float32) + convolved + conv_bias
    ).astype(jnp.bfloat16)
    whole = gather_all(hidden, "rows", "tm", 1).reshape(-1, channels)
    query = jnp.dot(hidden, w_query, preferred_element_type=jnp.float32).astype(jnp.bfloat16)
    pair = jnp.dot(whole, w_pair, preferred_element_type=jnp.float32).astype(jnp.bfloat16)
    keys = jnp.concatenate([pair[:, :channels], every_pair[:, :channels]], axis=0)
    values = jnp.concatenate([pair[:, channels:], every_pair[:, channels:]], axis=0)
    mixed = attend(query, keys, values, heads)
    attended = (jnp.dot(mixed, w_out, preferred_element_type=jnp.float32) + out_bias).astype(
        jnp.bfloat16
    )
    return (
        hidden.reshape(count, band_rows, width, channels),
        attended.reshape(count, band_rows, width, channels),
    )


def solution(mesh):
    blocks = P("tm", "rows", None, None)
    return jax.shard_map(
        shards,
        mesh=mesh,
        in_specs=(blocks, P(), P(), P("tm", None), P(), P(), P(), P(), P()),
        out_specs=(blocks, blocks),
        check_vma=False,
    )
```

```python
import jax
import jax.numpy as jnp
from jax import lax
from jax.sharding import PartitionSpec as P

HD = 80


def extended(value, axis, dim, width):
    size = lax.axis_size(axis)
    length = value.shape[dim]
    up = [(i, i + 1) for i in range(size - 1)]
    down = [(j, i) for i, j in up]
    last = lax.slice_in_dim(value, length - width, length, axis=dim)
    initial = lax.slice_in_dim(value, 0, width, axis=dim)
    before = lax.ppermute(last, axis, up)
    after = lax.ppermute(initial, axis, down)
    return jnp.concatenate([before, value, after], axis=dim)


def attend_block(state, query_heads, keys, values, heads):
    top, total, summed = state
    length = keys.shape[0]
    key_heads = keys.reshape(length, heads, HD)
    value_heads = values.reshape(length, heads, HD)
    scores = jnp.einsum(
        "qhd,khd->hqk", query_heads, key_heads, preferred_element_type=jnp.float32
    )
    scores = scores * HD ** (-0.5)
    block_top = jnp.max(scores, axis=2)
    new_top = block_top if top is None else jnp.maximum(top, block_top)
    weights = jnp.exp(scores - new_top[..., None])
    block_total = jnp.sum(weights, axis=2)
    product = jnp.einsum(
        "hqk,khd->hqd",
        weights.astype(jnp.bfloat16),
        value_heads,
        preferred_element_type=jnp.float32,
    )
    if top is None:
        return (new_top, block_total, product)
    factor = jnp.exp(top - new_top)
    return (new_top, total * factor + block_total, summed * factor[..., None] + product)


def doubling_gather(value, axis):
    size = lax.axis_size(axis)
    step = 1
    while step < size:
        pairs = [(j, j ^ step) for j in range(size)]
        value = jnp.concatenate([value, lax.ppermute(value, axis, pairs)], axis=0)
        step *= 2
    return value


def shards(frames, conv_weight, conv_bias, ref_features, w_query, w_key, w_value, w_out, out_bias):
    count, band_rows, width, channels = frames.shape
    heads = channels // HD
    band = band_rows * width
    w_pair = jnp.concatenate([w_key, w_value], axis=1)
    every_feature = doubling_gather(ref_features, "tm")
    activated = jax.nn.silu(frames.astype(jnp.float32)).astype(jnp.bfloat16)
    padded = extended(activated, "rows", 1, 1)
    padded = jnp.pad(padded, ((0, 0), (0, 0), (1, 1), (0, 0)))
    convolved = jnp.zeros((count * band, channels), jnp.float32)
    for row_tap in range(3):
        for col_tap in range(3):
            window = padded[:, row_tap : row_tap + band_rows, col_tap : col_tap + width].reshape(
                count * band, channels
            )
            convolved = convolved + jnp.dot(
                window, conv_weight[row_tap, col_tap], preferred_element_type=jnp.float32
            )
    hidden = (
        frames.reshape(count * band, channels).astype(jnp.float32) + convolved + conv_bias
    ).astype(jnp.bfloat16)
    rows = lax.axis_size("rows")
    others = jnp.concatenate(
        [
            lax.ppermute(hidden, "rows", [(j, (j + shift) % rows) for j in range(rows)])
            for shift in range(1, rows)
        ],
        axis=0,
    )
    query = jnp.dot(hidden, w_query, preferred_element_type=jnp.float32).astype(jnp.bfloat16)
    query_heads = query.reshape(band, heads, HD)
    state = (None, None, None)
    for source in (hidden, others, every_feature):
        pair = jnp.dot(source, w_pair, preferred_element_type=jnp.float32).astype(jnp.bfloat16)
        state = attend_block(state, query_heads, pair[:, :channels], pair[:, channels:], heads)
    top, total, summed = state
    mixed = summed / total[..., None]
    mixed = jnp.transpose(mixed, (1, 0, 2)).reshape(band, channels).astype(jnp.bfloat16)
    attended = (jnp.dot(mixed, w_out, preferred_element_type=jnp.float32) + out_bias).astype(
        jnp.bfloat16
    )
    return (
        hidden.reshape(count, band_rows, width, channels),
        attended.reshape(count, band_rows, width, channels),
    )


def solution(mesh):
    blocks = P("tm", "rows", None, None)
    return jax.shard_map(
        shards,
        mesh=mesh,
        in_specs=(blocks, P(), P(), P("tm", None), P(), P(), P(), P(), P()),
        out_specs=(blocks, blocks),
        check_vma=False,
    )
```

```python
import functools

import jax
import jax.numpy as jnp
import numpy as np
from jax import lax
from jax.experimental import pallas as pl
from jax.experimental.pallas import tpu as pltpu
from jax.sharding import Mesh
from jax.sharding import PartitionSpec as P

HD = 80


MESH = pl.DeviceIdType.MESH
TM_PARTS = ("y_hi", "x", "z")
ROW_PARTS = ("y_lo", "core")


def distinct(values):
    return len(set(values))


def fine_mesh(mesh):
    devices = np.asarray(mesh.devices)
    tm, rows = devices.shape
    try:
        column = devices[:, 0]
        nx = distinct(d.coords[0] for d in column)
        nz = distinct(d.coords[2] for d in column)
        cores = distinct(d.core_on_chip for d in devices[0])
    except (AttributeError, IndexError, TypeError):
        nx, nz, cores = tm, 1, rows
    if tm % (nx * nz) or rows % cores:
        nx, nz, cores = tm, 1, rows
    shape = (tm // (nx * nz), nx, nz, rows // cores, cores)
    return Mesh(devices.reshape(shape), TM_PARTS + ROW_PARTS)


def staged_kernel(sizes, x_ref, out_ref, local_sem, *sems):
    where = [lax.axis_index(axis) for axis in TM_PARTS]
    strides = [sizes[1] * sizes[2], sizes[2], 1]
    me = where[0] * strides[0] + where[1] * strides[1] + where[2]
    barrier = pltpu.get_barrier_semaphore()
    greeted = 0
    for level in (2, 1, 0):
        for shift in range(1, sizes[level]):
            peer = lax.rem(where[level] + shift, sizes[level])
            pl.semaphore_signal(
                barrier, inc=1, device_id={TM_PARTS[level]: peer}, device_id_type=MESH
            )
            greeted += 1
    pl.semaphore_wait(barrier, greeted)
    local = pltpu.make_async_copy(x_ref, out_ref.at[pl.ds(me, 1)], local_sem)
    local.start()
    local.wait()
    for stage, level in enumerate((2, 1, 0)):
        span = strides[level]
        first = me - lax.rem(me, span)
        held = out_ref.at[pl.ds(first, span)]
        send_sem, recv_sem = sems[2 * stage], sems[2 * stage + 1]
        copies = []
        for shift in range(1, sizes[level]):
            peer = lax.rem(where[level] + shift, sizes[level])
            copy = pltpu.make_async_remote_copy(
                src_ref=held,
                dst_ref=held,
                send_sem=send_sem.at[shift],
                recv_sem=recv_sem.at[shift],
                device_id={TM_PARTS[level]: peer},
                device_id_type=MESH,
            )
            copy.start()
            copies.append(copy)
        for copy in copies:
            copy.wait()


def staged_gather(value):
    sizes = [lax.axis_size(axis) for axis in TM_PARTS]
    total = sizes[0] * sizes[1] * sizes[2]
    sems = []
    for level in (2, 1, 0):
        sems += [pltpu.SemaphoreType.DMA((sizes[level],))] * 2
    gathered = pl.pallas_call(
        functools.partial(staged_kernel, sizes),
        out_shape=jax.ShapeDtypeStruct((total,) + value.shape, value.dtype),
        in_specs=[pl.BlockSpec(memory_space=pl.ANY)],
        out_specs=pl.BlockSpec(memory_space=pl.ANY),
        scratch_shapes=[pltpu.SemaphoreType.DMA] + sems,
        compiler_params=pltpu.CompilerParams(collective_id=0, has_side_effects=True),
    )(value[None])
    return gathered.reshape((total * value.shape[0],) + value.shape[1:])


def extended(value, axis, dim, width):
    size = lax.axis_size(axis)
    length = value.shape[dim]
    up = [(i, i + 1) for i in range(size - 1)]
    down = [(j, i) for i, j in up]
    last = lax.slice_in_dim(value, length - width, length, axis=dim)
    initial = lax.slice_in_dim(value, 0, width, axis=dim)
    before = lax.ppermute(last, axis, up)
    after = lax.ppermute(initial, axis, down)
    return jnp.concatenate([before, value, after], axis=dim)


def attend_block(state, query_heads, keys, values, heads):
    top, total, summed = state
    length = keys.shape[0]
    key_heads = keys.reshape(length, heads, HD)
    value_heads = values.reshape(length, heads, HD)
    scores = jnp.einsum(
        "qhd,khd->hqk", query_heads, key_heads, preferred_element_type=jnp.float32
    )
    scores = scores * HD ** (-0.5)
    block_top = jnp.max(scores, axis=2)
    new_top = block_top if top is None else jnp.maximum(top, block_top)
    weights = jnp.exp(scores - new_top[..., None])
    block_total = jnp.sum(weights, axis=2)
    product = jnp.einsum(
        "hqk,khd->hqd",
        weights.astype(jnp.bfloat16),
        value_heads,
        preferred_element_type=jnp.float32,
    )
    if top is None:
        return (new_top, block_total, product)
    factor = jnp.exp(top - new_top)
    return (new_top, total * factor + block_total, summed * factor[..., None] + product)


def doubling_gather(value, axis):
    size = lax.axis_size(axis)
    step = 1
    while step < size:
        pairs = [(j, j ^ step) for j in range(size)]
        value = jnp.concatenate([value, lax.ppermute(value, axis, pairs)], axis=0)
        step *= 2
    return value


def shards(frames, conv_weight, conv_bias, ref_features, w_query, w_key, w_value, w_out, out_bias):
    count, band_rows, width, channels = frames.shape
    heads = channels // HD
    band = band_rows * width
    w_pair = jnp.concatenate([w_key, w_value], axis=1)
    every_feature = staged_gather(ref_features)
    activated = jax.nn.silu(frames.astype(jnp.float32)).astype(jnp.bfloat16)
    padded = extended(activated, ROW_PARTS, 1, 1)
    padded = jnp.pad(padded, ((0, 0), (0, 0), (1, 1), (0, 0)))
    convolved = jnp.zeros((count * band, channels), jnp.float32)
    for row_tap in range(3):
        for col_tap in range(3):
            window = padded[:, row_tap : row_tap + band_rows, col_tap : col_tap + width].reshape(
                count * band, channels
            )
            convolved = convolved + jnp.dot(
                window, conv_weight[row_tap, col_tap], preferred_element_type=jnp.float32
            )
    hidden = (
        frames.reshape(count * band, channels).astype(jnp.float32) + convolved + conv_bias
    ).astype(jnp.bfloat16)
    rows = lax.axis_size(ROW_PARTS)
    others = jnp.concatenate(
        [
            lax.ppermute(hidden, ROW_PARTS, [(j, (j + shift) % rows) for j in range(rows)])
            for shift in range(1, rows)
        ],
        axis=0,
    )
    query = jnp.dot(hidden, w_query, preferred_element_type=jnp.float32).astype(jnp.bfloat16)
    query_heads = query.reshape(band, heads, HD)
    state = (None, None, None)
    for source in (hidden, others, every_feature):
        pair = jnp.dot(source, w_pair, preferred_element_type=jnp.float32).astype(jnp.bfloat16)
        state = attend_block(state, query_heads, pair[:, :channels], pair[:, channels:], heads)
    top, total, summed = state
    mixed = summed / total[..., None]
    mixed = jnp.transpose(mixed, (1, 0, 2)).reshape(band, channels).astype(jnp.bfloat16)
    attended = (jnp.dot(mixed, w_out, preferred_element_type=jnp.float32) + out_bias).astype(
        jnp.bfloat16
    )
    return (
        hidden.reshape(count, band_rows, width, channels),
        attended.reshape(count, band_rows, width, channels),
    )


def solution(mesh):
    fine = fine_mesh(mesh)
    blocks = P(TM_PARTS, ROW_PARTS, None, None)
    return jax.shard_map(
        shards,
        mesh=fine,
        in_specs=(blocks, P(), P(), P(TM_PARTS, None), P(), P(), P(), P(), P()),
        out_specs=(blocks, blocks),
        check_vma=False,
    )
```

```python
import functools

import jax
import jax.numpy as jnp
import numpy as np
from jax import lax
from jax.experimental import pallas as pl
from jax.experimental.pallas import tpu as pltpu
from jax.sharding import Mesh
from jax.sharding import PartitionSpec as P

HD = 80


MESH = pl.DeviceIdType.MESH
TM_PARTS = ("y_hi", "x", "z")
ROW_PARTS = ("y_lo", "core")


def distinct(values):
    return len(set(values))


def fine_mesh(mesh):
    devices = np.asarray(mesh.devices)
    tm, rows = devices.shape
    try:
        column = devices[:, 0]
        nx = distinct(d.coords[0] for d in column)
        nz = distinct(d.coords[2] for d in column)
        cores = distinct(d.core_on_chip for d in devices[0])
    except (AttributeError, IndexError, TypeError):
        nx, nz, cores = tm, 1, rows
    if tm % (nx * nz) or rows % cores:
        nx, nz, cores = tm, 1, rows
    shape = (tm // (nx * nz), nx, nz, rows // cores, cores)
    return Mesh(devices.reshape(shape), TM_PARTS + ROW_PARTS)


def staged_kernel(sizes, x_ref, out_ref, local_sem, *sems):
    high, across, along = sizes
    half = along // 2
    yh, xx, zz = [lax.axis_index(axis) for axis in TM_PARTS]
    low, core = [lax.axis_index(axis) for axis in ROW_PARTS]
    me = (yh * across + xx) * along + zz
    mine = me - zz
    other_core = 1 - core
    z_peer = lambda shift: {"z": lax.rem(zz + shift, along)}
    x_peer = lambda shift: {"x": lax.rem(xx + shift, across)}
    y_peer = {"y_hi": 1 - yh, "y_lo": 1 - low}
    c_peer = {"core": other_core}
    peers = [z_peer(s) for s in range(1, along)] + [x_peer(s) for s in range(1, across)]
    peers += [y_peer, c_peer]
    barrier = pltpu.get_barrier_semaphore()
    for peer in peers:
        pl.semaphore_signal(barrier, inc=1, device_id=peer, device_id_type=MESH)
    pl.semaphore_wait(barrier, len(peers))
    local = pltpu.make_async_copy(x_ref, out_ref.at[pl.ds(me, 1)], local_sem)
    local.start()
    local.wait()

    def exchange(pairs, send_sem, recv_sem):
        copies = []
        for index, (ref, peer) in enumerate(pairs):
            copy = pltpu.make_async_remote_copy(
                src_ref=ref,
                dst_ref=ref,
                send_sem=send_sem.at[index],
                recv_sem=recv_sem.at[index],
                device_id=peer,
                device_id_type=MESH,
            )
            copy.start()
            copies.append(copy)
        for copy in copies:
            copy.wait()

    own = out_ref.at[pl.ds(me, 1)]
    exchange([(own, z_peer(s)) for s in range(1, along)], sems[0], sems[1])
    start = mine + core * half
    part = out_ref.at[pl.ds(start, half)]
    exchange([(part, x_peer(s)) for s in range(1, across)], sems[2], sems[3])
    base = yh * across * along + core * half
    chunks = [out_ref.at[pl.ds(base + g * along, half)] for g in range(across)]
    exchange([(chunk, y_peer) for chunk in chunks], sems[4], sems[5])
    regions = high * across
    region = yh * across + xx
    groups = []
    for step in range(1, regions):
        j = lax.rem(region + step, regions)
        groups.append(out_ref.at[pl.ds(j * along + core * half, half)])
    exchange([(chunk, c_peer) for chunk in groups], sems[6], sems[7])


def staged_gather(value):
    sizes = [lax.axis_size(axis) for axis in TM_PARTS]
    total = sizes[0] * sizes[1] * sizes[2]
    sems = []
    for count in (sizes[2], sizes[1], sizes[1], sizes[0] * sizes[1]):
        sems += [pltpu.SemaphoreType.DMA((count,))] * 2
    gathered = pl.pallas_call(
        functools.partial(staged_kernel, sizes),
        out_shape=jax.ShapeDtypeStruct((total,) + value.shape, value.dtype),
        in_specs=[pl.BlockSpec(memory_space=pl.ANY)],
        out_specs=pl.BlockSpec(memory_space=pl.ANY),
        scratch_shapes=[pltpu.SemaphoreType.DMA] + sems,
        compiler_params=pltpu.CompilerParams(collective_id=0, has_side_effects=True),
    )(value[None])
    return gathered.reshape((total * value.shape[0],) + value.shape[1:])


def extended(value, axis, dim, width):
    size = lax.axis_size(axis)
    length = value.shape[dim]
    up = [(i, i + 1) for i in range(size - 1)]
    down = [(j, i) for i, j in up]
    last = lax.slice_in_dim(value, length - width, length, axis=dim)
    initial = lax.slice_in_dim(value, 0, width, axis=dim)
    before = lax.ppermute(last, axis, up)
    after = lax.ppermute(initial, axis, down)
    return jnp.concatenate([before, value, after], axis=dim)


def attend_block(state, query_heads, keys, values, heads):
    top, total, summed = state
    length = keys.shape[0]
    key_heads = keys.reshape(length, heads, HD)
    value_heads = values.reshape(length, heads, HD)
    scores = jnp.einsum(
        "qhd,khd->hqk", query_heads, key_heads, preferred_element_type=jnp.float32
    )
    scores = scores * HD ** (-0.5)
    block_top = jnp.max(scores, axis=2)
    new_top = block_top if top is None else jnp.maximum(top, block_top)
    weights = jnp.exp(scores - new_top[..., None])
    block_total = jnp.sum(weights, axis=2)
    product = jnp.einsum(
        "hqk,khd->hqd",
        weights.astype(jnp.bfloat16),
        value_heads,
        preferred_element_type=jnp.float32,
    )
    if top is None:
        return (new_top, block_total, product)
    factor = jnp.exp(top - new_top)
    return (new_top, total * factor + block_total, summed * factor[..., None] + product)


def doubling_gather(value, axis):
    size = lax.axis_size(axis)
    step = 1
    while step < size:
        pairs = [(j, j ^ step) for j in range(size)]
        value = jnp.concatenate([value, lax.ppermute(value, axis, pairs)], axis=0)
        step *= 2
    return value


def shards(frames, conv_weight, conv_bias, ref_features, w_query, w_key, w_value, w_out, out_bias):
    count, band_rows, width, channels = frames.shape
    heads = channels // HD
    band = band_rows * width
    w_pair = jnp.concatenate([w_key, w_value], axis=1)
    every_feature = staged_gather(ref_features)
    activated = jax.nn.silu(frames.astype(jnp.float32)).astype(jnp.bfloat16)
    padded = extended(activated, ROW_PARTS, 1, 1)
    padded = jnp.pad(padded, ((0, 0), (0, 0), (1, 1), (0, 0)))
    convolved = jnp.zeros((count * band, channels), jnp.float32)
    for row_tap in range(3):
        for col_tap in range(3):
            window = padded[:, row_tap : row_tap + band_rows, col_tap : col_tap + width].reshape(
                count * band, channels
            )
            convolved = convolved + jnp.dot(
                window, conv_weight[row_tap, col_tap], preferred_element_type=jnp.float32
            )
    hidden = (
        frames.reshape(count * band, channels).astype(jnp.float32) + convolved + conv_bias
    ).astype(jnp.bfloat16)
    rows = lax.axis_size(ROW_PARTS)
    others = jnp.concatenate(
        [
            lax.ppermute(hidden, ROW_PARTS, [(j, (j + shift) % rows) for j in range(rows)])
            for shift in range(1, rows)
        ],
        axis=0,
    )
    query = jnp.dot(hidden, w_query, preferred_element_type=jnp.float32).astype(jnp.bfloat16)
    query_heads = query.reshape(band, heads, HD)
    state = (None, None, None)
    for source in (hidden, others, every_feature):
        pair = jnp.dot(source, w_pair, preferred_element_type=jnp.float32).astype(jnp.bfloat16)
        state = attend_block(state, query_heads, pair[:, :channels], pair[:, channels:], heads)
    top, total, summed = state
    mixed = summed / total[..., None]
    mixed = jnp.transpose(mixed, (1, 0, 2)).reshape(band, channels).astype(jnp.bfloat16)
    attended = (jnp.dot(mixed, w_out, preferred_element_type=jnp.float32) + out_bias).astype(
        jnp.bfloat16
    )
    return (
        hidden.reshape(count, band_rows, width, channels),
        attended.reshape(count, band_rows, width, channels),
    )


def solution(mesh):
    fine = fine_mesh(mesh)
    blocks = P(TM_PARTS, ROW_PARTS, None, None)
    return jax.shard_map(
        shards,
        mesh=fine,
        in_specs=(blocks, P(), P(), P(TM_PARTS, None), P(), P(), P(), P(), P()),
        out_specs=(blocks, blocks),
        check_vma=False,
    )
```

```python
import functools

import jax
import jax.numpy as jnp
import numpy as np
from jax import lax
from jax.experimental import pallas as pl
from jax.experimental.pallas import tpu as pltpu
from jax.sharding import Mesh
from jax.sharding import PartitionSpec as P

HD = 80


MESH = pl.DeviceIdType.MESH
TM_PARTS = ("y_hi", "x", "z")
ROW_PARTS = ("y_lo", "core")


def distinct(values):
    return len(set(values))


def fine_mesh(mesh):
    devices = np.asarray(mesh.devices)
    tm, rows = devices.shape
    try:
        column = devices[:, 0]
        nx = distinct(d.coords[0] for d in column)
        nz = distinct(d.coords[2] for d in column)
        cores = distinct(d.core_on_chip for d in devices[0])
    except (AttributeError, IndexError, TypeError):
        nx, nz, cores = tm, 1, rows
    if tm % (nx * nz) or rows % cores:
        nx, nz, cores = tm, 1, rows
    shape = (tm // (nx * nz), nx, nz, rows // cores, cores)
    return Mesh(devices.reshape(shape), TM_PARTS + ROW_PARTS)


def staged_kernel(sizes, x_ref, out_ref, local_sem, *sems):
    high, across, along = sizes
    half = along // 2
    yh, xx, zz = [lax.axis_index(axis) for axis in TM_PARTS]
    low, core = [lax.axis_index(axis) for axis in ROW_PARTS]
    me = (yh * across + xx) * along + zz
    mine = me - zz
    other_core = 1 - core
    z_peer = lambda shift: {"z": lax.rem(zz + shift, along)}
    x_peer = lambda shift: {"x": lax.rem(xx + shift, across)}
    y_peer = {"y_hi": 1 - yh, "y_lo": 1 - low}
    c_peer = {"core": other_core}
    peers = [z_peer(s) for s in range(1, along)] + [x_peer(s) for s in range(1, across)]
    peers += [y_peer, c_peer]
    barrier = pltpu.get_barrier_semaphore()
    for peer in peers:
        pl.semaphore_signal(barrier, inc=1, device_id=peer, device_id_type=MESH)
    pl.semaphore_wait(barrier, len(peers))
    local = pltpu.make_async_copy(x_ref, out_ref.at[pl.ds(me, 1)], local_sem)
    local.start()
    local.wait()

    def exchange(pairs, send_sem, recv_sem):
        copies = []
        for index, (ref, peer) in enumerate(pairs):
            copy = pltpu.make_async_remote_copy(
                src_ref=ref,
                dst_ref=ref,
                send_sem=send_sem.at[index],
                recv_sem=recv_sem.at[index],
                device_id=peer,
                device_id_type=MESH,
            )
            copy.start()
            copies.append(copy)
        for copy in copies:
            copy.wait()

    own = out_ref.at[pl.ds(me, 1)]
    exchange([(own, z_peer(s)) for s in range(1, along)], sems[0], sems[1])
    start = mine + core * half
    part = out_ref.at[pl.ds(start, half)]
    exchange([(part, x_peer(s)) for s in range(1, across)], sems[2], sems[3])
    base = yh * across * along + core * half
    chunks = [out_ref.at[pl.ds(base + g * along, half)] for g in range(across)]
    exchange([(chunk, y_peer) for chunk in chunks], sems[4], sems[5])
    regions = high * across
    region = yh * across + xx
    groups = []
    for step in range(1, regions):
        j = lax.rem(region + step, regions)
        groups.append(out_ref.at[pl.ds(j * along + core * half, half)])
    exchange([(chunk, c_peer) for chunk in groups], sems[6], sems[7])


def staged_gather(value):
    sizes = [lax.axis_size(axis) for axis in TM_PARTS]
    total = sizes[0] * sizes[1] * sizes[2]
    sems = []
    for count in (sizes[2], sizes[1], sizes[1], sizes[0] * sizes[1]):
        sems += [pltpu.SemaphoreType.DMA((count,))] * 2
    gathered = pl.pallas_call(
        functools.partial(staged_kernel, sizes),
        out_shape=jax.ShapeDtypeStruct((total,) + value.shape, value.dtype),
        in_specs=[pl.BlockSpec(memory_space=pl.ANY)],
        out_specs=pl.BlockSpec(memory_space=pl.ANY),
        scratch_shapes=[pltpu.SemaphoreType.DMA] + sems,
        compiler_params=pltpu.CompilerParams(collective_id=0, has_side_effects=True),
    )(value[None])
    return gathered.reshape((total * value.shape[0],) + value.shape[1:])


def extended(value, axis, dim, width):
    size = lax.axis_size(axis)
    length = value.shape[dim]
    up = [(i, i + 1) for i in range(size - 1)]
    down = [(j, i) for i, j in up]
    last = lax.slice_in_dim(value, length - width, length, axis=dim)
    initial = lax.slice_in_dim(value, 0, width, axis=dim)
    before = lax.ppermute(last, axis, up)
    after = lax.ppermute(initial, axis, down)
    return jnp.concatenate([before, value, after], axis=dim)


def attend_block(state, query_heads, keys, values, heads):
    top, total, summed = state
    length = keys.shape[0]
    key_heads = keys.reshape(length, heads, HD)
    value_heads = values.reshape(length, heads, HD)
    scores = jnp.einsum(
        "qhd,khd->hqk", query_heads, key_heads, preferred_element_type=jnp.float32
    )
    scores = scores * HD ** (-0.5)
    block_top = jnp.max(scores, axis=2)
    new_top = block_top if top is None else jnp.maximum(top, block_top)
    weights = jnp.exp(scores - new_top[..., None])
    block_total = jnp.sum(weights, axis=2)
    product = jnp.einsum(
        "hqk,khd->hqd",
        weights.astype(jnp.bfloat16),
        value_heads,
        preferred_element_type=jnp.float32,
    )
    if top is None:
        return (new_top, block_total, product)
    factor = jnp.exp(top - new_top)
    return (new_top, total * factor + block_total, summed * factor[..., None] + product)


def attention_kernel(heads, q_ref, k_ref, v_ref, rk_ref, rv_ref, o_ref):
    for head in range(heads):
        lanes = slice(head * HD, (head + 1) * HD)
        query = q_ref[:, lanes]
        parts = []
        for key_ref, value_ref in ((k_ref, v_ref), (rk_ref, rv_ref)):
            scores = lax.dot_general(
                query,
                key_ref[:, lanes],
                (((1,), (1,)), ((), ())),
                preferred_element_type=jnp.float32,
            )
            parts.append((scores * HD ** (-0.5), value_ref))
        top = jnp.maximum(
            jnp.max(parts[0][0], axis=1, keepdims=True),
            jnp.max(parts[1][0], axis=1, keepdims=True),
        )
        total = None
        summed = None
        for scores, value_ref in parts:
            weights = jnp.exp(scores - top)
            block_total = jnp.sum(weights, axis=1, keepdims=True)
            product = jnp.dot(
                weights.astype(jnp.bfloat16),
                value_ref[:, lanes],
                preferred_element_type=jnp.float32,
            )
            total = block_total if total is None else total + block_total
            summed = product if summed is None else summed + product
        o_ref[:, lanes] = (summed / total).astype(o_ref.dtype)


def attention(query, keys, values, ref_keys, ref_values, heads, tile):
    tokens, channels = query.shape
    whole = lambda array: pl.BlockSpec(array.shape, lambda i: (0, 0))
    return pl.pallas_call(
        functools.partial(attention_kernel, heads),
        out_shape=jax.ShapeDtypeStruct((tokens, channels), jnp.bfloat16),
        grid=(tokens // tile,),
        in_specs=[
            pl.BlockSpec((tile, channels), lambda i: (i, 0)),
            whole(keys),
            whole(values),
            whole(ref_keys),
            whole(ref_values),
        ],
        out_specs=pl.BlockSpec((tile, channels), lambda i: (i, 0)),
    )(query, keys, values, ref_keys, ref_values)


def doubling_gather(value, axis):
    size = lax.axis_size(axis)
    step = 1
    while step < size:
        pairs = [(j, j ^ step) for j in range(size)]
        value = jnp.concatenate([value, lax.ppermute(value, axis, pairs)], axis=0)
        step *= 2
    return value


def shards(frames, conv_weight, conv_bias, ref_features, w_query, w_key, w_value, w_out, out_bias):
    count, band_rows, width, channels = frames.shape
    heads = channels // HD
    band = band_rows * width
    every_feature = staged_gather(ref_features)
    activated = jax.nn.silu(frames.astype(jnp.float32)).astype(jnp.bfloat16)
    padded = extended(activated, ROW_PARTS, 1, 1)
    padded = jnp.pad(padded, ((0, 0), (0, 0), (1, 1), (0, 0)))
    convolved = jnp.zeros((count * band, channels), jnp.float32)
    for row_tap in range(3):
        for col_tap in range(3):
            window = padded[:, row_tap : row_tap + band_rows, col_tap : col_tap + width].reshape(
                count * band, channels
            )
            convolved = convolved + jnp.dot(
                window, conv_weight[row_tap, col_tap], preferred_element_type=jnp.float32
            )
    hidden = (
        frames.reshape(count * band, channels).astype(jnp.float32) + convolved + conv_bias
    ).astype(jnp.bfloat16)
    rows = lax.axis_size(ROW_PARTS)
    others = jnp.concatenate(
        [
            lax.ppermute(hidden, ROW_PARTS, [(j, (j + shift) % rows) for j in range(rows)])
            for shift in range(1, rows)
        ],
        axis=0,
    )
    query = jnp.dot(hidden, w_query, preferred_element_type=jnp.float32).astype(jnp.bfloat16)
    source = jnp.concatenate([hidden, others], axis=0)
    project = lambda rows, weight: jnp.dot(
        rows, weight, preferred_element_type=jnp.float32
    ).astype(jnp.bfloat16)
    mixed = attention(
        query,
        project(source, w_key),
        project(source, w_value),
        project(every_feature, w_key),
        project(every_feature, w_value),
        heads,
        128,
    )
    attended = (jnp.dot(mixed, w_out, preferred_element_type=jnp.float32) + out_bias).astype(
        jnp.bfloat16
    )
    return (
        hidden.reshape(count, band_rows, width, channels),
        attended.reshape(count, band_rows, width, channels),
    )


def solution(mesh):
    fine = fine_mesh(mesh)
    blocks = P(TM_PARTS, ROW_PARTS, None, None)
    return jax.shard_map(
        shards,
        mesh=fine,
        in_specs=(blocks, P(), P(), P(TM_PARTS, None), P(), P(), P(), P(), P()),
        out_specs=(blocks, blocks),
        check_vma=False,
    )
```

```python
import functools

import jax
import jax.numpy as jnp
import numpy as np
from jax import lax
from jax.experimental import pallas as pl
from jax.experimental.pallas import tpu as pltpu
from jax.sharding import Mesh
from jax.sharding import PartitionSpec as P

HD = 80


MESH = pl.DeviceIdType.MESH
TM_PARTS = ("y_hi", "x", "z")
ROW_PARTS = ("y_lo", "core")


def distinct(values):
    return len(set(values))


def fine_mesh(mesh):
    devices = np.asarray(mesh.devices)
    tm, rows = devices.shape
    try:
        column = devices[:, 0]
        nx = distinct(d.coords[0] for d in column)
        nz = distinct(d.coords[2] for d in column)
        cores = distinct(d.core_on_chip for d in devices[0])
    except (AttributeError, IndexError, TypeError):
        nx, nz, cores = tm, 1, rows
    if tm % (nx * nz) or rows % cores:
        nx, nz, cores = tm, 1, rows
    shape = (tm // (nx * nz), nx, nz, rows // cores, cores)
    return Mesh(devices.reshape(shape), TM_PARTS + ROW_PARTS)


def staged_kernel(sizes, x_ref, band_ref, out_ref, whole_ref, local_sem, band_sem, *sems):
    high, across, along = sizes
    half = along // 2
    yh, xx, zz = [lax.axis_index(axis) for axis in TM_PARTS]
    low, core = [lax.axis_index(axis) for axis in ROW_PARTS]
    me = (yh * across + xx) * along + zz
    mine = me - zz
    other_core = 1 - core
    z_peer = lambda shift: {"z": lax.rem(zz + shift, along)}
    x_peer = lambda shift: {"x": lax.rem(xx + shift, across)}
    y_peer = {"y_hi": 1 - yh, "y_lo": 1 - low}
    c_peer = {"core": other_core}
    peers = [z_peer(s) for s in range(1, along)] + [x_peer(s) for s in range(1, across)]
    peers += [y_peer, c_peer]
    cores = lax.axis_size("core")
    bands = lax.axis_size("y_lo") * cores
    band = low * cores + core
    band_peer = lambda shift: {
        "y_lo": lax.rem(band + shift, bands) // cores,
        "core": lax.rem(band + shift, bands) % cores,
    }
    peers += [band_peer(shift) for shift in range(1, bands)]
    barrier = pltpu.get_barrier_semaphore()
    for peer in peers:
        pl.semaphore_signal(barrier, inc=1, device_id=peer, device_id_type=MESH)
    pl.semaphore_wait(barrier, len(peers))
    band_copies = []
    for shift in range(1, bands):
        copy = pltpu.make_async_remote_copy(
            src_ref=band_ref,
            dst_ref=whole_ref.at[band],
            send_sem=sems[8].at[shift],
            recv_sem=sems[9].at[shift],
            device_id=band_peer(shift),
            device_id_type=MESH,
        )
        copy.start()
        band_copies.append(copy)
    own_band = pltpu.make_async_copy(band_ref, whole_ref.at[band], band_sem)
    own_band.start()
    local = pltpu.make_async_copy(x_ref, out_ref.at[pl.ds(me, 1)], local_sem)
    local.start()
    local.wait()

    def exchange(pairs, send_sem, recv_sem):
        copies = []
        for index, (ref, peer) in enumerate(pairs):
            copy = pltpu.make_async_remote_copy(
                src_ref=ref,
                dst_ref=ref,
                send_sem=send_sem.at[index],
                recv_sem=recv_sem.at[index],
                device_id=peer,
                device_id_type=MESH,
            )
            copy.start()
            copies.append(copy)
        for copy in copies:
            copy.wait()

    own = out_ref.at[pl.ds(me, 1)]
    exchange([(own, z_peer(s)) for s in range(1, along)], sems[0], sems[1])
    start = mine + core * half
    part = out_ref.at[pl.ds(start, half)]
    exchange([(part, x_peer(s)) for s in range(1, across)], sems[2], sems[3])
    base = yh * across * along + core * half
    chunks = [out_ref.at[pl.ds(base + g * along, half)] for g in range(across)]
    exchange([(chunk, y_peer) for chunk in chunks], sems[4], sems[5])
    regions = high * across
    region = yh * across + xx
    groups = []
    for step in range(1, regions):
        j = lax.rem(region + step, regions)
        groups.append(out_ref.at[pl.ds(j * along + core * half, half)])
    exchange([(chunk, c_peer) for chunk in groups], sems[6], sems[7])
    own_band.wait()
    for copy in band_copies:
        copy.wait()


def staged_gather(value, hidden):
    sizes = [lax.axis_size(axis) for axis in TM_PARTS]
    total = sizes[0] * sizes[1] * sizes[2]
    bands = lax.axis_size(ROW_PARTS)
    sems = []
    for count in (sizes[2], sizes[1], sizes[1], sizes[0] * sizes[1], bands):
        sems += [pltpu.SemaphoreType.DMA((count,))] * 2
    gathered, whole = pl.pallas_call(
        functools.partial(staged_kernel, sizes),
        out_shape=(
            jax.ShapeDtypeStruct((total,) + value.shape, value.dtype),
            jax.ShapeDtypeStruct((bands,) + hidden.shape, hidden.dtype),
        ),
        in_specs=[pl.BlockSpec(memory_space=pl.ANY)] * 2,
        out_specs=(pl.BlockSpec(memory_space=pl.ANY),) * 2,
        scratch_shapes=[pltpu.SemaphoreType.DMA] * 2 + sems,
        compiler_params=pltpu.CompilerParams(collective_id=0, has_side_effects=True),
    )(value[None], hidden)
    every = gathered.reshape((total * value.shape[0],) + value.shape[1:])
    return every, whole.reshape((bands * hidden.shape[0],) + hidden.shape[1:])


def extended(value, axis, dim, width):
    size = lax.axis_size(axis)
    length = value.shape[dim]
    up = [(i, i + 1) for i in range(size - 1)]
    down = [(j, i) for i, j in up]
    last = lax.slice_in_dim(value, length - width, length, axis=dim)
    initial = lax.slice_in_dim(value, 0, width, axis=dim)
    before = lax.ppermute(last, axis, up)
    after = lax.ppermute(initial, axis, down)
    return jnp.concatenate([before, value, after], axis=dim)


def attend_block(state, query_heads, keys, values, heads):
    top, total, summed = state
    length = keys.shape[0]
    key_heads = keys.reshape(length, heads, HD)
    value_heads = values.reshape(length, heads, HD)
    scores = jnp.einsum(
        "qhd,khd->hqk", query_heads, key_heads, preferred_element_type=jnp.float32
    )
    scores = scores * HD ** (-0.5)
    block_top = jnp.max(scores, axis=2)
    new_top = block_top if top is None else jnp.maximum(top, block_top)
    weights = jnp.exp(scores - new_top[..., None])
    block_total = jnp.sum(weights, axis=2)
    product = jnp.einsum(
        "hqk,khd->hqd",
        weights.astype(jnp.bfloat16),
        value_heads,
        preferred_element_type=jnp.float32,
    )
    if top is None:
        return (new_top, block_total, product)
    factor = jnp.exp(top - new_top)
    return (new_top, total * factor + block_total, summed * factor[..., None] + product)


def attention_kernel(heads, q_ref, k_ref, v_ref, rk_ref, rv_ref, o_ref):
    for head in range(heads):
        lanes = slice(head * HD, (head + 1) * HD)
        query = q_ref[:, lanes]
        parts = []
        for key_ref, value_ref in ((k_ref, v_ref), (rk_ref, rv_ref)):
            scores = lax.dot_general(
                query,
                key_ref[:, lanes],
                (((1,), (1,)), ((), ())),
                preferred_element_type=jnp.float32,
            )
            parts.append((scores * HD ** (-0.5), value_ref))
        top = jnp.maximum(
            jnp.max(parts[0][0], axis=1, keepdims=True),
            jnp.max(parts[1][0], axis=1, keepdims=True),
        )
        total = None
        summed = None
        for scores, value_ref in parts:
            weights = jnp.exp(scores - top)
            block_total = jnp.sum(weights, axis=1, keepdims=True)
            product = jnp.dot(
                weights.astype(jnp.bfloat16),
                value_ref[:, lanes],
                preferred_element_type=jnp.float32,
            )
            total = block_total if total is None else total + block_total
            summed = product if summed is None else summed + product
        o_ref[:, lanes] = (summed / total).astype(o_ref.dtype)


def attention(query, keys, values, ref_keys, ref_values, heads, tile):
    tokens, channels = query.shape
    whole = lambda array: pl.BlockSpec(array.shape, lambda i: (0, 0))
    return pl.pallas_call(
        functools.partial(attention_kernel, heads),
        out_shape=jax.ShapeDtypeStruct((tokens, channels), jnp.bfloat16),
        grid=(tokens // tile,),
        in_specs=[
            pl.BlockSpec((tile, channels), lambda i: (i, 0)),
            whole(keys),
            whole(values),
            whole(ref_keys),
            whole(ref_values),
        ],
        out_specs=pl.BlockSpec((tile, channels), lambda i: (i, 0)),
    )(query, keys, values, ref_keys, ref_values)


def doubling_gather(value, axis):
    size = lax.axis_size(axis)
    step = 1
    while step < size:
        pairs = [(j, j ^ step) for j in range(size)]
        value = jnp.concatenate([value, lax.ppermute(value, axis, pairs)], axis=0)
        step *= 2
    return value


def shards(frames, conv_weight, conv_bias, ref_features, w_query, w_key, w_value, w_out, out_bias):
    count, band_rows, width, channels = frames.shape
    heads = channels // HD
    band = band_rows * width
    activated = jax.nn.silu(frames.astype(jnp.float32)).astype(jnp.bfloat16)
    padded = extended(activated, ROW_PARTS, 1, 1)
    padded = jnp.pad(padded, ((0, 0), (0, 0), (1, 1), (0, 0)))
    convolved = jnp.zeros((count * band, channels), jnp.float32)
    for row_tap in range(3):
        for col_tap in range(3):
            window = padded[:, row_tap : row_tap + band_rows, col_tap : col_tap + width].reshape(
                count * band, channels
            )
            convolved = convolved + jnp.dot(
                window, conv_weight[row_tap, col_tap], preferred_element_type=jnp.float32
            )
    hidden = (
        frames.reshape(count * band, channels).astype(jnp.float32) + convolved + conv_bias
    ).astype(jnp.bfloat16)
    every_feature, source = staged_gather(ref_features, hidden)
    query = jnp.dot(hidden, w_query, preferred_element_type=jnp.float32).astype(jnp.bfloat16)
    project = lambda rows, weight: jnp.dot(
        rows, weight, preferred_element_type=jnp.float32
    ).astype(jnp.bfloat16)
    mixed = attention(
        query,
        project(source, w_key),
        project(source, w_value),
        project(every_feature, w_key),
        project(every_feature, w_value),
        heads,
        128,
    )
    attended = (jnp.dot(mixed, w_out, preferred_element_type=jnp.float32) + out_bias).astype(
        jnp.bfloat16
    )
    return (
        hidden.reshape(count, band_rows, width, channels),
        attended.reshape(count, band_rows, width, channels),
    )


def solution(mesh):
    fine = fine_mesh(mesh)
    blocks = P(TM_PARTS, ROW_PARTS, None, None)
    return jax.shard_map(
        shards,
        mesh=fine,
        in_specs=(blocks, P(), P(), P(TM_PARTS, None), P(), P(), P(), P(), P()),
        out_specs=(blocks, blocks),
        check_vma=False,
    )
```

```python
import functools

import jax
import jax.numpy as jnp
import numpy as np
from jax import lax
from jax.experimental import pallas as pl
from jax.experimental.pallas import tpu as pltpu
from jax.sharding import Mesh
from jax.sharding import PartitionSpec as P

HD = 80


MESH = pl.DeviceIdType.MESH
TM_PARTS = ("y_hi", "x", "z")
ROW_PARTS = ("y_lo", "core")


def distinct(values):
    return len(set(values))


def fine_mesh(mesh):
    devices = np.asarray(mesh.devices)
    tm, rows = devices.shape
    try:
        column = devices[:, 0]
        nx = distinct(d.coords[0] for d in column)
        nz = distinct(d.coords[2] for d in column)
        cores = distinct(d.core_on_chip for d in devices[0])
    except (AttributeError, IndexError, TypeError):
        nx, nz, cores = tm, 1, rows
    if tm % (nx * nz) or rows % cores:
        nx, nz, cores = tm, 1, rows
    shape = (tm // (nx * nz), nx, nz, rows // cores, cores)
    return Mesh(devices.reshape(shape), TM_PARTS + ROW_PARTS)


def staged_kernel(sizes, x_ref, out_ref, local_sem, *sems):
    high, across, along = sizes
    half = along // 2
    yh, xx, zz = [lax.axis_index(axis) for axis in TM_PARTS]
    low, core = [lax.axis_index(axis) for axis in ROW_PARTS]
    me = (yh * across + xx) * along + zz
    mine = me - zz
    other_core = 1 - core
    z_peer = lambda shift: {"z": lax.rem(zz + shift, along)}
    x_peer = lambda shift: {"x": lax.rem(xx + shift, across)}
    y_peer = {"y_hi": 1 - yh, "y_lo": 1 - low}
    c_peer = {"core": other_core}
    peers = [z_peer(s) for s in range(1, along)] + [x_peer(s) for s in range(1, across)]
    peers += [y_peer, c_peer]
    barrier = pltpu.get_barrier_semaphore()
    for peer in peers:
        pl.semaphore_signal(barrier, inc=1, device_id=peer, device_id_type=MESH)
    pl.semaphore_wait(barrier, len(peers))
    local = pltpu.make_async_copy(x_ref, out_ref.at[pl.ds(me, 1)], local_sem)
    local.start()
    local.wait()

    def exchange(pairs, send_sem, recv_sem):
        copies = []
        for index, (ref, peer) in enumerate(pairs):
            copy = pltpu.make_async_remote_copy(
                src_ref=ref,
                dst_ref=ref,
                send_sem=send_sem.at[index],
                recv_sem=recv_sem.at[index],
                device_id=peer,
                device_id_type=MESH,
            )
            copy.start()
            copies.append(copy)
        for copy in copies:
            copy.wait()

    own = out_ref.at[pl.ds(me, 1)]
    exchange([(own, z_peer(s)) for s in range(1, along)], sems[0], sems[1])
    start = mine + core * half
    part = out_ref.at[pl.ds(start, half)]
    exchange([(part, x_peer(s)) for s in range(1, across)], sems[2], sems[3])
    base = yh * across * along + core * half
    chunks = [out_ref.at[pl.ds(base + g * along, half)] for g in range(across)]
    exchange([(chunk, y_peer) for chunk in chunks], sems[4], sems[5])
    regions = high * across
    region = yh * across + xx
    groups = []
    for step in range(1, regions):
        j = lax.rem(region + step, regions)
        groups.append(out_ref.at[pl.ds(j * along + core * half, half)])
    exchange([(chunk, c_peer) for chunk in groups], sems[6], sems[7])


def staged_gather(value):
    sizes = [lax.axis_size(axis) for axis in TM_PARTS]
    total = sizes[0] * sizes[1] * sizes[2]
    sems = []
    for count in (sizes[2], sizes[1], sizes[1], sizes[0] * sizes[1]):
        sems += [pltpu.SemaphoreType.DMA((count,))] * 2
    gathered = pl.pallas_call(
        functools.partial(staged_kernel, sizes),
        out_shape=jax.ShapeDtypeStruct((total,) + value.shape, value.dtype),
        in_specs=[pl.BlockSpec(memory_space=pl.ANY)],
        out_specs=pl.BlockSpec(memory_space=pl.ANY),
        scratch_shapes=[pltpu.SemaphoreType.DMA] + sems,
        compiler_params=pltpu.CompilerParams(collective_id=0, has_side_effects=True),
    )(value[None])
    return gathered.reshape((total * value.shape[0],) + value.shape[1:])


def extended(value, axis, dim, width):
    size = lax.axis_size(axis)
    length = value.shape[dim]
    up = [(i, i + 1) for i in range(size - 1)]
    down = [(j, i) for i, j in up]
    last = lax.slice_in_dim(value, length - width, length, axis=dim)
    initial = lax.slice_in_dim(value, 0, width, axis=dim)
    before = lax.ppermute(last, axis, up)
    after = lax.ppermute(initial, axis, down)
    return jnp.concatenate([before, value, after], axis=dim)


def attend_block(state, query_heads, keys, values, heads):
    top, total, summed = state
    length = keys.shape[0]
    key_heads = keys.reshape(length, heads, HD)
    value_heads = values.reshape(length, heads, HD)
    scores = jnp.einsum(
        "qhd,khd->hqk", query_heads, key_heads, preferred_element_type=jnp.float32
    )
    scores = scores * HD ** (-0.5)
    block_top = jnp.max(scores, axis=2)
    new_top = block_top if top is None else jnp.maximum(top, block_top)
    weights = jnp.exp(scores - new_top[..., None])
    block_total = jnp.sum(weights, axis=2)
    product = jnp.einsum(
        "hqk,khd->hqd",
        weights.astype(jnp.bfloat16),
        value_heads,
        preferred_element_type=jnp.float32,
    )
    if top is None:
        return (new_top, block_total, product)
    factor = jnp.exp(top - new_top)
    return (new_top, total * factor + block_total, summed * factor[..., None] + product)


def attention_kernel(heads, q_ref, k_ref, v_ref, rk_ref, rv_ref, o_ref):
    for head in range(heads):
        lanes = slice(head * HD, (head + 1) * HD)
        query = q_ref[:, lanes]
        parts = []
        for key_ref, value_ref in ((k_ref, v_ref), (rk_ref, rv_ref)):
            scores = jnp.dot(
                query, key_ref[lanes, :], preferred_element_type=jnp.float32
            )
            parts.append((scores * HD ** (-0.5), value_ref))
        top = jnp.maximum(
            jnp.max(parts[0][0], axis=1, keepdims=True),
            jnp.max(parts[1][0], axis=1, keepdims=True),
        )
        total = None
        summed = None
        for scores, value_ref in parts:
            weights = jnp.exp(scores - top)
            block_total = jnp.sum(weights, axis=1, keepdims=True)
            product = jnp.dot(
                weights.astype(jnp.bfloat16),
                value_ref[:, lanes],
                preferred_element_type=jnp.float32,
            )
            total = block_total if total is None else total + block_total
            summed = product if summed is None else summed + product
        o_ref[:, lanes] = (summed / total).astype(o_ref.dtype)


def attention(query, keys, values, ref_keys, ref_values, heads):
    tokens, channels = query.shape
    whole = lambda array: pl.BlockSpec(array.shape, lambda i: (0, 0))
    operands = (query, keys, values, ref_keys, ref_values)
    return pl.pallas_call(
        functools.partial(attention_kernel, heads),
        out_shape=jax.ShapeDtypeStruct((tokens, channels), jnp.bfloat16),
        grid=(1,),
        in_specs=[whole(array) for array in operands],
        out_specs=pl.BlockSpec((tokens, channels), lambda i: (0, 0)),
    )(*operands)


def doubling_gather(value, axis):
    size = lax.axis_size(axis)
    step = 1
    while step < size:
        pairs = [(j, j ^ step) for j in range(size)]
        value = jnp.concatenate([value, lax.ppermute(value, axis, pairs)], axis=0)
        step *= 2
    return value


def shards(frames, conv_weight, conv_bias, ref_features, w_query, w_key, w_value, w_out, out_bias):
    count, band_rows, width, channels = frames.shape
    heads = channels // HD
    band = band_rows * width
    every_feature = staged_gather(ref_features)
    activated = jax.nn.silu(frames.astype(jnp.float32)).astype(jnp.bfloat16)
    padded = extended(activated, ROW_PARTS, 1, 1)
    padded = jnp.pad(padded, ((0, 0), (0, 0), (1, 1), (0, 0)))
    convolved = jnp.zeros((count * band, channels), jnp.float32)
    for row_tap in range(3):
        for col_tap in range(3):
            window = padded[:, row_tap : row_tap + band_rows, col_tap : col_tap + width].reshape(
                count * band, channels
            )
            convolved = convolved + jnp.dot(
                window, conv_weight[row_tap, col_tap], preferred_element_type=jnp.float32
            )
    hidden = (
        frames.reshape(count * band, channels).astype(jnp.float32) + convolved + conv_bias
    ).astype(jnp.bfloat16)
    rows = lax.axis_size(ROW_PARTS)
    others = jnp.concatenate(
        [
            lax.ppermute(hidden, ROW_PARTS, [(j, (j + shift) % rows) for j in range(rows)])
            for shift in range(1, rows)
        ],
        axis=0,
    )
    query = jnp.dot(hidden, w_query, preferred_element_type=jnp.float32).astype(jnp.bfloat16)
    source = jnp.concatenate([hidden, others], axis=0)
    project = lambda rows, weight: jnp.dot(
        rows, weight, preferred_element_type=jnp.float32
    ).astype(jnp.bfloat16)
    flipped = lambda rows, weight: jnp.einsum(
        "tc,cd->dt", rows, weight, preferred_element_type=jnp.float32
    ).astype(jnp.bfloat16)
    mixed = attention(
        query,
        flipped(source, w_key),
        project(source, w_value),
        flipped(every_feature, w_key),
        project(every_feature, w_value),
        heads,
    )
    attended = (jnp.dot(mixed, w_out, preferred_element_type=jnp.float32) + out_bias).astype(
        jnp.bfloat16
    )
    return (
        hidden.reshape(count, band_rows, width, channels),
        attended.reshape(count, band_rows, width, channels),
    )


def solution(mesh):
    fine = fine_mesh(mesh)
    blocks = P(TM_PARTS, ROW_PARTS, None, None)
    return jax.shard_map(
        shards,
        mesh=fine,
        in_specs=(blocks, P(), P(), P(TM_PARTS, None), P(), P(), P(), P(), P()),
        out_specs=(blocks, blocks),
        check_vma=False,
    )
```

```python
import functools

import jax
import jax.numpy as jnp
import numpy as np
from jax import lax
from jax.experimental import pallas as pl
from jax.experimental.pallas import tpu as pltpu
from jax.sharding import Mesh
from jax.sharding import PartitionSpec as P

HD = 80


MESH = pl.DeviceIdType.MESH
TM_PARTS = ("y_hi", "x", "z")
ROW_PARTS = ("y_lo", "core")


def distinct(values):
    return len(set(values))


def fine_mesh(mesh):
    devices = np.asarray(mesh.devices)
    tm, rows = devices.shape
    try:
        column = devices[:, 0]
        nx = distinct(d.coords[0] for d in column)
        nz = distinct(d.coords[2] for d in column)
        cores = distinct(d.core_on_chip for d in devices[0])
    except (AttributeError, IndexError, TypeError):
        nx, nz, cores = tm, 1, rows
    if tm % (nx * nz) or rows % cores:
        nx, nz, cores = tm, 1, rows
    shape = (tm // (nx * nz), nx, nz, rows // cores, cores)
    return Mesh(devices.reshape(shape), TM_PARTS + ROW_PARTS)


def staged_kernel(sizes, x_ref, after_ref, out_ref, local_sem, *sems):
    high, across, along = sizes
    half = along // 2
    yh, xx, zz = [lax.axis_index(axis) for axis in TM_PARTS]
    low, core = [lax.axis_index(axis) for axis in ROW_PARTS]
    me = (yh * across + xx) * along + zz
    mine = me - zz
    other_core = 1 - core
    z_peer = lambda shift: {"z": lax.rem(zz + shift, along)}
    x_peer = lambda shift: {"x": lax.rem(xx + shift, across)}
    y_peer = {"y_hi": 1 - yh, "y_lo": 1 - low}
    c_peer = {"core": other_core}
    peers = [z_peer(s) for s in range(1, along)] + [x_peer(s) for s in range(1, across)]
    peers += [y_peer, c_peer]
    barrier = pltpu.get_barrier_semaphore()
    for peer in peers:
        pl.semaphore_signal(barrier, inc=1, device_id=peer, device_id_type=MESH)
    pl.semaphore_wait(barrier, len(peers))
    local = pltpu.make_async_copy(x_ref, out_ref.at[pl.ds(me, 1)], local_sem)
    local.start()
    local.wait()

    def exchange(pairs, send_sem, recv_sem):
        copies = []
        for index, (ref, peer) in enumerate(pairs):
            copy = pltpu.make_async_remote_copy(
                src_ref=ref,
                dst_ref=ref,
                send_sem=send_sem.at[index],
                recv_sem=recv_sem.at[index],
                device_id=peer,
                device_id_type=MESH,
            )
            copy.start()
            copies.append(copy)
        for copy in copies:
            copy.wait()

    own = out_ref.at[pl.ds(me, 1)]
    exchange([(own, z_peer(s)) for s in range(1, along)], sems[0], sems[1])
    start = mine + core * half
    part = out_ref.at[pl.ds(start, half)]
    exchange([(part, x_peer(s)) for s in range(1, across)], sems[2], sems[3])
    base = yh * across * along + core * half
    chunks = [out_ref.at[pl.ds(base + g * along, half)] for g in range(across)]
    exchange([(chunk, y_peer) for chunk in chunks], sems[4], sems[5])
    regions = high * across
    region = yh * across + xx
    groups = []
    for step in range(1, regions):
        j = lax.rem(region + step, regions)
        groups.append(out_ref.at[pl.ds(j * along + core * half, half)])
    exchange([(chunk, c_peer) for chunk in groups], sems[6], sems[7])


def staged_gather(value, after):
    sizes = [lax.axis_size(axis) for axis in TM_PARTS]
    total = sizes[0] * sizes[1] * sizes[2]
    sems = []
    for count in (sizes[2], sizes[1], sizes[1], sizes[0] * sizes[1]):
        sems += [pltpu.SemaphoreType.DMA((count,))] * 2
    gathered = pl.pallas_call(
        functools.partial(staged_kernel, sizes),
        out_shape=jax.ShapeDtypeStruct((total,) + value.shape, value.dtype),
        in_specs=[pl.BlockSpec(memory_space=pl.ANY)] * 2,
        out_specs=pl.BlockSpec(memory_space=pl.ANY),
        scratch_shapes=[pltpu.SemaphoreType.DMA] + sems,
        compiler_params=pltpu.CompilerParams(collective_id=0, has_side_effects=True),
    )(value[None], after)
    return gathered.reshape((total * value.shape[0],) + value.shape[1:])


def extended(value, axis, dim, width):
    size = lax.axis_size(axis)
    length = value.shape[dim]
    up = [(i, i + 1) for i in range(size - 1)]
    down = [(j, i) for i, j in up]
    last = lax.slice_in_dim(value, length - width, length, axis=dim)
    initial = lax.slice_in_dim(value, 0, width, axis=dim)
    before = lax.ppermute(last, axis, up)
    after = lax.ppermute(initial, axis, down)
    return jnp.concatenate([before, value, after], axis=dim)


def attend_block(state, query_heads, keys, values, heads):
    top, total, summed = state
    length = keys.shape[0]
    key_heads = keys.reshape(length, heads, HD)
    value_heads = values.reshape(length, heads, HD)
    scores = jnp.einsum(
        "qhd,khd->hqk", query_heads, key_heads, preferred_element_type=jnp.float32
    )
    scores = scores * HD ** (-0.5)
    block_top = jnp.max(scores, axis=2)
    new_top = block_top if top is None else jnp.maximum(top, block_top)
    weights = jnp.exp(scores - new_top[..., None])
    block_total = jnp.sum(weights, axis=2)
    product = jnp.einsum(
        "hqk,khd->hqd",
        weights.astype(jnp.bfloat16),
        value_heads,
        preferred_element_type=jnp.float32,
    )
    if top is None:
        return (new_top, block_total, product)
    factor = jnp.exp(top - new_top)
    return (new_top, total * factor + block_total, summed * factor[..., None] + product)


def attention_kernel(heads, q_ref, k_ref, v_ref, rk_ref, rv_ref, o_ref):
    for head in range(heads):
        lanes = slice(head * HD, (head + 1) * HD)
        query = q_ref[:, lanes]
        parts = []
        for key_ref, value_ref in ((k_ref, v_ref), (rk_ref, rv_ref)):
            scores = jnp.dot(
                query, key_ref[lanes, :], preferred_element_type=jnp.float32
            )
            parts.append((scores * HD ** (-0.5), value_ref))
        top = jnp.maximum(
            jnp.max(parts[0][0], axis=1, keepdims=True),
            jnp.max(parts[1][0], axis=1, keepdims=True),
        )
        total = None
        summed = None
        for scores, value_ref in parts:
            weights = jnp.exp(scores - top)
            block_total = jnp.sum(weights, axis=1, keepdims=True)
            product = jnp.dot(
                weights.astype(jnp.bfloat16),
                value_ref[:, lanes],
                preferred_element_type=jnp.float32,
            )
            total = block_total if total is None else total + block_total
            summed = product if summed is None else summed + product
        o_ref[:, lanes] = (summed / total).astype(o_ref.dtype)


def attention(query, keys, values, ref_keys, ref_values, heads):
    tokens, channels = query.shape
    whole = lambda array: pl.BlockSpec(array.shape, lambda i: (0, 0))
    operands = (query, keys, values, ref_keys, ref_values)
    return pl.pallas_call(
        functools.partial(attention_kernel, heads),
        out_shape=jax.ShapeDtypeStruct((tokens, channels), jnp.bfloat16),
        grid=(1,),
        in_specs=[whole(array) for array in operands],
        out_specs=pl.BlockSpec((tokens, channels), lambda i: (0, 0)),
    )(*operands)


def doubling_gather(value, axis):
    size = lax.axis_size(axis)
    step = 1
    while step < size:
        pairs = [(j, j ^ step) for j in range(size)]
        value = jnp.concatenate([value, lax.ppermute(value, axis, pairs)], axis=0)
        step *= 2
    return value


def shards(frames, conv_weight, conv_bias, ref_features, w_query, w_key, w_value, w_out, out_bias):
    count, band_rows, width, channels = frames.shape
    heads = channels // HD
    band = band_rows * width
    activated = jax.nn.silu(frames.astype(jnp.float32)).astype(jnp.bfloat16)
    padded = extended(activated, ROW_PARTS, 1, 1)
    padded = jnp.pad(padded, ((0, 0), (0, 0), (1, 1), (0, 0)))
    convolved = jnp.zeros((count * band, channels), jnp.float32)
    for row_tap in range(3):
        for col_tap in range(3):
            window = padded[:, row_tap : row_tap + band_rows, col_tap : col_tap + width].reshape(
                count * band, channels
            )
            convolved = convolved + jnp.dot(
                window, conv_weight[row_tap, col_tap], preferred_element_type=jnp.float32
            )
    hidden = (
        frames.reshape(count * band, channels).astype(jnp.float32) + convolved + conv_bias
    ).astype(jnp.bfloat16)
    rows = lax.axis_size(ROW_PARTS)
    others = jnp.concatenate(
        [
            lax.ppermute(hidden, ROW_PARTS, [(j, (j + shift) % rows) for j in range(rows)])
            for shift in range(1, rows)
        ],
        axis=0,
    )
    every_feature = staged_gather(ref_features, hidden)
    query = jnp.dot(hidden, w_query, preferred_element_type=jnp.float32).astype(jnp.bfloat16)
    source = jnp.concatenate([hidden, others], axis=0)
    project = lambda rows, weight: jnp.dot(
        rows, weight, preferred_element_type=jnp.float32
    ).astype(jnp.bfloat16)
    flipped = lambda rows, weight: jnp.einsum(
        "tc,cd->dt", rows, weight, preferred_element_type=jnp.float32
    ).astype(jnp.bfloat16)
    mixed = attention(
        query,
        flipped(source, w_key),
        project(source, w_value),
        flipped(every_feature, w_key),
        project(every_feature, w_value),
        heads,
    )
    attended = (jnp.dot(mixed, w_out, preferred_element_type=jnp.float32) + out_bias).astype(
        jnp.bfloat16
    )
    return (
        hidden.reshape(count, band_rows, width, channels),
        attended.reshape(count, band_rows, width, channels),
    )


def solution(mesh):
    fine = fine_mesh(mesh)
    blocks = P(TM_PARTS, ROW_PARTS, None, None)
    return jax.shard_map(
        shards,
        mesh=fine,
        in_specs=(blocks, P(), P(), P(TM_PARTS, None), P(), P(), P(), P(), P()),
        out_specs=(blocks, blocks),
        check_vma=False,
    )
```

```python
import functools

import jax
import jax.numpy as jnp
import numpy as np
from jax import lax
from jax.experimental import pallas as pl
from jax.experimental.pallas import tpu as pltpu
from jax.sharding import Mesh
from jax.sharding import PartitionSpec as P

HD = 80


MESH = pl.DeviceIdType.MESH
TM_PARTS = ("y_hi", "x", "z")
ROW_PARTS = ("y_lo", "core")


def distinct(values):
    return len(set(values))


def fine_mesh(mesh):
    devices = np.asarray(mesh.devices)
    tm, rows = devices.shape
    try:
        column = devices[:, 0]
        nx = distinct(d.coords[0] for d in column)
        nz = distinct(d.coords[2] for d in column)
        cores = distinct(d.core_on_chip for d in devices[0])
    except (AttributeError, IndexError, TypeError):
        nx, nz, cores = tm, 1, rows
    if tm % (nx * nz) or rows % cores:
        nx, nz, cores = tm, 1, rows
    shape = (tm // (nx * nz), nx, nz, rows // cores, cores)
    return Mesh(devices.reshape(shape), TM_PARTS + ROW_PARTS)


def staged_kernel(sizes, x_ref, after_ref, out_ref, local_sem, *sems):
    high, across, along = sizes
    half = along // 2
    yh, xx, zz = [lax.axis_index(axis) for axis in TM_PARTS]
    low, core = [lax.axis_index(axis) for axis in ROW_PARTS]
    me = (yh * across + xx) * along + zz
    mine = me - zz
    other_core = 1 - core
    z_peer = lambda shift: {"z": lax.rem(zz + shift, along)}
    x_peer = lambda shift: {"x": lax.rem(xx + shift, across)}
    y_peer = {"y_hi": 1 - yh, "y_lo": 1 - low}
    c_peer = {"core": other_core}
    peers = [z_peer(s) for s in range(1, along)] + [x_peer(s) for s in range(1, across)]
    peers += [y_peer, c_peer]
    barrier = pltpu.get_barrier_semaphore()
    for peer in peers:
        pl.semaphore_signal(barrier, inc=1, device_id=peer, device_id_type=MESH)
    pl.semaphore_wait(barrier, len(peers))
    local = pltpu.make_async_copy(x_ref, out_ref.at[pl.ds(me, 1)], local_sem)
    local.start()
    local.wait()

    def exchange(pairs, send_sem, recv_sem):
        copies = []
        for index, (ref, peer) in enumerate(pairs):
            copy = pltpu.make_async_remote_copy(
                src_ref=ref,
                dst_ref=ref,
                send_sem=send_sem.at[index],
                recv_sem=recv_sem.at[index],
                device_id=peer,
                device_id_type=MESH,
            )
            copy.start()
            copies.append(copy)
        for copy in copies:
            copy.wait()

    own = out_ref.at[pl.ds(me, 1)]
    exchange([(own, z_peer(s)) for s in range(1, along)], sems[0], sems[1])
    start = mine + core * half
    part = out_ref.at[pl.ds(start, half)]
    exchange([(part, x_peer(s)) for s in range(1, across)], sems[2], sems[3])
    base = yh * across * along + core * half
    chunks = [out_ref.at[pl.ds(base + g * along, half)] for g in range(across)]
    exchange([(chunk, y_peer) for chunk in chunks], sems[4], sems[5])
    regions = high * across
    region = yh * across + xx
    groups = []
    for step in range(1, regions):
        j = lax.rem(region + step, regions)
        groups.append(out_ref.at[pl.ds(j * along + core * half, half)])
    exchange([(chunk, c_peer) for chunk in groups], sems[6], sems[7])


def staged_gather(value, after):
    sizes = [lax.axis_size(axis) for axis in TM_PARTS]
    total = sizes[0] * sizes[1] * sizes[2]
    sems = []
    for count in (sizes[2], sizes[1], sizes[1], sizes[0] * sizes[1]):
        sems += [pltpu.SemaphoreType.DMA((count,))] * 2
    gathered = pl.pallas_call(
        functools.partial(staged_kernel, sizes),
        out_shape=jax.ShapeDtypeStruct((total,) + value.shape, value.dtype),
        in_specs=[pl.BlockSpec(memory_space=pl.ANY)] * 2,
        out_specs=pl.BlockSpec(memory_space=pl.ANY),
        scratch_shapes=[pltpu.SemaphoreType.DMA] + sems,
        compiler_params=pltpu.CompilerParams(collective_id=0, has_side_effects=True),
    )(value[None], after)
    return gathered.reshape((total * value.shape[0],) + value.shape[1:])


def extended(value, axis, dim, width):
    size = lax.axis_size(axis)
    length = value.shape[dim]
    up = [(i, i + 1) for i in range(size - 1)]
    down = [(j, i) for i, j in up]
    last = lax.slice_in_dim(value, length - width, length, axis=dim)
    initial = lax.slice_in_dim(value, 0, width, axis=dim)
    before = lax.ppermute(last, axis, up)
    after = lax.ppermute(initial, axis, down)
    return jnp.concatenate([before, value, after], axis=dim)


def attend_block(state, query_heads, keys, values, heads):
    top, total, summed = state
    length = keys.shape[0]
    key_heads = keys.reshape(length, heads, HD)
    value_heads = values.reshape(length, heads, HD)
    scores = jnp.einsum(
        "qhd,khd->hqk", query_heads, key_heads, preferred_element_type=jnp.float32
    )
    scores = scores * HD ** (-0.5)
    block_top = jnp.max(scores, axis=2)
    new_top = block_top if top is None else jnp.maximum(top, block_top)
    weights = jnp.exp(scores - new_top[..., None])
    block_total = jnp.sum(weights, axis=2)
    product = jnp.einsum(
        "hqk,khd->hqd",
        weights.astype(jnp.bfloat16),
        value_heads,
        preferred_element_type=jnp.float32,
    )
    if top is None:
        return (new_top, block_total, product)
    factor = jnp.exp(top - new_top)
    return (new_top, total * factor + block_total, summed * factor[..., None] + product)


def attention_kernel(heads, q_ref, k_ref, v_ref, o_ref):
    for head in range(heads):
        lanes = slice(head * HD, (head + 1) * HD)
        scores = jnp.dot(q_ref[:, lanes], k_ref[lanes, :], preferred_element_type=jnp.float32)
        scores = scores * HD ** (-0.5)
        top = jnp.max(scores, axis=1, keepdims=True)
        weights = jnp.exp(scores - top)
        total = jnp.sum(weights, axis=1, keepdims=True)
        summed = jnp.dot(
            weights.astype(jnp.bfloat16), v_ref[:, lanes], preferred_element_type=jnp.float32
        )
        o_ref[:, lanes] = (summed / total).astype(o_ref.dtype)


def attention(query, keys, values, heads):
    tokens, channels = query.shape
    whole = lambda array: pl.BlockSpec(array.shape, lambda i: (0, 0))
    operands = (query, keys, values)
    return pl.pallas_call(
        functools.partial(attention_kernel, heads),
        out_shape=jax.ShapeDtypeStruct((tokens, channels), jnp.bfloat16),
        grid=(1,),
        in_specs=[whole(array) for array in operands],
        out_specs=pl.BlockSpec((tokens, channels), lambda i: (0, 0)),
    )(*operands)


def doubling_gather(value, axis):
    size = lax.axis_size(axis)
    step = 1
    while step < size:
        pairs = [(j, j ^ step) for j in range(size)]
        value = jnp.concatenate([value, lax.ppermute(value, axis, pairs)], axis=0)
        step *= 2
    return value


def shards(frames, conv_weight, conv_bias, ref_features, w_query, w_key, w_value, w_out, out_bias):
    count, band_rows, width, channels = frames.shape
    heads = channels // HD
    band = band_rows * width
    activated = jax.nn.silu(frames.astype(jnp.float32)).astype(jnp.bfloat16)
    padded = extended(activated, ROW_PARTS, 1, 1)
    padded = jnp.pad(padded, ((0, 0), (0, 0), (1, 1), (0, 0)))
    convolved = jnp.zeros((count * band, channels), jnp.float32)
    for row_tap in range(3):
        for col_tap in range(3):
            window = padded[:, row_tap : row_tap + band_rows, col_tap : col_tap + width].reshape(
                count * band, channels
            )
            convolved = convolved + jnp.dot(
                window, conv_weight[row_tap, col_tap], preferred_element_type=jnp.float32
            )
    hidden = (
        frames.reshape(count * band, channels).astype(jnp.float32) + convolved + conv_bias
    ).astype(jnp.bfloat16)
    rows = lax.axis_size(ROW_PARTS)
    others = jnp.concatenate(
        [
            lax.ppermute(hidden, ROW_PARTS, [(j, (j + shift) % rows) for j in range(rows)])
            for shift in range(1, rows)
        ],
        axis=0,
    )
    query = jnp.dot(hidden, w_query, preferred_element_type=jnp.float32).astype(jnp.bfloat16)
    every_feature = staged_gather(ref_features, query)
    source = jnp.concatenate([hidden, others, every_feature], axis=0)
    keys = jnp.einsum("tc,cd->dt", source, w_key, preferred_element_type=jnp.float32)
    values = jnp.dot(source, w_value, preferred_element_type=jnp.float32)
    mixed = attention(query, keys.astype(jnp.bfloat16), values.astype(jnp.bfloat16), heads)
    attended = (jnp.dot(mixed, w_out, preferred_element_type=jnp.float32) + out_bias).astype(
        jnp.bfloat16
    )
    return (
        hidden.reshape(count, band_rows, width, channels),
        attended.reshape(count, band_rows, width, channels),
    )


def solution(mesh):
    fine = fine_mesh(mesh)
    blocks = P(TM_PARTS, ROW_PARTS, None, None)
    return jax.shard_map(
        shards,
        mesh=fine,
        in_specs=(blocks, P(), P(), P(TM_PARTS, None), P(), P(), P(), P(), P()),
        out_specs=(blocks, blocks),
        check_vma=False,
    )
```

```python
import functools

import jax
import jax.numpy as jnp
import numpy as np
from jax import lax
from jax.experimental import pallas as pl
from jax.experimental.pallas import tpu as pltpu
from jax.sharding import Mesh
from jax.sharding import PartitionSpec as P

HD = 80


MESH = pl.DeviceIdType.MESH
TM_PARTS = ("y_hi", "x", "z")
ROW_PARTS = ("y_lo", "core")


def distinct(values):
    return len(set(values))


def fine_mesh(mesh):
    devices = np.asarray(mesh.devices)
    tm, rows = devices.shape
    try:
        column = devices[:, 0]
        nx = distinct(d.coords[0] for d in column)
        nz = distinct(d.coords[2] for d in column)
        cores = distinct(d.core_on_chip for d in devices[0])
    except (AttributeError, IndexError, TypeError):
        nx, nz, cores = tm, 1, rows
    if tm % (nx * nz) or rows % cores:
        nx, nz, cores = tm, 1, rows
    shape = (tm // (nx * nz), nx, nz, rows // cores, cores)
    return Mesh(devices.reshape(shape), TM_PARTS + ROW_PARTS)


def staged_kernel(sizes, x_ref, after_ref, out_ref, local_sem, *sems):
    high, across, along = sizes
    half = along // 2
    yh, xx, zz = [lax.axis_index(axis) for axis in TM_PARTS]
    low, core = [lax.axis_index(axis) for axis in ROW_PARTS]
    me = (yh * across + xx) * along + zz
    mine = me - zz
    other_core = 1 - core
    z_peer = lambda shift: {"z": lax.rem(zz + shift, along)}
    x_peer = lambda shift: {"x": lax.rem(xx + shift, across)}
    y_peer = {"y_hi": 1 - yh, "y_lo": 1 - low}
    c_peer = {"core": other_core}
    peers = [z_peer(s) for s in range(1, along)] + [x_peer(s) for s in range(1, across)]
    peers += [y_peer, c_peer]
    barrier = pltpu.get_barrier_semaphore()
    for peer in peers:
        pl.semaphore_signal(barrier, inc=1, device_id=peer, device_id_type=MESH)
    pl.semaphore_wait(barrier, len(peers))
    local = pltpu.make_async_copy(x_ref, out_ref.at[pl.ds(me, 1)], local_sem)
    local.start()
    local.wait()

    def exchange(pairs, send_sem, recv_sem):
        copies = []
        for index, (ref, peer) in enumerate(pairs):
            copy = pltpu.make_async_remote_copy(
                src_ref=ref,
                dst_ref=ref,
                send_sem=send_sem.at[index],
                recv_sem=recv_sem.at[index],
                device_id=peer,
                device_id_type=MESH,
            )
            copy.start()
            copies.append(copy)
        for copy in copies:
            copy.wait()

    own = out_ref.at[pl.ds(me, 1)]
    exchange([(own, z_peer(s)) for s in range(1, along)], sems[0], sems[1])
    start = mine + core * half
    part = out_ref.at[pl.ds(start, half)]
    exchange([(part, x_peer(s)) for s in range(1, across)], sems[2], sems[3])
    base = yh * across * along + core * half
    chunks = [out_ref.at[pl.ds(base + g * along, half)] for g in range(across)]
    exchange([(chunk, y_peer) for chunk in chunks], sems[4], sems[5])
    regions = high * across
    region = yh * across + xx
    groups = []
    for step in range(1, regions):
        j = lax.rem(region + step, regions)
        groups.append(out_ref.at[pl.ds(j * along + core * half, half)])
    exchange([(chunk, c_peer) for chunk in groups], sems[6], sems[7])


def staged_gather(value, after):
    sizes = [lax.axis_size(axis) for axis in TM_PARTS]
    total = sizes[0] * sizes[1] * sizes[2]
    sems = []
    for count in (sizes[2], sizes[1], sizes[1], sizes[0] * sizes[1]):
        sems += [pltpu.SemaphoreType.DMA((count,))] * 2
    gathered = pl.pallas_call(
        functools.partial(staged_kernel, sizes),
        out_shape=jax.ShapeDtypeStruct((total,) + value.shape, value.dtype),
        in_specs=[pl.BlockSpec(memory_space=pl.ANY)] * 2,
        out_specs=pl.BlockSpec(memory_space=pl.ANY),
        scratch_shapes=[pltpu.SemaphoreType.DMA] + sems,
        compiler_params=pltpu.CompilerParams(collective_id=0, has_side_effects=True),
    )(value[None], after)
    return gathered.reshape((total * value.shape[0],) + value.shape[1:])


def extended(value, axis, dim, width):
    size = lax.axis_size(axis)
    length = value.shape[dim]
    up = [(i, i + 1) for i in range(size - 1)]
    down = [(j, i) for i, j in up]
    last = lax.slice_in_dim(value, length - width, length, axis=dim)
    initial = lax.slice_in_dim(value, 0, width, axis=dim)
    before = lax.ppermute(last, axis, up)
    after = lax.ppermute(initial, axis, down)
    return jnp.concatenate([before, value, after], axis=dim)


def attend_block(state, query_heads, keys, values, heads):
    top, total, summed = state
    length = keys.shape[0]
    key_heads = keys.reshape(length, heads, HD)
    value_heads = values.reshape(length, heads, HD)
    scores = jnp.einsum(
        "qhd,khd->hqk", query_heads, key_heads, preferred_element_type=jnp.float32
    )
    scores = scores * HD ** (-0.5)
    block_top = jnp.max(scores, axis=2)
    new_top = block_top if top is None else jnp.maximum(top, block_top)
    weights = jnp.exp(scores - new_top[..., None])
    block_total = jnp.sum(weights, axis=2)
    product = jnp.einsum(
        "hqk,khd->hqd",
        weights.astype(jnp.bfloat16),
        value_heads,
        preferred_element_type=jnp.float32,
    )
    if top is None:
        return (new_top, block_total, product)
    factor = jnp.exp(top - new_top)
    return (new_top, total * factor + block_total, summed * factor[..., None] + product)


def attention_kernel(heads, q_ref, k_ref, s_ref, w_ref, o_ref, v_ref):
    v_ref[...] = jnp.dot(
        s_ref[...], w_ref[...], preferred_element_type=jnp.float32
    ).astype(v_ref.dtype)
    for head in range(heads):
        lanes = slice(head * HD, (head + 1) * HD)
        scores = jnp.dot(q_ref[:, lanes], k_ref[lanes, :], preferred_element_type=jnp.float32)
        scores = scores * HD ** (-0.5)
        top = jnp.max(scores, axis=1, keepdims=True)
        weights = jnp.exp(scores - top)
        total = jnp.sum(weights, axis=1, keepdims=True)
        summed = jnp.dot(
            weights.astype(jnp.bfloat16), v_ref[:, lanes], preferred_element_type=jnp.float32
        )
        o_ref[:, lanes] = (summed / total).astype(o_ref.dtype)


def attention(query, keys, source, w_value, heads):
    tokens, channels = query.shape
    whole = lambda array: pl.BlockSpec(array.shape, lambda i: (0, 0))
    operands = (query, keys, source, w_value)
    return pl.pallas_call(
        functools.partial(attention_kernel, heads),
        out_shape=jax.ShapeDtypeStruct((tokens, channels), jnp.bfloat16),
        grid=(1,),
        in_specs=[whole(array) for array in operands],
        out_specs=pl.BlockSpec((tokens, channels), lambda i: (0, 0)),
        scratch_shapes=[pltpu.VMEM((source.shape[0], w_value.shape[1]), jnp.bfloat16)],
    )(*operands)


def doubling_gather(value, axis):
    size = lax.axis_size(axis)
    step = 1
    while step < size:
        pairs = [(j, j ^ step) for j in range(size)]
        value = jnp.concatenate([value, lax.ppermute(value, axis, pairs)], axis=0)
        step *= 2
    return value


def shards(frames, conv_weight, conv_bias, ref_features, w_query, w_key, w_value, w_out, out_bias):
    count, band_rows, width, channels = frames.shape
    heads = channels // HD
    band = band_rows * width
    activated = jax.nn.silu(frames.astype(jnp.float32)).astype(jnp.bfloat16)
    padded = extended(activated, ROW_PARTS, 1, 1)
    padded = jnp.pad(padded, ((0, 0), (0, 0), (1, 1), (0, 0)))
    convolved = jnp.zeros((count * band, channels), jnp.float32)
    for row_tap in range(3):
        for col_tap in range(3):
            window = padded[:, row_tap : row_tap + band_rows, col_tap : col_tap + width].reshape(
                count * band, channels
            )
            convolved = convolved + jnp.dot(
                window, conv_weight[row_tap, col_tap], preferred_element_type=jnp.float32
            )
    hidden = (
        frames.reshape(count * band, channels).astype(jnp.float32) + convolved + conv_bias
    ).astype(jnp.bfloat16)
    rows = lax.axis_size(ROW_PARTS)
    others = jnp.concatenate(
        [
            lax.ppermute(hidden, ROW_PARTS, [(j, (j + shift) % rows) for j in range(rows)])
            for shift in range(1, rows)
        ],
        axis=0,
    )
    query = jnp.dot(hidden, w_query, preferred_element_type=jnp.float32).astype(jnp.bfloat16)
    every_feature = staged_gather(ref_features, query)
    source = jnp.concatenate([hidden, others, every_feature], axis=0)
    keys = jnp.einsum("tc,cd->dt", source, w_key, preferred_element_type=jnp.float32)
    mixed = attention(query, keys.astype(jnp.bfloat16), source, w_value, heads)
    attended = (jnp.dot(mixed, w_out, preferred_element_type=jnp.float32) + out_bias).astype(
        jnp.bfloat16
    )
    return (
        hidden.reshape(count, band_rows, width, channels),
        attended.reshape(count, band_rows, width, channels),
    )


def solution(mesh):
    fine = fine_mesh(mesh)
    blocks = P(TM_PARTS, ROW_PARTS, None, None)
    return jax.shard_map(
        shards,
        mesh=fine,
        in_specs=(blocks, P(), P(), P(TM_PARTS, None), P(), P(), P(), P(), P()),
        out_specs=(blocks, blocks),
        check_vma=False,
    )
```

```python
import functools

import jax
import jax.numpy as jnp
import numpy as np
from jax import lax
from jax.experimental import pallas as pl
from jax.experimental.pallas import tpu as pltpu
from jax.sharding import Mesh
from jax.sharding import PartitionSpec as P

HD = 80


MESH = pl.DeviceIdType.MESH
TM_PARTS = ("y_hi", "x", "z")
ROW_PARTS = ("y_lo", "core")


def distinct(values):
    return len(set(values))


def fine_mesh(mesh):
    devices = np.asarray(mesh.devices)
    tm, rows = devices.shape
    try:
        column = devices[:, 0]
        nx = distinct(d.coords[0] for d in column)
        nz = distinct(d.coords[2] for d in column)
        cores = distinct(d.core_on_chip for d in devices[0])
    except (AttributeError, IndexError, TypeError):
        nx, nz, cores = tm, 1, rows
    if tm % (nx * nz) or rows % cores:
        nx, nz, cores = tm, 1, rows
    shape = (tm // (nx * nz), nx, nz, rows // cores, cores)
    return Mesh(devices.reshape(shape), TM_PARTS + ROW_PARTS)


def staged_kernel(sizes, x_ref, after_ref, out_ref, local_sem, *sems):
    high, across, along = sizes
    half = along // 2
    yh, xx, zz = [lax.axis_index(axis) for axis in TM_PARTS]
    low, core = [lax.axis_index(axis) for axis in ROW_PARTS]
    me = (yh * across + xx) * along + zz
    mine = me - zz
    other_core = 1 - core
    z_peer = lambda shift: {"z": lax.rem(zz + shift, along)}
    x_peer = lambda shift: {"x": lax.rem(xx + shift, across)}
    y_peer = {"y_hi": 1 - yh, "y_lo": 1 - low}
    c_peer = {"core": other_core}
    peers = [z_peer(s) for s in range(1, along)] + [x_peer(s) for s in range(1, across)]
    peers += [y_peer, c_peer]
    barrier = pltpu.get_barrier_semaphore()
    for peer in peers:
        pl.semaphore_signal(barrier, inc=1, device_id=peer, device_id_type=MESH)
    pl.semaphore_wait(barrier, len(peers))
    local = pltpu.make_async_copy(x_ref, out_ref.at[pl.ds(me, 1)], local_sem)
    local.start()
    local.wait()

    def exchange(pairs, send_sem, recv_sem):
        copies = []
        for index, (ref, peer) in enumerate(pairs):
            copy = pltpu.make_async_remote_copy(
                src_ref=ref,
                dst_ref=ref,
                send_sem=send_sem.at[index],
                recv_sem=recv_sem.at[index],
                device_id=peer,
                device_id_type=MESH,
            )
            copy.start()
            copies.append(copy)
        for copy in copies:
            copy.wait()

    own = out_ref.at[pl.ds(me, 1)]
    exchange([(own, z_peer(s)) for s in range(1, along)], sems[0], sems[1])
    start = mine + core * half
    part = out_ref.at[pl.ds(start, half)]
    exchange([(part, x_peer(s)) for s in range(1, across)], sems[2], sems[3])
    base = yh * across * along + core * half
    chunks = [out_ref.at[pl.ds(base + g * along, half)] for g in range(across)]
    exchange([(chunk, y_peer) for chunk in chunks], sems[4], sems[5])
    regions = high * across
    region = yh * across + xx
    groups = []
    for step in range(1, regions):
        j = lax.rem(region + step, regions)
        groups.append(out_ref.at[pl.ds(j * along + core * half, half)])
    exchange([(chunk, c_peer) for chunk in groups], sems[6], sems[7])


def staged_gather(value, after):
    sizes = [lax.axis_size(axis) for axis in TM_PARTS]
    total = sizes[0] * sizes[1] * sizes[2]
    sems = []
    for count in (sizes[2], sizes[1], sizes[1], sizes[0] * sizes[1]):
        sems += [pltpu.SemaphoreType.DMA((count,))] * 2
    gathered = pl.pallas_call(
        functools.partial(staged_kernel, sizes),
        out_shape=jax.ShapeDtypeStruct((total,) + value.shape, value.dtype),
        in_specs=[pl.BlockSpec(memory_space=pl.ANY)] * 2,
        out_specs=pl.BlockSpec(memory_space=pl.ANY),
        scratch_shapes=[pltpu.SemaphoreType.DMA] + sems,
        compiler_params=pltpu.CompilerParams(collective_id=0, has_side_effects=True),
    )(value[None], after)
    return gathered.reshape((total * value.shape[0],) + value.shape[1:])


def extended(value, axis, dim, width):
    size = lax.axis_size(axis)
    length = value.shape[dim]
    up = [(i, i + 1) for i in range(size - 1)]
    down = [(j, i) for i, j in up]
    last = lax.slice_in_dim(value, length - width, length, axis=dim)
    initial = lax.slice_in_dim(value, 0, width, axis=dim)
    before = lax.ppermute(last, axis, up)
    after = lax.ppermute(initial, axis, down)
    return jnp.concatenate([before, value, after], axis=dim)


def attend_block(state, query_heads, keys, values, heads):
    top, total, summed = state
    length = keys.shape[0]
    key_heads = keys.reshape(length, heads, HD)
    value_heads = values.reshape(length, heads, HD)
    scores = jnp.einsum(
        "qhd,khd->hqk", query_heads, key_heads, preferred_element_type=jnp.float32
    )
    scores = scores * HD ** (-0.5)
    block_top = jnp.max(scores, axis=2)
    new_top = block_top if top is None else jnp.maximum(top, block_top)
    weights = jnp.exp(scores - new_top[..., None])
    block_total = jnp.sum(weights, axis=2)
    product = jnp.einsum(
        "hqk,khd->hqd",
        weights.astype(jnp.bfloat16),
        value_heads,
        preferred_element_type=jnp.float32,
    )
    if top is None:
        return (new_top, block_total, product)
    factor = jnp.exp(top - new_top)
    return (new_top, total * factor + block_total, summed * factor[..., None] + product)


def attention_kernel(heads, parts, *refs):
    q_ref, wk_ref, wv_ref = refs[:3]
    sources = refs[3 : 3 + parts]
    o_ref, k_ref, v_ref = refs[3 + parts :]
    offset = 0
    for source in sources:
        rows = source.shape[0]
        k_ref[:, offset : offset + rows] = lax.dot_general(
            wk_ref[...], source[...], (((1,), (1,)), ((), ())), preferred_element_type=jnp.float32
        ).astype(k_ref.dtype)
        v_ref[offset : offset + rows, :] = jnp.dot(
            source[...], wv_ref[...], preferred_element_type=jnp.float32
        ).astype(v_ref.dtype)
        offset += rows
    for head in range(heads):
        lanes = slice(head * HD, (head + 1) * HD)
        scores = jnp.dot(q_ref[:, lanes], k_ref[lanes, :], preferred_element_type=jnp.float32)
        scores = scores * HD ** (-0.5)
        top = jnp.max(scores, axis=1, keepdims=True)
        weights = jnp.exp(scores - top)
        total = jnp.sum(weights, axis=1, keepdims=True)
        summed = jnp.dot(
            weights.astype(jnp.bfloat16), v_ref[:, lanes], preferred_element_type=jnp.float32
        )
        o_ref[:, lanes] = (summed / total).astype(o_ref.dtype)


def attention(query, w_key_t, w_value, sources, heads):
    tokens, channels = query.shape
    length = sum(source.shape[0] for source in sources)
    whole = lambda array: pl.BlockSpec(array.shape, lambda i: (0, 0))
    operands = (query, w_key_t, w_value) + tuple(sources)
    return pl.pallas_call(
        functools.partial(attention_kernel, heads, len(sources)),
        out_shape=jax.ShapeDtypeStruct((tokens, channels), jnp.bfloat16),
        grid=(1,),
        in_specs=[whole(array) for array in operands],
        out_specs=pl.BlockSpec((tokens, channels), lambda i: (0, 0)),
        scratch_shapes=[
            pltpu.VMEM((channels, length), jnp.bfloat16),
            pltpu.VMEM((length, channels), jnp.bfloat16),
        ],
    )(*operands)


def doubling_gather(value, axis):
    size = lax.axis_size(axis)
    step = 1
    while step < size:
        pairs = [(j, j ^ step) for j in range(size)]
        value = jnp.concatenate([value, lax.ppermute(value, axis, pairs)], axis=0)
        step *= 2
    return value


def shards(frames, conv_weight, conv_bias, ref_features, w_query, w_key, w_value, w_out, out_bias):
    count, band_rows, width, channels = frames.shape
    heads = channels // HD
    band = band_rows * width
    activated = jax.nn.silu(frames.astype(jnp.float32)).astype(jnp.bfloat16)
    padded = extended(activated, ROW_PARTS, 1, 1)
    padded = jnp.pad(padded, ((0, 0), (0, 0), (1, 1), (0, 0)))
    convolved = jnp.zeros((count * band, channels), jnp.float32)
    for row_tap in range(3):
        for col_tap in range(3):
            window = padded[:, row_tap : row_tap + band_rows, col_tap : col_tap + width].reshape(
                count * band, channels
            )
            convolved = convolved + jnp.dot(
                window, conv_weight[row_tap, col_tap], preferred_element_type=jnp.float32
            )
    hidden = (
        frames.reshape(count * band, channels).astype(jnp.float32) + convolved + conv_bias
    ).astype(jnp.bfloat16)
    rows = lax.axis_size(ROW_PARTS)
    others = [
        lax.ppermute(hidden, ROW_PARTS, [(j, (j + shift) % rows) for j in range(rows)])
        for shift in range(1, rows)
    ]
    query = jnp.dot(hidden, w_query, preferred_element_type=jnp.float32).astype(jnp.bfloat16)
    every_feature = staged_gather(ref_features, query)
    sources = [hidden] + others + [every_feature]
    mixed = attention(query, jnp.transpose(w_key), w_value, sources, heads)
    attended = (jnp.dot(mixed, w_out, preferred_element_type=jnp.float32) + out_bias).astype(
        jnp.bfloat16
    )
    return (
        hidden.reshape(count, band_rows, width, channels),
        attended.reshape(count, band_rows, width, channels),
    )


def solution(mesh):
    fine = fine_mesh(mesh)
    blocks = P(TM_PARTS, ROW_PARTS, None, None)
    return jax.shard_map(
        shards,
        mesh=fine,
        in_specs=(blocks, P(), P(), P(TM_PARTS, None), P(), P(), P(), P(), P()),
        out_specs=(blocks, blocks),
        check_vma=False,
    )
```

```python
import functools

import jax
import jax.numpy as jnp
import numpy as np
from jax import lax
from jax.experimental import pallas as pl
from jax.experimental.pallas import tpu as pltpu
from jax.sharding import Mesh
from jax.sharding import PartitionSpec as P

HD = 80


MESH = pl.DeviceIdType.MESH
TM_PARTS = ("y_hi", "x", "z")
ROW_PARTS = ("y_lo", "core")


def distinct(values):
    return len(set(values))


def fine_mesh(mesh):
    devices = np.asarray(mesh.devices)
    tm, rows = devices.shape
    try:
        column = devices[:, 0]
        nx = distinct(d.coords[0] for d in column)
        nz = distinct(d.coords[2] for d in column)
        cores = distinct(d.core_on_chip for d in devices[0])
    except (AttributeError, IndexError, TypeError):
        nx, nz, cores = tm, 1, rows
    if tm % (nx * nz) or rows % cores:
        nx, nz, cores = tm, 1, rows
    shape = (tm // (nx * nz), nx, nz, rows // cores, cores)
    return Mesh(devices.reshape(shape), TM_PARTS + ROW_PARTS)


def staged_kernel(sizes, x_ref, after_ref, out_ref, local_sem, *sems):
    high, across, along = sizes
    plane = across * along
    half = plane // 2
    yh, xx, zz = [lax.axis_index(axis) for axis in TM_PARTS]
    low, core = [lax.axis_index(axis) for axis in ROW_PARTS]
    spot = xx * along + zz
    me = yh * plane + spot

    def plane_peer(shift):
        place = lax.rem(spot + shift, plane)
        return {"x": place // along, "z": lax.rem(place, along)}

    y_peer = {"y_hi": 1 - yh, "y_lo": 1 - low}
    c_peer = {"core": 1 - core}
    peers = [plane_peer(shift) for shift in range(1, plane)] + [y_peer, c_peer]
    barrier = pltpu.get_barrier_semaphore()
    for peer in peers:
        pl.semaphore_signal(barrier, inc=1, device_id=peer, device_id_type=MESH)
    pl.semaphore_wait(barrier, len(peers))
    own = out_ref.at[pl.ds(me, 1)]
    local = pltpu.make_async_copy(x_ref, own, local_sem)
    local.start()
    local.wait()

    def exchange(pairs, send_sem, recv_sem):
        copies = []
        for index, (ref, peer) in enumerate(pairs):
            copy = pltpu.make_async_remote_copy(
                src_ref=ref,
                dst_ref=ref,
                send_sem=send_sem.at[index],
                recv_sem=recv_sem.at[index],
                device_id=peer,
                device_id_type=MESH,
            )
            copy.start()
            copies.append(copy)
        for copy in copies:
            copy.wait()

    exchange([(own, plane_peer(shift)) for shift in range(1, plane)], sems[0], sems[1])
    mine = out_ref.at[pl.ds(yh * plane + core * half, half)]
    exchange([(mine, y_peer)], sems[2], sems[3])
    theirs = out_ref.at[pl.ds((1 - yh) * plane + core * half, half)]
    exchange([(theirs, c_peer)], sems[4], sems[5])


def staged_gather(value, after):
    sizes = [lax.axis_size(axis) for axis in TM_PARTS]
    total = sizes[0] * sizes[1] * sizes[2]
    sems = []
    for count in (sizes[1] * sizes[2], 1, 1):
        sems += [pltpu.SemaphoreType.DMA((count,))] * 2
    gathered = pl.pallas_call(
        functools.partial(staged_kernel, sizes),
        out_shape=jax.ShapeDtypeStruct((total,) + value.shape, value.dtype),
        in_specs=[pl.BlockSpec(memory_space=pl.ANY)] * 2,
        out_specs=pl.BlockSpec(memory_space=pl.ANY),
        scratch_shapes=[pltpu.SemaphoreType.DMA] + sems,
        compiler_params=pltpu.CompilerParams(collective_id=0, has_side_effects=True),
    )(value[None], after)
    return gathered.reshape((total * value.shape[0],) + value.shape[1:])


def extended(value, axis, dim, width):
    size = lax.axis_size(axis)
    length = value.shape[dim]
    up = [(i, i + 1) for i in range(size - 1)]
    down = [(j, i) for i, j in up]
    last = lax.slice_in_dim(value, length - width, length, axis=dim)
    initial = lax.slice_in_dim(value, 0, width, axis=dim)
    before = lax.ppermute(last, axis, up)
    after = lax.ppermute(initial, axis, down)
    return jnp.concatenate([before, value, after], axis=dim)


def attend_block(state, query_heads, keys, values, heads):
    top, total, summed = state
    length = keys.shape[0]
    key_heads = keys.reshape(length, heads, HD)
    value_heads = values.reshape(length, heads, HD)
    scores = jnp.einsum(
        "qhd,khd->hqk", query_heads, key_heads, preferred_element_type=jnp.float32
    )
    scores = scores * HD ** (-0.5)
    block_top = jnp.max(scores, axis=2)
    new_top = block_top if top is None else jnp.maximum(top, block_top)
    weights = jnp.exp(scores - new_top[..., None])
    block_total = jnp.sum(weights, axis=2)
    product = jnp.einsum(
        "hqk,khd->hqd",
        weights.astype(jnp.bfloat16),
        value_heads,
        preferred_element_type=jnp.float32,
    )
    if top is None:
        return (new_top, block_total, product)
    factor = jnp.exp(top - new_top)
    return (new_top, total * factor + block_total, summed * factor[..., None] + product)


def attention_kernel(heads, parts, *refs):
    q_ref, wk_ref, wv_ref = refs[:3]
    sources = refs[3 : 3 + parts]
    o_ref, k_ref, v_ref = refs[3 + parts :]
    offset = 0
    for source in sources:
        rows = source.shape[0]
        k_ref[:, offset : offset + rows] = lax.dot_general(
            wk_ref[...], source[...], (((1,), (1,)), ((), ())), preferred_element_type=jnp.float32
        ).astype(k_ref.dtype)
        v_ref[offset : offset + rows, :] = jnp.dot(
            source[...], wv_ref[...], preferred_element_type=jnp.float32
        ).astype(v_ref.dtype)
        offset += rows
    for head in range(heads):
        lanes = slice(head * HD, (head + 1) * HD)
        scores = jnp.dot(q_ref[:, lanes], k_ref[lanes, :], preferred_element_type=jnp.float32)
        scores = scores * HD ** (-0.5)
        top = jnp.max(scores, axis=1, keepdims=True)
        weights = jnp.exp(scores - top)
        total = jnp.sum(weights, axis=1, keepdims=True)
        summed = jnp.dot(
            weights.astype(jnp.bfloat16), v_ref[:, lanes], preferred_element_type=jnp.float32
        )
        o_ref[:, lanes] = (summed / total).astype(o_ref.dtype)


def attention(query, w_key_t, w_value, sources, heads):
    tokens, channels = query.shape
    length = sum(source.shape[0] for source in sources)
    whole = lambda array: pl.BlockSpec(array.shape, lambda i: (0, 0))
    operands = (query, w_key_t, w_value) + tuple(sources)
    return pl.pallas_call(
        functools.partial(attention_kernel, heads, len(sources)),
        out_shape=jax.ShapeDtypeStruct((tokens, channels), jnp.bfloat16),
        grid=(1,),
        in_specs=[whole(array) for array in operands],
        out_specs=pl.BlockSpec((tokens, channels), lambda i: (0, 0)),
        scratch_shapes=[
            pltpu.VMEM((channels, length), jnp.bfloat16),
            pltpu.VMEM((length, channels), jnp.bfloat16),
        ],
    )(*operands)


def doubling_gather(value, axis):
    size = lax.axis_size(axis)
    step = 1
    while step < size:
        pairs = [(j, j ^ step) for j in range(size)]
        value = jnp.concatenate([value, lax.ppermute(value, axis, pairs)], axis=0)
        step *= 2
    return value


def shards(frames, conv_weight, conv_bias, ref_features, w_query, w_key, w_value, w_out, out_bias):
    count, band_rows, width, channels = frames.shape
    heads = channels // HD
    band = band_rows * width
    activated = jax.nn.silu(frames.astype(jnp.float32)).astype(jnp.bfloat16)
    padded = extended(activated, ROW_PARTS, 1, 1)
    padded = jnp.pad(padded, ((0, 0), (0, 0), (1, 1), (0, 0)))
    convolved = jnp.zeros((count * band, channels), jnp.float32)
    for row_tap in range(3):
        for col_tap in range(3):
            window = padded[:, row_tap : row_tap + band_rows, col_tap : col_tap + width].reshape(
                count * band, channels
            )
            convolved = convolved + jnp.dot(
                window, conv_weight[row_tap, col_tap], preferred_element_type=jnp.float32
            )
    hidden = (
        frames.reshape(count * band, channels).astype(jnp.float32) + convolved + conv_bias
    ).astype(jnp.bfloat16)
    rows = lax.axis_size(ROW_PARTS)
    others = [
        lax.ppermute(hidden, ROW_PARTS, [(j, (j + shift) % rows) for j in range(rows)])
        for shift in range(1, rows)
    ]
    query = jnp.dot(hidden, w_query, preferred_element_type=jnp.float32).astype(jnp.bfloat16)
    every_feature = staged_gather(ref_features, query)
    sources = [hidden] + others + [every_feature]
    mixed = attention(query, jnp.transpose(w_key), w_value, sources, heads)
    attended = (jnp.dot(mixed, w_out, preferred_element_type=jnp.float32) + out_bias).astype(
        jnp.bfloat16
    )
    return (
        hidden.reshape(count, band_rows, width, channels),
        attended.reshape(count, band_rows, width, channels),
    )


def solution(mesh):
    fine = fine_mesh(mesh)
    blocks = P(TM_PARTS, ROW_PARTS, None, None)
    return jax.shard_map(
        shards,
        mesh=fine,
        in_specs=(blocks, P(), P(), P(TM_PARTS, None), P(), P(), P(), P(), P()),
        out_specs=(blocks, blocks),
        check_vma=False,
    )
```

```python
import functools

import jax
import jax.numpy as jnp
import numpy as np
from jax import lax
from jax.experimental import pallas as pl
from jax.experimental.pallas import tpu as pltpu
from jax.sharding import Mesh
from jax.sharding import PartitionSpec as P

HD = 80


MESH = pl.DeviceIdType.MESH
TM_PARTS = ("y_hi", "x", "z")
ROW_PARTS = ("y_lo", "core")


def distinct(values):
    return len(set(values))


def fine_mesh(mesh):
    devices = np.asarray(mesh.devices)
    tm, rows = devices.shape
    try:
        column = devices[:, 0]
        nx = distinct(d.coords[0] for d in column)
        nz = distinct(d.coords[2] for d in column)
        cores = distinct(d.core_on_chip for d in devices[0])
    except (AttributeError, IndexError, TypeError):
        nx, nz, cores = tm, 1, rows
    if tm % (nx * nz) or rows % cores:
        nx, nz, cores = tm, 1, rows
    shape = (tm // (nx * nz), nx, nz, rows // cores, cores)
    return Mesh(devices.reshape(shape), TM_PARTS + ROW_PARTS)


def staged_kernel(sizes, x_ref, after_ref, out_ref, local_sem, *sems):
    high, across, along = sizes
    half = along // 2
    yh, xx, zz = [lax.axis_index(axis) for axis in TM_PARTS]
    low, core = [lax.axis_index(axis) for axis in ROW_PARTS]
    me = (yh * across + xx) * along + zz
    mine = me - zz
    other_core = 1 - core
    z_peer = lambda shift: {"z": lax.rem(zz + shift, along)}
    x_peer = lambda shift: {"x": lax.rem(xx + shift, across)}
    y_peer = {"y_hi": 1 - yh, "y_lo": 1 - low}
    c_peer = {"core": other_core}
    peers = [z_peer(s) for s in range(1, along)] + [x_peer(s) for s in range(1, across)]
    peers += [y_peer, c_peer]
    barrier = pltpu.get_barrier_semaphore()
    for peer in peers:
        pl.semaphore_signal(barrier, inc=1, device_id=peer, device_id_type=MESH)
    pl.semaphore_wait(barrier, len(peers))
    local = pltpu.make_async_copy(x_ref, out_ref.at[pl.ds(me, 1)], local_sem)
    local.start()
    local.wait()

    def exchange(pairs, send_sem, recv_sem):
        copies = []
        for index, (ref, peer) in enumerate(pairs):
            copy = pltpu.make_async_remote_copy(
                src_ref=ref,
                dst_ref=ref,
                send_sem=send_sem.at[index],
                recv_sem=recv_sem.at[index],
                device_id=peer,
                device_id_type=MESH,
            )
            copy.start()
            copies.append(copy)
        for copy in copies:
            copy.wait()

    own = out_ref.at[pl.ds(me, 1)]
    exchange([(own, z_peer(s)) for s in range(1, along)], sems[0], sems[1])
    start = mine + core * half
    part = out_ref.at[pl.ds(start, half)]
    exchange([(part, x_peer(s)) for s in range(1, across)], sems[2], sems[3])
    base = yh * across * along + core * half
    chunks = [out_ref.at[pl.ds(base + g * along, half)] for g in range(across)]
    exchange([(chunk, y_peer) for chunk in chunks], sems[4], sems[5])
    regions = high * across
    region = yh * across + xx
    groups = []
    for step in range(1, regions):
        j = lax.rem(region + step, regions)
        groups.append(out_ref.at[pl.ds(j * along + core * half, half)])
    exchange([(chunk, c_peer) for chunk in groups], sems[6], sems[7])


def staged_gather(value, after):
    sizes = [lax.axis_size(axis) for axis in TM_PARTS]
    total = sizes[0] * sizes[1] * sizes[2]
    sems = []
    for count in (sizes[2], sizes[1], sizes[1], sizes[0] * sizes[1]):
        sems += [pltpu.SemaphoreType.DMA((count,))] * 2
    gathered = pl.pallas_call(
        functools.partial(staged_kernel, sizes),
        out_shape=jax.ShapeDtypeStruct((total,) + value.shape, value.dtype),
        in_specs=[pl.BlockSpec(memory_space=pl.ANY)] * 2,
        out_specs=pl.BlockSpec(memory_space=pl.ANY),
        scratch_shapes=[pltpu.SemaphoreType.DMA] + sems,
        compiler_params=pltpu.CompilerParams(collective_id=0, has_side_effects=True),
    )(value[None], after)
    return gathered.reshape((total * value.shape[0],) + value.shape[1:])


def extended(value, axis, dim, width):
    size = lax.axis_size(axis)
    length = value.shape[dim]
    up = [(i, i + 1) for i in range(size - 1)]
    down = [(j, i) for i, j in up]
    last = lax.slice_in_dim(value, length - width, length, axis=dim)
    initial = lax.slice_in_dim(value, 0, width, axis=dim)
    before = lax.ppermute(last, axis, up)
    after = lax.ppermute(initial, axis, down)
    return jnp.concatenate([before, value, after], axis=dim)


def attend_block(state, query_heads, keys, values, heads):
    top, total, summed = state
    length = keys.shape[0]
    key_heads = keys.reshape(length, heads, HD)
    value_heads = values.reshape(length, heads, HD)
    scores = jnp.einsum(
        "qhd,khd->hqk", query_heads, key_heads, preferred_element_type=jnp.float32
    )
    scores = scores * HD ** (-0.5)
    block_top = jnp.max(scores, axis=2)
    new_top = block_top if top is None else jnp.maximum(top, block_top)
    weights = jnp.exp(scores - new_top[..., None])
    block_total = jnp.sum(weights, axis=2)
    product = jnp.einsum(
        "hqk,khd->hqd",
        weights.astype(jnp.bfloat16),
        value_heads,
        preferred_element_type=jnp.float32,
    )
    if top is None:
        return (new_top, block_total, product)
    factor = jnp.exp(top - new_top)
    return (new_top, total * factor + block_total, summed * factor[..., None] + product)


def attention_kernel(heads, parts, *refs):
    q_ref, wk_ref, wv_ref, wo_ref, bias_ref = refs[:5]
    sources = refs[5 : 5 + parts]
    o_ref, k_ref, v_ref, mixed_ref = refs[5 + parts :]
    offset = 0
    for source in sources:
        rows = source.shape[0]
        k_ref[:, offset : offset + rows] = lax.dot_general(
            wk_ref[...], source[...], (((0,), (1,)), ((), ())), preferred_element_type=jnp.float32
        ).astype(k_ref.dtype)
        v_ref[offset : offset + rows, :] = jnp.dot(
            source[...], wv_ref[...], preferred_element_type=jnp.float32
        ).astype(v_ref.dtype)
        offset += rows
    for head in range(heads):
        lanes = slice(head * HD, (head + 1) * HD)
        scores = jnp.dot(q_ref[:, lanes], k_ref[lanes, :], preferred_element_type=jnp.float32)
        scores = scores * HD ** (-0.5)
        top = jnp.max(scores, axis=1, keepdims=True)
        weights = jnp.exp(scores - top)
        total = jnp.sum(weights, axis=1, keepdims=True)
        summed = jnp.dot(
            weights.astype(jnp.bfloat16), v_ref[:, lanes], preferred_element_type=jnp.float32
        )
        mixed_ref[:, lanes] = (summed / total).astype(mixed_ref.dtype)
    attended = jnp.dot(mixed_ref[...], wo_ref[...], preferred_element_type=jnp.float32)
    o_ref[...] = (attended + bias_ref[...]).astype(o_ref.dtype)


def attention(query, w_key, w_value, w_out, out_bias, sources, heads):
    tokens, channels = query.shape
    length = sum(source.shape[0] for source in sources)
    whole = lambda array: pl.BlockSpec(array.shape, lambda i: (0, 0))
    operands = (query, w_key, w_value, w_out, out_bias.reshape(1, -1)) + tuple(sources)
    return pl.pallas_call(
        functools.partial(attention_kernel, heads, len(sources)),
        out_shape=jax.ShapeDtypeStruct((tokens, channels), jnp.bfloat16),
        grid=(1,),
        in_specs=[whole(array) for array in operands],
        out_specs=pl.BlockSpec((tokens, channels), lambda i: (0, 0)),
        scratch_shapes=[
            pltpu.VMEM((channels, length), jnp.bfloat16),
            pltpu.VMEM((length, channels), jnp.bfloat16),
            pltpu.VMEM((tokens, channels), jnp.bfloat16),
        ],
    )(*operands)


def doubling_gather(value, axis):
    size = lax.axis_size(axis)
    step = 1
    while step < size:
        pairs = [(j, j ^ step) for j in range(size)]
        value = jnp.concatenate([value, lax.ppermute(value, axis, pairs)], axis=0)
        step *= 2
    return value


def shards(frames, conv_weight, conv_bias, ref_features, w_query, w_key, w_value, w_out, out_bias):
    count, band_rows, width, channels = frames.shape
    heads = channels // HD
    band = band_rows * width
    activated = jax.nn.silu(frames.astype(jnp.float32)).astype(jnp.bfloat16)
    padded = extended(activated, ROW_PARTS, 1, 1)
    padded = jnp.pad(padded, ((0, 0), (0, 0), (1, 1), (0, 0)))
    convolved = jnp.zeros((count * band, channels), jnp.float32)
    for row_tap in range(3):
        for col_tap in range(3):
            window = padded[:, row_tap : row_tap + band_rows, col_tap : col_tap + width].reshape(
                count * band, channels
            )
            convolved = convolved + jnp.dot(
                window, conv_weight[row_tap, col_tap], preferred_element_type=jnp.float32
            )
    hidden = (
        frames.reshape(count * band, channels).astype(jnp.float32) + convolved + conv_bias
    ).astype(jnp.bfloat16)
    rows = lax.axis_size(ROW_PARTS)
    others = [
        lax.ppermute(hidden, ROW_PARTS, [(j, (j + shift) % rows) for j in range(rows)])
        for shift in range(1, rows)
    ]
    query = jnp.dot(hidden, w_query, preferred_element_type=jnp.float32).astype(jnp.bfloat16)
    every_feature = staged_gather(ref_features, query)
    sources = [hidden] + others + [every_feature]
    attended = attention(query, w_key, w_value, w_out, out_bias, sources, heads)
    return (
        hidden.reshape(count, band_rows, width, channels),
        attended.reshape(count, band_rows, width, channels),
    )


def solution(mesh):
    fine = fine_mesh(mesh)
    blocks = P(TM_PARTS, ROW_PARTS, None, None)
    return jax.shard_map(
        shards,
        mesh=fine,
        in_specs=(blocks, P(), P(), P(TM_PARTS, None), P(), P(), P(), P(), P()),
        out_specs=(blocks, blocks),
        check_vma=False,
    )
```

```python
import functools

import jax
import jax.numpy as jnp
import numpy as np
from jax import lax
from jax.experimental import pallas as pl
from jax.experimental.pallas import tpu as pltpu
from jax.sharding import Mesh
from jax.sharding import PartitionSpec as P

HD = 80


MESH = pl.DeviceIdType.MESH
TM_PARTS = ("y_hi", "x", "z")
ROW_PARTS = ("y_lo", "core")


def distinct(values):
    return len(set(values))


def fine_mesh(mesh):
    devices = np.asarray(mesh.devices)
    tm, rows = devices.shape
    try:
        column = devices[:, 0]
        nx = distinct(d.coords[0] for d in column)
        nz = distinct(d.coords[2] for d in column)
        cores = distinct(d.core_on_chip for d in devices[0])
    except (AttributeError, IndexError, TypeError):
        nx, nz, cores = tm, 1, rows
    if tm % (nx * nz) or rows % cores:
        nx, nz, cores = tm, 1, rows
    shape = (tm // (nx * nz), nx, nz, rows // cores, cores)
    return Mesh(devices.reshape(shape), TM_PARTS + ROW_PARTS)


def staged_kernel(sizes, x_ref, after_ref, out_ref, local_sem, *sems):
    high, across, along = sizes
    half = along // 2
    yh, xx, zz = [lax.axis_index(axis) for axis in TM_PARTS]
    low, core = [lax.axis_index(axis) for axis in ROW_PARTS]
    me = (yh * across + xx) * along + zz
    mine = me - zz
    other_core = 1 - core
    z_peer = lambda shift: {"z": lax.rem(zz + shift, along)}
    x_peer = lambda shift: {"x": lax.rem(xx + shift, across)}
    y_peer = {"y_hi": 1 - yh, "y_lo": 1 - low}
    c_peer = {"core": other_core}
    peers = [z_peer(s) for s in range(1, along)] + [x_peer(s) for s in range(1, across)]
    peers += [y_peer, c_peer]
    barrier = pltpu.get_barrier_semaphore()
    for peer in peers:
        pl.semaphore_signal(barrier, inc=1, device_id=peer, device_id_type=MESH)
    pl.semaphore_wait(barrier, len(peers))
    local = pltpu.make_async_copy(x_ref, out_ref.at[pl.ds(me, 1)], local_sem)
    local.start()
    local.wait()

    def exchange(pairs, send_sem, recv_sem):
        copies = []
        for index, (ref, peer) in enumerate(pairs):
            copy = pltpu.make_async_remote_copy(
                src_ref=ref,
                dst_ref=ref,
                send_sem=send_sem.at[index],
                recv_sem=recv_sem.at[index],
                device_id=peer,
                device_id_type=MESH,
            )
            copy.start()
            copies.append(copy)
        for copy in copies:
            copy.wait()

    own = out_ref.at[pl.ds(me, 1)]
    exchange([(own, z_peer(s)) for s in range(1, along)], sems[0], sems[1])
    start = mine + core * half
    part = out_ref.at[pl.ds(start, half)]
    exchange([(part, x_peer(s)) for s in range(1, across)], sems[2], sems[3])
    base = yh * across * along + core * half
    chunks = [out_ref.at[pl.ds(base + g * along, half)] for g in range(across)]
    exchange([(chunk, y_peer) for chunk in chunks], sems[4], sems[5])
    regions = high * across
    region = yh * across + xx
    groups = []
    for step in range(1, regions):
        j = lax.rem(region + step, regions)
        groups.append(out_ref.at[pl.ds(j * along + core * half, half)])
    exchange([(chunk, c_peer) for chunk in groups], sems[6], sems[7])


def staged_gather(value, after):
    sizes = [lax.axis_size(axis) for axis in TM_PARTS]
    total = sizes[0] * sizes[1] * sizes[2]
    sems = []
    for count in (sizes[2], sizes[1], sizes[1], sizes[0] * sizes[1]):
        sems += [pltpu.SemaphoreType.DMA((count,))] * 2
    gathered = pl.pallas_call(
        functools.partial(staged_kernel, sizes),
        out_shape=jax.ShapeDtypeStruct((total,) + value.shape, value.dtype),
        in_specs=[pl.BlockSpec(memory_space=pl.ANY)] * 2,
        out_specs=pl.BlockSpec(memory_space=pl.ANY),
        scratch_shapes=[pltpu.SemaphoreType.DMA] + sems,
        compiler_params=pltpu.CompilerParams(collective_id=0, has_side_effects=True),
    )(value[None], after)
    return gathered.reshape((total * value.shape[0],) + value.shape[1:])


def extended(value, axis, dim, width):
    size = lax.axis_size(axis)
    length = value.shape[dim]
    up = [(i, i + 1) for i in range(size - 1)]
    down = [(j, i) for i, j in up]
    last = lax.slice_in_dim(value, length - width, length, axis=dim)
    initial = lax.slice_in_dim(value, 0, width, axis=dim)
    before = lax.ppermute(last, axis, up)
    after = lax.ppermute(initial, axis, down)
    return jnp.concatenate([before, value, after], axis=dim)


def attend_block(state, query_heads, keys, values, heads):
    top, total, summed = state
    length = keys.shape[0]
    key_heads = keys.reshape(length, heads, HD)
    value_heads = values.reshape(length, heads, HD)
    scores = jnp.einsum(
        "qhd,khd->hqk", query_heads, key_heads, preferred_element_type=jnp.float32
    )
    scores = scores * HD ** (-0.5)
    block_top = jnp.max(scores, axis=2)
    new_top = block_top if top is None else jnp.maximum(top, block_top)
    weights = jnp.exp(scores - new_top[..., None])
    block_total = jnp.sum(weights, axis=2)
    product = jnp.einsum(
        "hqk,khd->hqd",
        weights.astype(jnp.bfloat16),
        value_heads,
        preferred_element_type=jnp.float32,
    )
    if top is None:
        return (new_top, block_total, product)
    factor = jnp.exp(top - new_top)
    return (new_top, total * factor + block_total, summed * factor[..., None] + product)


def attention_kernel(heads, parts, *refs):
    wq_ref, wk_ref, wv_ref, wo_ref, bias_ref = refs[:5]
    sources = refs[5 : 5 + parts]
    o_ref, k_ref, v_ref, mixed_ref, q_ref = refs[5 + parts :]
    q_ref[...] = jnp.dot(
        sources[0][...], wq_ref[...], preferred_element_type=jnp.float32
    ).astype(q_ref.dtype)
    offset = 0
    for source in sources:
        rows = source.shape[0]
        k_ref[:, offset : offset + rows] = lax.dot_general(
            wk_ref[...], source[...], (((0,), (1,)), ((), ())), preferred_element_type=jnp.float32
        ).astype(k_ref.dtype)
        v_ref[offset : offset + rows, :] = jnp.dot(
            source[...], wv_ref[...], preferred_element_type=jnp.float32
        ).astype(v_ref.dtype)
        offset += rows
    for head in range(heads):
        lanes = slice(head * HD, (head + 1) * HD)
        scores = jnp.dot(q_ref[:, lanes], k_ref[lanes, :], preferred_element_type=jnp.float32)
        scores = scores * HD ** (-0.5)
        top = jnp.max(scores, axis=1, keepdims=True)
        weights = jnp.exp(scores - top)
        total = jnp.sum(weights, axis=1, keepdims=True)
        summed = jnp.dot(
            weights.astype(jnp.bfloat16), v_ref[:, lanes], preferred_element_type=jnp.float32
        )
        mixed_ref[:, lanes] = (summed / total).astype(mixed_ref.dtype)
    attended = jnp.dot(mixed_ref[...], wo_ref[...], preferred_element_type=jnp.float32)
    o_ref[...] = (attended + bias_ref[...]).astype(o_ref.dtype)


def attention(w_query, w_key, w_value, w_out, out_bias, sources, heads):
    tokens, channels = sources[0].shape
    length = sum(source.shape[0] for source in sources)
    whole = lambda array: pl.BlockSpec(array.shape, lambda i: (0, 0))
    operands = (w_query, w_key, w_value, w_out, out_bias.reshape(1, -1)) + tuple(sources)
    return pl.pallas_call(
        functools.partial(attention_kernel, heads, len(sources)),
        out_shape=jax.ShapeDtypeStruct((tokens, channels), jnp.bfloat16),
        grid=(1,),
        in_specs=[whole(array) for array in operands],
        out_specs=pl.BlockSpec((tokens, channels), lambda i: (0, 0)),
        scratch_shapes=[
            pltpu.VMEM((channels, length), jnp.bfloat16),
            pltpu.VMEM((length, channels), jnp.bfloat16),
            pltpu.VMEM((tokens, channels), jnp.bfloat16),
            pltpu.VMEM((tokens, channels), jnp.bfloat16),
        ],
    )(*operands)


def doubling_gather(value, axis):
    size = lax.axis_size(axis)
    step = 1
    while step < size:
        pairs = [(j, j ^ step) for j in range(size)]
        value = jnp.concatenate([value, lax.ppermute(value, axis, pairs)], axis=0)
        step *= 2
    return value


def shards(frames, conv_weight, conv_bias, ref_features, w_query, w_key, w_value, w_out, out_bias):
    count, band_rows, width, channels = frames.shape
    heads = channels // HD
    band = band_rows * width
    activated = jax.nn.silu(frames.astype(jnp.float32)).astype(jnp.bfloat16)
    padded = extended(activated, ROW_PARTS, 1, 1)
    padded = jnp.pad(padded, ((0, 0), (0, 0), (1, 1), (0, 0)))
    convolved = jnp.zeros((count * band, channels), jnp.float32)
    for row_tap in range(3):
        for col_tap in range(3):
            window = padded[:, row_tap : row_tap + band_rows, col_tap : col_tap + width].reshape(
                count * band, channels
            )
            convolved = convolved + jnp.dot(
                window, conv_weight[row_tap, col_tap], preferred_element_type=jnp.float32
            )
    hidden = (
        frames.reshape(count * band, channels).astype(jnp.float32) + convolved + conv_bias
    ).astype(jnp.bfloat16)
    rows = lax.axis_size(ROW_PARTS)
    others = [
        lax.ppermute(hidden, ROW_PARTS, [(j, (j + shift) % rows) for j in range(rows)])
        for shift in range(1, rows)
    ]
    every_feature = staged_gather(ref_features, hidden)
    sources = [hidden] + others + [every_feature]
    attended = attention(w_query, w_key, w_value, w_out, out_bias, sources, heads)
    return (
        hidden.reshape(count, band_rows, width, channels),
        attended.reshape(count, band_rows, width, channels),
    )


def solution(mesh):
    fine = fine_mesh(mesh)
    blocks = P(TM_PARTS, ROW_PARTS, None, None)
    return jax.shard_map(
        shards,
        mesh=fine,
        in_specs=(blocks, P(), P(), P(TM_PARTS, None), P(), P(), P(), P(), P()),
        out_specs=(blocks, blocks),
        check_vma=False,
    )
```

```python
import functools

import jax
import jax.numpy as jnp
import numpy as np
from jax import lax
from jax.experimental import pallas as pl
from jax.experimental.pallas import tpu as pltpu
from jax.sharding import Mesh
from jax.sharding import PartitionSpec as P

HD = 80


MESH = pl.DeviceIdType.MESH
TM_PARTS = ("y_hi", "x", "z")
ROW_PARTS = ("y_lo", "core")


def distinct(values):
    return len(set(values))


def fine_mesh(mesh):
    devices = np.asarray(mesh.devices)
    tm, rows = devices.shape
    try:
        column = devices[:, 0]
        nx = distinct(d.coords[0] for d in column)
        nz = distinct(d.coords[2] for d in column)
        cores = distinct(d.core_on_chip for d in devices[0])
    except (AttributeError, IndexError, TypeError):
        nx, nz, cores = tm, 1, rows
    if tm % (nx * nz) or rows % cores:
        nx, nz, cores = tm, 1, rows
    shape = (tm // (nx * nz), nx, nz, rows // cores, cores)
    return Mesh(devices.reshape(shape), TM_PARTS + ROW_PARTS)


def staged_kernel(sizes, x_ref, after_ref, out_ref, local_sem, *sems):
    high, across, along = sizes
    half = along // 2
    yh, xx, zz = [lax.axis_index(axis) for axis in TM_PARTS]
    low, core = [lax.axis_index(axis) for axis in ROW_PARTS]
    z_peer = lambda shift: {"z": lax.rem(zz + shift, along)}
    x_peer = lambda shift: {"x": lax.rem(xx + shift, across)}
    y_peer = {"y_hi": 1 - yh, "y_lo": 1 - low}
    c_peer = {"core": 1 - core}
    peers = [z_peer(s) for s in range(1, along)] + [x_peer(s) for s in range(1, across)]
    peers += [y_peer, c_peer]
    barrier = pltpu.get_barrier_semaphore()
    for peer in peers:
        pl.semaphore_signal(barrier, inc=1, device_id=peer, device_id_type=MESH)
    pl.semaphore_wait(barrier, len(peers))

    def block_of(z):
        return ((z // half * high + yh) * across + xx) * half + lax.rem(z, half)

    own = out_ref.at[pl.ds(block_of(zz), 1)]
    mine = zz // half == core

    @pl.when(mine)
    def _():
        local = pltpu.make_async_copy(x_ref, own, local_sem)
        local.start()
        local.wait()

    def remote(ref, peer, send_sem, recv_sem):
        return pltpu.make_async_remote_copy(
            src_ref=ref,
            dst_ref=ref,
            send_sem=send_sem,
            recv_sem=recv_sem,
            device_id=peer,
            device_id_type=MESH,
        )

    z_copies = [remote(own, z_peer(s), sems[0].at[s], sems[1].at[s]) for s in range(1, along)]

    @pl.when(mine)
    def _():
        for copy in z_copies:
            copy.start()
        for copy in z_copies:
            copy.wait_send()

    for s, copy in zip(range(1, along), z_copies):
        sender = lax.rem(zz + along - s, along)

        @pl.when(sender // half == core)
        def _():
            copy.wait_recv()

    def exchange(pairs, send_sem, recv_sem):
        copies = [remote(ref, peer, send_sem.at[i], recv_sem.at[i]) for i, (ref, peer) in enumerate(pairs)]
        for copy in copies:
            copy.start()
        for copy in copies:
            copy.wait()

    group = out_ref.at[pl.ds(((core * high + yh) * across + xx) * half, half)]
    exchange([(group, x_peer(s)) for s in range(1, across)], sems[2], sems[3])
    row = out_ref.at[pl.ds((core * high + yh) * across * half, across * half)]
    exchange([(row, y_peer)], sems[4], sems[5])
    whole = out_ref.at[pl.ds(core * high * across * half, high * across * half)]
    exchange([(whole, c_peer)], sems[6], sems[7])


def staged_gather(value, after):
    sizes = [lax.axis_size(axis) for axis in TM_PARTS]
    total = sizes[0] * sizes[1] * sizes[2]
    sems = []
    for count in (sizes[2], sizes[1], 1, 1):
        sems += [pltpu.SemaphoreType.DMA((count,))] * 2
    gathered = pl.pallas_call(
        functools.partial(staged_kernel, sizes),
        out_shape=jax.ShapeDtypeStruct((total,) + value.shape, value.dtype),
        in_specs=[pl.BlockSpec(memory_space=pl.ANY)] * 2,
        out_specs=pl.BlockSpec(memory_space=pl.ANY),
        scratch_shapes=[pltpu.SemaphoreType.DMA] + sems,
        compiler_params=pltpu.CompilerParams(collective_id=0, has_side_effects=True),
    )(value[None], after)
    return gathered.reshape((total * value.shape[0],) + value.shape[1:])


def extended(value, axis, dim, width):
    size = lax.axis_size(axis)
    length = value.shape[dim]
    up = [(i, i + 1) for i in range(size - 1)]
    down = [(j, i) for i, j in up]
    last = lax.slice_in_dim(value, length - width, length, axis=dim)
    initial = lax.slice_in_dim(value, 0, width, axis=dim)
    before = lax.ppermute(last, axis, up)
    after = lax.ppermute(initial, axis, down)
    return jnp.concatenate([before, value, after], axis=dim)


def attend_block(state, query_heads, keys, values, heads):
    top, total, summed = state
    length = keys.shape[0]
    key_heads = keys.reshape(length, heads, HD)
    value_heads = values.reshape(length, heads, HD)
    scores = jnp.einsum(
        "qhd,khd->hqk", query_heads, key_heads, preferred_element_type=jnp.float32
    )
    scores = scores * HD ** (-0.5)
    block_top = jnp.max(scores, axis=2)
    new_top = block_top if top is None else jnp.maximum(top, block_top)
    weights = jnp.exp(scores - new_top[..., None])
    block_total = jnp.sum(weights, axis=2)
    product = jnp.einsum(
        "hqk,khd->hqd",
        weights.astype(jnp.bfloat16),
        value_heads,
        preferred_element_type=jnp.float32,
    )
    if top is None:
        return (new_top, block_total, product)
    factor = jnp.exp(top - new_top)
    return (new_top, total * factor + block_total, summed * factor[..., None] + product)


def attention_kernel(heads, parts, *refs):
    wq_ref, wk_ref, wv_ref, wo_ref, bias_ref = refs[:5]
    sources = refs[5 : 5 + parts]
    o_ref, k_ref, v_ref, mixed_ref, q_ref = refs[5 + parts :]
    q_ref[...] = jnp.dot(
        sources[0][...], wq_ref[...], preferred_element_type=jnp.float32
    ).astype(q_ref.dtype)
    offset = 0
    for source in sources:
        rows = source.shape[0]
        k_ref[:, offset : offset + rows] = lax.dot_general(
            wk_ref[...], source[...], (((0,), (1,)), ((), ())), preferred_element_type=jnp.float32
        ).astype(k_ref.dtype)
        v_ref[offset : offset + rows, :] = jnp.dot(
            source[...], wv_ref[...], preferred_element_type=jnp.float32
        ).astype(v_ref.dtype)
        offset += rows
    for head in range(heads):
        lanes = slice(head * HD, (head + 1) * HD)
        scores = jnp.dot(q_ref[:, lanes], k_ref[lanes, :], preferred_element_type=jnp.float32)
        scores = scores * HD ** (-0.5)
        top = jnp.max(scores, axis=1, keepdims=True)
        weights = jnp.exp(scores - top)
        total = jnp.sum(weights, axis=1, keepdims=True)
        summed = jnp.dot(
            weights.astype(jnp.bfloat16), v_ref[:, lanes], preferred_element_type=jnp.float32
        )
        mixed_ref[:, lanes] = (summed / total).astype(mixed_ref.dtype)
    attended = jnp.dot(mixed_ref[...], wo_ref[...], preferred_element_type=jnp.float32)
    o_ref[...] = (attended + bias_ref[...]).astype(o_ref.dtype)


def attention(w_query, w_key, w_value, w_out, out_bias, sources, heads):
    tokens, channels = sources[0].shape
    length = sum(source.shape[0] for source in sources)
    whole = lambda array: pl.BlockSpec(array.shape, lambda i: (0, 0))
    operands = (w_query, w_key, w_value, w_out, out_bias.reshape(1, -1)) + tuple(sources)
    return pl.pallas_call(
        functools.partial(attention_kernel, heads, len(sources)),
        out_shape=jax.ShapeDtypeStruct((tokens, channels), jnp.bfloat16),
        grid=(1,),
        in_specs=[whole(array) for array in operands],
        out_specs=pl.BlockSpec((tokens, channels), lambda i: (0, 0)),
        scratch_shapes=[
            pltpu.VMEM((channels, length), jnp.bfloat16),
            pltpu.VMEM((length, channels), jnp.bfloat16),
            pltpu.VMEM((tokens, channels), jnp.bfloat16),
            pltpu.VMEM((tokens, channels), jnp.bfloat16),
        ],
    )(*operands)


def doubling_gather(value, axis):
    size = lax.axis_size(axis)
    step = 1
    while step < size:
        pairs = [(j, j ^ step) for j in range(size)]
        value = jnp.concatenate([value, lax.ppermute(value, axis, pairs)], axis=0)
        step *= 2
    return value


def shards(frames, conv_weight, conv_bias, ref_features, w_query, w_key, w_value, w_out, out_bias):
    count, band_rows, width, channels = frames.shape
    heads = channels // HD
    band = band_rows * width
    activated = jax.nn.silu(frames.astype(jnp.float32)).astype(jnp.bfloat16)
    padded = extended(activated, ROW_PARTS, 1, 1)
    padded = jnp.pad(padded, ((0, 0), (0, 0), (1, 1), (0, 0)))
    convolved = jnp.zeros((count * band, channels), jnp.float32)
    for row_tap in range(3):
        for col_tap in range(3):
            window = padded[:, row_tap : row_tap + band_rows, col_tap : col_tap + width].reshape(
                count * band, channels
            )
            convolved = convolved + jnp.dot(
                window, conv_weight[row_tap, col_tap], preferred_element_type=jnp.float32
            )
    hidden = (
        frames.reshape(count * band, channels).astype(jnp.float32) + convolved + conv_bias
    ).astype(jnp.bfloat16)
    rows = lax.axis_size(ROW_PARTS)
    others = [
        lax.ppermute(hidden, ROW_PARTS, [(j, (j + shift) % rows) for j in range(rows)])
        for shift in range(1, rows)
    ]
    every_feature = staged_gather(ref_features, hidden)
    sources = [hidden] + others + [every_feature]
    attended = attention(w_query, w_key, w_value, w_out, out_bias, sources, heads)
    return (
        hidden.reshape(count, band_rows, width, channels),
        attended.reshape(count, band_rows, width, channels),
    )


def solution(mesh):
    fine = fine_mesh(mesh)
    blocks = P(TM_PARTS, ROW_PARTS, None, None)
    return jax.shard_map(
        shards,
        mesh=fine,
        in_specs=(blocks, P(), P(), P(TM_PARTS, None), P(), P(), P(), P(), P()),
        out_specs=(blocks, blocks),
        check_vma=False,
    )
```

```python
import functools

import jax
import jax.numpy as jnp
import numpy as np
from jax import lax
from jax.experimental import pallas as pl
from jax.experimental.pallas import tpu as pltpu
from jax.sharding import Mesh
from jax.sharding import PartitionSpec as P

HD = 80


MESH = pl.DeviceIdType.MESH
TM_PARTS = ("y_hi", "x", "z")
ROW_PARTS = ("y_lo", "core")


def distinct(values):
    return len(set(values))


def fine_mesh(mesh):
    devices = np.asarray(mesh.devices)
    tm, rows = devices.shape
    try:
        column = devices[:, 0]
        nx = distinct(d.coords[0] for d in column)
        nz = distinct(d.coords[2] for d in column)
        cores = distinct(d.core_on_chip for d in devices[0])
    except (AttributeError, IndexError, TypeError):
        nx, nz, cores = tm, 1, rows
    if tm % (nx * nz) or rows % cores:
        nx, nz, cores = tm, 1, rows
    shape = (tm // (nx * nz), nx, nz, rows // cores, cores)
    return Mesh(devices.reshape(shape), TM_PARTS + ROW_PARTS)


def staged_kernel(sizes, x_ref, after_ref, out_ref, local_sem, *sems):
    high, across, along = sizes
    half = along // 2
    yh, xx, zz = [lax.axis_index(axis) for axis in TM_PARTS]
    low, core = [lax.axis_index(axis) for axis in ROW_PARTS]
    z_peer = lambda shift: {"z": lax.rem(zz + shift, along)}
    x_peer = lambda shift: {"x": lax.rem(xx + shift, across)}
    y_peer = {"y_hi": 1 - yh, "y_lo": 1 - low}
    c_peer = {"core": 1 - core}
    peers = [z_peer(s) for s in range(1, along)] + [x_peer(s) for s in range(1, across)]
    peers += [y_peer, c_peer]
    barrier = pltpu.get_barrier_semaphore()
    for peer in peers:
        pl.semaphore_signal(barrier, inc=1, device_id=peer, device_id_type=MESH)
    pl.semaphore_wait(barrier, len(peers))

    def block_of(z):
        return ((z // half * high + yh) * across + xx) * half + lax.rem(z, half)

    own = out_ref.at[pl.ds(block_of(zz), 1)]
    mine = zz // half == core

    @pl.when(mine)
    def _():
        local = pltpu.make_async_copy(x_ref, own, local_sem)
        local.start()
        local.wait()

    def remote(ref, peer, send_sem, recv_sem):
        return pltpu.make_async_remote_copy(
            src_ref=ref,
            dst_ref=ref,
            send_sem=send_sem,
            recv_sem=recv_sem,
            device_id=peer,
            device_id_type=MESH,
        )

    z_copies = [remote(own, z_peer(s), sems[0].at[s], sems[1].at[s]) for s in range(1, along)]

    @pl.when(mine)
    def _():
        for copy in z_copies:
            copy.start()
        for copy in z_copies:
            copy.wait_send()

    for s, copy in zip(range(1, along), z_copies):
        sender = lax.rem(zz + along - s, along)

        @pl.when(sender // half == core)
        def _():
            copy.wait_recv()

    def exchange(pairs, send_sem, recv_sem):
        copies = [remote(ref, peer, send_sem.at[i], recv_sem.at[i]) for i, (ref, peer) in enumerate(pairs)]
        for copy in copies:
            copy.start()
        for copy in copies:
            copy.wait()

    group = out_ref.at[pl.ds(((core * high + yh) * across + xx) * half, half)]
    exchange([(group, x_peer(s)) for s in range(1, across)], sems[2], sems[3])
    row = out_ref.at[pl.ds((core * high + yh) * across * half, across * half)]
    exchange([(row, y_peer)], sems[4], sems[5])
    whole = out_ref.at[pl.ds(core * high * across * half, high * across * half)]
    exchange([(whole, c_peer)], sems[6], sems[7])


def staged_gather(value, after):
    sizes = [lax.axis_size(axis) for axis in TM_PARTS]
    total = sizes[0] * sizes[1] * sizes[2]
    sems = []
    for count in (sizes[2], sizes[1], 1, 1):
        sems += [pltpu.SemaphoreType.DMA((count,))] * 2
    gathered = pl.pallas_call(
        functools.partial(staged_kernel, sizes),
        out_shape=jax.ShapeDtypeStruct((total,) + value.shape, value.dtype),
        in_specs=[pl.BlockSpec(memory_space=pl.ANY)] * 2,
        out_specs=pl.BlockSpec(memory_space=pl.ANY),
        scratch_shapes=[pltpu.SemaphoreType.DMA] + sems,
        compiler_params=pltpu.CompilerParams(collective_id=0, has_side_effects=True),
    )(value[None], after)
    return gathered.reshape((total * value.shape[0],) + value.shape[1:])


def extended(value, axis, dim, width):
    size = lax.axis_size(axis)
    length = value.shape[dim]
    up = [(i, i + 1) for i in range(size - 1)]
    down = [(j, i) for i, j in up]
    last = lax.slice_in_dim(value, length - width, length, axis=dim)
    initial = lax.slice_in_dim(value, 0, width, axis=dim)
    before = lax.ppermute(last, axis, up)
    after = lax.ppermute(initial, axis, down)
    return jnp.concatenate([before, value, after], axis=dim)


def attend_block(state, query_heads, keys, values, heads):
    top, total, summed = state
    length = keys.shape[0]
    key_heads = keys.reshape(length, heads, HD)
    value_heads = values.reshape(length, heads, HD)
    scores = jnp.einsum(
        "qhd,khd->hqk", query_heads, key_heads, preferred_element_type=jnp.float32
    )
    scores = scores * HD ** (-0.5)
    block_top = jnp.max(scores, axis=2)
    new_top = block_top if top is None else jnp.maximum(top, block_top)
    weights = jnp.exp(scores - new_top[..., None])
    block_total = jnp.sum(weights, axis=2)
    product = jnp.einsum(
        "hqk,khd->hqd",
        weights.astype(jnp.bfloat16),
        value_heads,
        preferred_element_type=jnp.float32,
    )
    if top is None:
        return (new_top, block_total, product)
    factor = jnp.exp(top - new_top)
    return (new_top, total * factor + block_total, summed * factor[..., None] + product)


def attention_kernel(heads, parts, *refs):
    wq_ref, wk_ref, wv_ref, wo_ref, bias_ref = refs[:5]
    sources = refs[5 : 5 + parts]
    o_ref, k_ref, v_ref, mixed_ref, q_ref = refs[5 + parts :]
    q_ref[...] = jnp.dot(
        sources[0][...], wq_ref[...], preferred_element_type=jnp.float32
    ).astype(q_ref.dtype)
    offset = 0
    for source in sources:
        rows = source.shape[0]
        k_ref[:, offset : offset + rows] = lax.dot_general(
            wk_ref[...], source[...], (((0,), (1,)), ((), ())), preferred_element_type=jnp.float32
        ).astype(k_ref.dtype)
        v_ref[offset : offset + rows, :] = jnp.dot(
            source[...], wv_ref[...], preferred_element_type=jnp.float32
        ).astype(v_ref.dtype)
        offset += rows
    tokens = q_ref.shape[0]
    tile = tokens // 2 if tokens % 16 == 0 else tokens
    for head in range(heads):
        lanes = slice(head * HD, (head + 1) * HD)
        for first in range(0, tokens, tile):
            rows = slice(first, first + tile)
            scores = jnp.dot(
                q_ref[rows, lanes], k_ref[lanes, :], preferred_element_type=jnp.float32
            )
            scores = scores * HD ** (-0.5)
            top = jnp.max(scores, axis=1, keepdims=True)
            weights = jnp.exp(scores - top)
            total = jnp.sum(weights, axis=1, keepdims=True)
            summed = jnp.dot(
                weights.astype(jnp.bfloat16), v_ref[:, lanes], preferred_element_type=jnp.float32
            )
            mixed_ref[rows, lanes] = (summed / total).astype(mixed_ref.dtype)
    attended = jnp.dot(mixed_ref[...], wo_ref[...], preferred_element_type=jnp.float32)
    o_ref[...] = (attended + bias_ref[...]).astype(o_ref.dtype)


def attention(w_query, w_key, w_value, w_out, out_bias, sources, heads):
    tokens, channels = sources[0].shape
    length = sum(source.shape[0] for source in sources)
    whole = lambda array: pl.BlockSpec(array.shape, lambda i: (0, 0))
    operands = (w_query, w_key, w_value, w_out, out_bias.reshape(1, -1)) + tuple(sources)
    return pl.pallas_call(
        functools.partial(attention_kernel, heads, len(sources)),
        out_shape=jax.ShapeDtypeStruct((tokens, channels), jnp.bfloat16),
        grid=(1,),
        in_specs=[whole(array) for array in operands],
        out_specs=pl.BlockSpec((tokens, channels), lambda i: (0, 0)),
        scratch_shapes=[
            pltpu.VMEM((channels, length), jnp.bfloat16),
            pltpu.VMEM((length, channels), jnp.bfloat16),
            pltpu.VMEM((tokens, channels), jnp.bfloat16),
            pltpu.VMEM((tokens, channels), jnp.bfloat16),
        ],
    )(*operands)


def doubling_gather(value, axis):
    size = lax.axis_size(axis)
    step = 1
    while step < size:
        pairs = [(j, j ^ step) for j in range(size)]
        value = jnp.concatenate([value, lax.ppermute(value, axis, pairs)], axis=0)
        step *= 2
    return value


def shards(frames, conv_weight, conv_bias, ref_features, w_query, w_key, w_value, w_out, out_bias):
    count, band_rows, width, channels = frames.shape
    heads = channels // HD
    band = band_rows * width
    activated = jax.nn.silu(frames.astype(jnp.float32)).astype(jnp.bfloat16)
    padded = extended(activated, ROW_PARTS, 1, 1)
    padded = jnp.pad(padded, ((0, 0), (0, 0), (1, 1), (0, 0)))
    convolved = jnp.zeros((count * band, channels), jnp.float32)
    for row_tap in range(3):
        for col_tap in range(3):
            window = padded[:, row_tap : row_tap + band_rows, col_tap : col_tap + width].reshape(
                count * band, channels
            )
            convolved = convolved + jnp.dot(
                window, conv_weight[row_tap, col_tap], preferred_element_type=jnp.float32
            )
    hidden = (
        frames.reshape(count * band, channels).astype(jnp.float32) + convolved + conv_bias
    ).astype(jnp.bfloat16)
    rows = lax.axis_size(ROW_PARTS)
    others = [
        lax.ppermute(hidden, ROW_PARTS, [(j, (j + shift) % rows) for j in range(rows)])
        for shift in range(1, rows)
    ]
    every_feature = staged_gather(ref_features, hidden)
    sources = [hidden] + others + [every_feature]
    attended = attention(w_query, w_key, w_value, w_out, out_bias, sources, heads)
    return (
        hidden.reshape(count, band_rows, width, channels),
        attended.reshape(count, band_rows, width, channels),
    )


def solution(mesh):
    fine = fine_mesh(mesh)
    blocks = P(TM_PARTS, ROW_PARTS, None, None)
    return jax.shard_map(
        shards,
        mesh=fine,
        in_specs=(blocks, P(), P(), P(TM_PARTS, None), P(), P(), P(), P(), P()),
        out_specs=(blocks, blocks),
        check_vma=False,
    )
```

```python
import functools

import jax
import jax.numpy as jnp
import numpy as np
from jax import lax
from jax.experimental import pallas as pl
from jax.experimental.pallas import tpu as pltpu
from jax.sharding import Mesh
from jax.sharding import PartitionSpec as P

HD = 80


MESH = pl.DeviceIdType.MESH
TM_PARTS = ("y_hi", "x", "z")
ROW_PARTS = ("y_lo", "core")


def distinct(values):
    return len(set(values))


def fine_mesh(mesh):
    devices = np.asarray(mesh.devices)
    tm, rows = devices.shape
    try:
        column = devices[:, 0]
        nx = distinct(d.coords[0] for d in column)
        nz = distinct(d.coords[2] for d in column)
        cores = distinct(d.core_on_chip for d in devices[0])
    except (AttributeError, IndexError, TypeError):
        nx, nz, cores = tm, 1, rows
    if tm % (nx * nz) or rows % cores:
        nx, nz, cores = tm, 1, rows
    shape = (tm // (nx * nz), nx, nz, rows // cores, cores)
    return Mesh(devices.reshape(shape), TM_PARTS + ROW_PARTS)


def staged_kernel(sizes, x_ref, after_ref, out_ref, local_sem, *sems):
    high, across, along = sizes
    half = along // 2
    yh, xx, zz = [lax.axis_index(axis) for axis in TM_PARTS]
    low, core = [lax.axis_index(axis) for axis in ROW_PARTS]
    z_peer = lambda shift: {"z": lax.rem(zz + shift, along)}
    x_peer = lambda shift: {"x": lax.rem(xx + shift, across)}
    y_peer = {"y_hi": 1 - yh, "y_lo": 1 - low}
    c_peer = {"core": 1 - core}
    peers = [z_peer(s) for s in range(1, along)] + [x_peer(s) for s in range(1, across)]
    peers += [y_peer, c_peer]
    barrier = pltpu.get_barrier_semaphore()
    for peer in peers:
        pl.semaphore_signal(barrier, inc=1, device_id=peer, device_id_type=MESH)
    pl.semaphore_wait(barrier, len(peers))

    def block_of(z):
        return ((z // half * high + yh) * across + xx) * half + lax.rem(z, half)

    own = out_ref.at[pl.ds(block_of(zz), 1)]
    mine = zz // half == core

    @pl.when(mine)
    def _():
        local = pltpu.make_async_copy(x_ref, own, local_sem)
        local.start()
        local.wait()

    def remote(ref, peer, send_sem, recv_sem):
        return pltpu.make_async_remote_copy(
            src_ref=ref,
            dst_ref=ref,
            send_sem=send_sem,
            recv_sem=recv_sem,
            device_id=peer,
            device_id_type=MESH,
        )

    z_copies = [remote(own, z_peer(s), sems[0].at[s], sems[1].at[s]) for s in range(1, along)]

    @pl.when(mine)
    def _():
        for copy in z_copies:
            copy.start()
        for copy in z_copies:
            copy.wait_send()

    for s, copy in zip(range(1, along), z_copies):
        sender = lax.rem(zz + along - s, along)

        @pl.when(sender // half == core)
        def _():
            copy.wait_recv()

    def exchange(pairs, send_sem, recv_sem):
        copies = [remote(ref, peer, send_sem.at[i], recv_sem.at[i]) for i, (ref, peer) in enumerate(pairs)]
        for copy in copies:
            copy.start()
        for copy in copies:
            copy.wait()

    group = out_ref.at[pl.ds(((core * high + yh) * across + xx) * half, half)]
    exchange([(group, x_peer(s)) for s in range(1, across)], sems[2], sems[3])
    row = out_ref.at[pl.ds((core * high + yh) * across * half, across * half)]
    exchange([(row, y_peer)], sems[4], sems[5])
    whole = out_ref.at[pl.ds(core * high * across * half, high * across * half)]
    exchange([(whole, c_peer)], sems[6], sems[7])


def staged_gather(value, after):
    sizes = [lax.axis_size(axis) for axis in TM_PARTS]
    total = sizes[0] * sizes[1] * sizes[2]
    sems = []
    for count in (sizes[2], sizes[1], 1, 1):
        sems += [pltpu.SemaphoreType.DMA((count,))] * 2
    gathered = pl.pallas_call(
        functools.partial(staged_kernel, sizes),
        out_shape=jax.ShapeDtypeStruct((total,) + value.shape, value.dtype),
        in_specs=[pl.BlockSpec(memory_space=pl.ANY)] * 2,
        out_specs=pl.BlockSpec(memory_space=pl.ANY),
        scratch_shapes=[pltpu.SemaphoreType.DMA] + sems,
        compiler_params=pltpu.CompilerParams(collective_id=0, has_side_effects=True),
    )(value[None], after)
    return gathered.reshape((total * value.shape[0],) + value.shape[1:])


def extended(value, axis, dim, width):
    size = lax.axis_size(axis)
    length = value.shape[dim]
    up = [(i, i + 1) for i in range(size - 1)]
    down = [(j, i) for i, j in up]
    last = lax.slice_in_dim(value, length - width, length, axis=dim)
    initial = lax.slice_in_dim(value, 0, width, axis=dim)
    before = lax.ppermute(last, axis, up)
    after = lax.ppermute(initial, axis, down)
    return jnp.concatenate([before, value, after], axis=dim)


def attend_block(state, query_heads, keys, values, heads):
    top, total, summed = state
    length = keys.shape[0]
    key_heads = keys.reshape(length, heads, HD)
    value_heads = values.reshape(length, heads, HD)
    scores = jnp.einsum(
        "qhd,khd->hqk", query_heads, key_heads, preferred_element_type=jnp.float32
    )
    scores = scores * HD ** (-0.5)
    block_top = jnp.max(scores, axis=2)
    new_top = block_top if top is None else jnp.maximum(top, block_top)
    weights = jnp.exp(scores - new_top[..., None])
    block_total = jnp.sum(weights, axis=2)
    product = jnp.einsum(
        "hqk,khd->hqd",
        weights.astype(jnp.bfloat16),
        value_heads,
        preferred_element_type=jnp.float32,
    )
    if top is None:
        return (new_top, block_total, product)
    factor = jnp.exp(top - new_top)
    return (new_top, total * factor + block_total, summed * factor[..., None] + product)


def attention_kernel(heads, parts, *refs):
    wq_ref, wk_ref, wv_ref, wo_ref, bias_ref = refs[:5]
    sources = refs[5 : 5 + parts]
    o_ref, k_ref, v_ref, mixed_ref, q_ref = refs[5 + parts :]
    q_ref[...] = jnp.dot(
        sources[0][...], wq_ref[...], preferred_element_type=jnp.float32
    ).astype(q_ref.dtype)
    offset = 0
    for source in sources:
        rows = source.shape[0]
        k_ref[:, offset : offset + rows] = lax.dot_general(
            wk_ref[...], source[...], (((0,), (1,)), ((), ())), preferred_element_type=jnp.float32
        ).astype(k_ref.dtype)
        v_ref[offset : offset + rows, :] = jnp.dot(
            source[...], wv_ref[...], preferred_element_type=jnp.float32
        ).astype(v_ref.dtype)
        offset += rows
    for head in range(heads):
        lanes = slice(head * HD, (head + 1) * HD)
        scores = jnp.dot(q_ref[:, lanes], k_ref[lanes, :], preferred_element_type=jnp.float32)
        scores = scores * HD ** (-0.5)
        top = jnp.max(scores, axis=1, keepdims=True)
        weights = jnp.exp(scores - top)
        total = jnp.sum(weights, axis=1, keepdims=True)
        summed = jnp.dot(
            weights.astype(jnp.bfloat16), v_ref[:, lanes], preferred_element_type=jnp.float32
        )
        mixed_ref[:, lanes] = (summed / total).astype(mixed_ref.dtype)
    attended = jnp.dot(mixed_ref[...], wo_ref[...], preferred_element_type=jnp.float32)
    o_ref[...] = (attended + bias_ref[...]).astype(o_ref.dtype)


def attention(w_query, w_key, w_value, w_out, out_bias, sources, heads):
    tokens, channels = sources[0].shape
    length = sum(source.shape[0] for source in sources)
    whole = lambda array: pl.BlockSpec(array.shape, lambda i: (0, 0))
    operands = (w_query, w_key, w_value, w_out, out_bias.reshape(1, -1)) + tuple(sources)
    return pl.pallas_call(
        functools.partial(attention_kernel, heads, len(sources)),
        out_shape=jax.ShapeDtypeStruct((tokens, channels), jnp.bfloat16),
        grid=(1,),
        in_specs=[whole(array) for array in operands],
        out_specs=pl.BlockSpec((tokens, channels), lambda i: (0, 0)),
        scratch_shapes=[
            pltpu.VMEM((channels, length), jnp.bfloat16),
            pltpu.VMEM((length, channels), jnp.bfloat16),
            pltpu.VMEM((tokens, channels), jnp.bfloat16),
            pltpu.VMEM((tokens, channels), jnp.bfloat16),
        ],
    )(*operands)


def doubling_gather(value, axis):
    size = lax.axis_size(axis)
    step = 1
    while step < size:
        pairs = [(j, j ^ step) for j in range(size)]
        value = jnp.concatenate([value, lax.ppermute(value, axis, pairs)], axis=0)
        step *= 2
    return value


def shards(frames, conv_weight, conv_bias, ref_features, w_query, w_key, w_value, w_out, out_bias):
    count, band_rows, width, channels = frames.shape
    heads = channels // HD
    band = band_rows * width
    padded = extended(frames, ROW_PARTS, 1, 1)
    padded = jax.nn.silu(padded.astype(jnp.float32)).astype(jnp.bfloat16)
    padded = jnp.pad(padded, ((0, 0), (0, 0), (1, 1), (0, 0)))
    convolved = jnp.zeros((count * band, channels), jnp.float32)
    for row_tap in range(3):
        for col_tap in range(3):
            window = padded[:, row_tap : row_tap + band_rows, col_tap : col_tap + width].reshape(
                count * band, channels
            )
            convolved = convolved + jnp.dot(
                window, conv_weight[row_tap, col_tap], preferred_element_type=jnp.float32
            )
    hidden = (
        frames.reshape(count * band, channels).astype(jnp.float32) + convolved + conv_bias
    ).astype(jnp.bfloat16)
    rows = lax.axis_size(ROW_PARTS)
    others = [
        lax.ppermute(hidden, ROW_PARTS, [(j, (j + shift) % rows) for j in range(rows)])
        for shift in range(1, rows)
    ]
    every_feature = staged_gather(ref_features, hidden)
    sources = [hidden] + others + [every_feature]
    attended = attention(w_query, w_key, w_value, w_out, out_bias, sources, heads)
    return (
        hidden.reshape(count, band_rows, width, channels),
        attended.reshape(count, band_rows, width, channels),
    )


def solution(mesh):
    fine = fine_mesh(mesh)
    blocks = P(TM_PARTS, ROW_PARTS, None, None)
    return jax.shard_map(
        shards,
        mesh=fine,
        in_specs=(blocks, P(), P(), P(TM_PARTS, None), P(), P(), P(), P(), P()),
        out_specs=(blocks, blocks),
        check_vma=False,
    )
```

```python
import functools

import jax
import jax.numpy as jnp
import numpy as np
from jax import lax
from jax.experimental import pallas as pl
from jax.experimental.pallas import tpu as pltpu
from jax.sharding import Mesh
from jax.sharding import PartitionSpec as P

HD = 80


MESH = pl.DeviceIdType.MESH
TM_PARTS = ("y_hi", "x", "z")
ROW_PARTS = ("y_lo", "core")


def distinct(values):
    return len(set(values))


def fine_mesh(mesh):
    devices = np.asarray(mesh.devices)
    tm, rows = devices.shape
    try:
        column = devices[:, 0]
        nx = distinct(d.coords[0] for d in column)
        nz = distinct(d.coords[2] for d in column)
        cores = distinct(d.core_on_chip for d in devices[0])
    except (AttributeError, IndexError, TypeError):
        nx, nz, cores = tm, 1, rows
    if tm % (nx * nz) or rows % cores:
        nx, nz, cores = tm, 1, rows
    shape = (tm // (nx * nz), nx, nz, rows // cores, cores)
    return Mesh(devices.reshape(shape), TM_PARTS + ROW_PARTS)


def staged_kernel(sizes, x_ref, h_ref, wq_ref, wk_ref, wv_ref, out_ref, q_ref, k_ref, v_ref, local_sem, *sems):
    high, across, along = sizes
    half = along // 2
    yh, xx, zz = [lax.axis_index(axis) for axis in TM_PARTS]
    low, core = [lax.axis_index(axis) for axis in ROW_PARTS]
    z_peer = lambda shift: {"z": lax.rem(zz + shift, along)}
    x_peer = lambda shift: {"x": lax.rem(xx + shift, across)}
    y_peer = {"y_hi": 1 - yh, "y_lo": 1 - low}
    c_peer = {"core": 1 - core}
    peers = [z_peer(s) for s in range(1, along)] + [x_peer(s) for s in range(1, across)]
    peers += [y_peer, c_peer]
    barrier = pltpu.get_barrier_semaphore()
    for peer in peers:
        pl.semaphore_signal(barrier, inc=1, device_id=peer, device_id_type=MESH)
    pl.semaphore_wait(barrier, len(peers))

    def block_of(z):
        return ((z // half * high + yh) * across + xx) * half + lax.rem(z, half)

    own = out_ref.at[pl.ds(block_of(zz), 1)]
    mine = zz // half == core

    @pl.when(mine)
    def _():
        local = pltpu.make_async_copy(x_ref, own, local_sem)
        local.start()
        local.wait()

    def remote(ref, peer, send_sem, recv_sem):
        return pltpu.make_async_remote_copy(
            src_ref=ref,
            dst_ref=ref,
            send_sem=send_sem,
            recv_sem=recv_sem,
            device_id=peer,
            device_id_type=MESH,
        )

    z_copies = [remote(own, z_peer(s), sems[0].at[s], sems[1].at[s]) for s in range(1, along)]

    @pl.when(mine)
    def _():
        for copy in z_copies:
            copy.start()

    band = h_ref[...]
    q_ref[...] = jnp.dot(band, wq_ref[...], preferred_element_type=jnp.float32).astype(q_ref.dtype)
    k_ref[...] = lax.dot_general(
        wk_ref[...], band, (((0,), (1,)), ((), ())), preferred_element_type=jnp.float32
    ).astype(k_ref.dtype)
    v_ref[...] = jnp.dot(band, wv_ref[...], preferred_element_type=jnp.float32).astype(v_ref.dtype)

    @pl.when(mine)
    def _():
        for copy in z_copies:
            copy.wait_send()

    for s, copy in zip(range(1, along), z_copies):
        sender = lax.rem(zz + along - s, along)

        @pl.when(sender // half == core)
        def _():
            copy.wait_recv()

    def exchange(pairs, send_sem, recv_sem):
        copies = [remote(ref, peer, send_sem.at[i], recv_sem.at[i]) for i, (ref, peer) in enumerate(pairs)]
        for copy in copies:
            copy.start()
        for copy in copies:
            copy.wait()

    group = out_ref.at[pl.ds(((core * high + yh) * across + xx) * half, half)]
    exchange([(group, x_peer(s)) for s in range(1, across)], sems[2], sems[3])
    row = out_ref.at[pl.ds((core * high + yh) * across * half, across * half)]
    exchange([(row, y_peer)], sems[4], sems[5])
    whole = out_ref.at[pl.ds(core * high * across * half, high * across * half)]
    exchange([(whole, c_peer)], sems[6], sems[7])


def staged_gather(value, band, w_query, w_key, w_value):
    sizes = [lax.axis_size(axis) for axis in TM_PARTS]
    total = sizes[0] * sizes[1] * sizes[2]
    tokens, channels = band.shape
    sems = []
    for count in (sizes[2], sizes[1], 1, 1):
        sems += [pltpu.SemaphoreType.DMA((count,))] * 2
    vmem = pl.BlockSpec(memory_space=pltpu.VMEM)
    gathered, query, key, value_part = pl.pallas_call(
        functools.partial(staged_kernel, sizes),
        out_shape=(
            jax.ShapeDtypeStruct((total,) + value.shape, value.dtype),
            jax.ShapeDtypeStruct((tokens, w_query.shape[1]), jnp.bfloat16),
            jax.ShapeDtypeStruct((w_key.shape[1], tokens), jnp.bfloat16),
            jax.ShapeDtypeStruct((tokens, w_value.shape[1]), jnp.bfloat16),
        ),
        in_specs=[pl.BlockSpec(memory_space=pl.ANY)] + [vmem] * 4,
        out_specs=(pl.BlockSpec(memory_space=pl.ANY), vmem, vmem, vmem),
        scratch_shapes=[pltpu.SemaphoreType.DMA] + sems,
        compiler_params=pltpu.CompilerParams(collective_id=0, has_side_effects=True),
    )(value[None], band, w_query, w_key, w_value)
    every = gathered.reshape((total * value.shape[0],) + value.shape[1:])
    return every, query, key, value_part


def extended(value, axis, dim, width):
    size = lax.axis_size(axis)
    length = value.shape[dim]
    up = [(i, i + 1) for i in range(size - 1)]
    down = [(j, i) for i, j in up]
    last = lax.slice_in_dim(value, length - width, length, axis=dim)
    initial = lax.slice_in_dim(value, 0, width, axis=dim)
    before = lax.ppermute(last, axis, up)
    after = lax.ppermute(initial, axis, down)
    return jnp.concatenate([before, value, after], axis=dim)


def attend_block(state, query_heads, keys, values, heads):
    top, total, summed = state
    length = keys.shape[0]
    key_heads = keys.reshape(length, heads, HD)
    value_heads = values.reshape(length, heads, HD)
    scores = jnp.einsum(
        "qhd,khd->hqk", query_heads, key_heads, preferred_element_type=jnp.float32
    )
    scores = scores * HD ** (-0.5)
    block_top = jnp.max(scores, axis=2)
    new_top = block_top if top is None else jnp.maximum(top, block_top)
    weights = jnp.exp(scores - new_top[..., None])
    block_total = jnp.sum(weights, axis=2)
    product = jnp.einsum(
        "hqk,khd->hqd",
        weights.astype(jnp.bfloat16),
        value_heads,
        preferred_element_type=jnp.float32,
    )
    if top is None:
        return (new_top, block_total, product)
    factor = jnp.exp(top - new_top)
    return (new_top, total * factor + block_total, summed * factor[..., None] + product)


def attention_kernel(heads, parts, *refs):
    q_ref, ko_ref, vo_ref, wk_ref, wv_ref, wo_ref, bias_ref = refs[:7]
    sources = refs[7 : 7 + parts]
    o_ref, k_ref, v_ref, mixed_ref = refs[7 + parts :]
    offset = vo_ref.shape[0]
    k_ref[:, :offset] = ko_ref[...]
    v_ref[:offset, :] = vo_ref[...]
    for source in sources:
        rows = source.shape[0]
        k_ref[:, offset : offset + rows] = lax.dot_general(
            wk_ref[...], source[...], (((0,), (1,)), ((), ())), preferred_element_type=jnp.float32
        ).astype(k_ref.dtype)
        v_ref[offset : offset + rows, :] = jnp.dot(
            source[...], wv_ref[...], preferred_element_type=jnp.float32
        ).astype(v_ref.dtype)
        offset += rows
    for head in range(heads):
        lanes = slice(head * HD, (head + 1) * HD)
        scores = jnp.dot(q_ref[:, lanes], k_ref[lanes, :], preferred_element_type=jnp.float32)
        scores = scores * HD ** (-0.5)
        top = jnp.max(scores, axis=1, keepdims=True)
        weights = jnp.exp(scores - top)
        total = jnp.sum(weights, axis=1, keepdims=True)
        summed = jnp.dot(
            weights.astype(jnp.bfloat16), v_ref[:, lanes], preferred_element_type=jnp.float32
        )
        mixed_ref[:, lanes] = (summed / total).astype(mixed_ref.dtype)
    attended = jnp.dot(mixed_ref[...], wo_ref[...], preferred_element_type=jnp.float32)
    o_ref[...] = (attended + bias_ref[...]).astype(o_ref.dtype)


def attention(query, own_key, own_value, w_key, w_value, w_out, out_bias, sources, heads):
    tokens, channels = query.shape
    length = own_value.shape[0] + sum(source.shape[0] for source in sources)
    whole = lambda array: pl.BlockSpec(array.shape, lambda i: (0, 0))
    operands = (query, own_key, own_value, w_key, w_value, w_out, out_bias.reshape(1, -1))
    operands += tuple(sources)
    return pl.pallas_call(
        functools.partial(attention_kernel, heads, len(sources)),
        out_shape=jax.ShapeDtypeStruct((tokens, channels), jnp.bfloat16),
        grid=(1,),
        in_specs=[whole(array) for array in operands],
        out_specs=pl.BlockSpec((tokens, channels), lambda i: (0, 0)),
        scratch_shapes=[
            pltpu.VMEM((channels, length), jnp.bfloat16),
            pltpu.VMEM((length, channels), jnp.bfloat16),
            pltpu.VMEM((tokens, channels), jnp.bfloat16),
        ],
    )(*operands)


def doubling_gather(value, axis):
    size = lax.axis_size(axis)
    step = 1
    while step < size:
        pairs = [(j, j ^ step) for j in range(size)]
        value = jnp.concatenate([value, lax.ppermute(value, axis, pairs)], axis=0)
        step *= 2
    return value


def shards(frames, conv_weight, conv_bias, ref_features, w_query, w_key, w_value, w_out, out_bias):
    count, band_rows, width, channels = frames.shape
    heads = channels // HD
    band = band_rows * width
    activated = jax.nn.silu(frames.astype(jnp.float32)).astype(jnp.bfloat16)
    padded = extended(activated, ROW_PARTS, 1, 1)
    padded = jnp.pad(padded, ((0, 0), (0, 0), (1, 1), (0, 0)))
    convolved = jnp.zeros((count * band, channels), jnp.float32)
    for row_tap in range(3):
        for col_tap in range(3):
            window = padded[:, row_tap : row_tap + band_rows, col_tap : col_tap + width].reshape(
                count * band, channels
            )
            convolved = convolved + jnp.dot(
                window, conv_weight[row_tap, col_tap], preferred_element_type=jnp.float32
            )
    hidden = (
        frames.reshape(count * band, channels).astype(jnp.float32) + convolved + conv_bias
    ).astype(jnp.bfloat16)
    rows = lax.axis_size(ROW_PARTS)
    others = [
        lax.ppermute(hidden, ROW_PARTS, [(j, (j + shift) % rows) for j in range(rows)])
        for shift in range(1, rows)
    ]
    every_feature, query, own_key, own_value = staged_gather(
        ref_features, hidden, w_query, w_key, w_value
    )
    sources = others + [every_feature]
    attended = attention(query, own_key, own_value, w_key, w_value, w_out, out_bias, sources, heads)
    return (
        hidden.reshape(count, band_rows, width, channels),
        attended.reshape(count, band_rows, width, channels),
    )


def solution(mesh):
    fine = fine_mesh(mesh)
    blocks = P(TM_PARTS, ROW_PARTS, None, None)
    return jax.shard_map(
        shards,
        mesh=fine,
        in_specs=(blocks, P(), P(), P(TM_PARTS, None), P(), P(), P(), P(), P()),
        out_specs=(blocks, blocks),
        check_vma=False,
    )
```

```python
import functools

import jax
import jax.numpy as jnp
import numpy as np
from jax import lax
from jax.experimental import pallas as pl
from jax.experimental.pallas import tpu as pltpu
from jax.sharding import Mesh
from jax.sharding import PartitionSpec as P

HD = 80


MESH = pl.DeviceIdType.MESH
TM_PARTS = ("y_hi", "x", "z")
ROW_PARTS = ("y_lo", "core")


def distinct(values):
    return len(set(values))


def fine_mesh(mesh):
    devices = np.asarray(mesh.devices)
    tm, rows = devices.shape
    try:
        column = devices[:, 0]
        nx = distinct(d.coords[0] for d in column)
        nz = distinct(d.coords[2] for d in column)
        cores = distinct(d.core_on_chip for d in devices[0])
    except (AttributeError, IndexError, TypeError):
        nx, nz, cores = tm, 1, rows
    if tm % (nx * nz) or rows % cores:
        nx, nz, cores = tm, 1, rows
    shape = (tm // (nx * nz), nx, nz, rows // cores, cores)
    return Mesh(devices.reshape(shape), TM_PARTS + ROW_PARTS)


def staged_kernel(sizes, x_ref, after_ref, out_ref, local_sem, *sems):
    high, across, along = sizes
    half = along // 2
    yh, xx, zz = [lax.axis_index(axis) for axis in TM_PARTS]
    low, core = [lax.axis_index(axis) for axis in ROW_PARTS]
    z_peer = lambda shift: {"z": lax.rem(zz + shift, along)}
    x_peer = lambda shift: {"x": lax.rem(xx + shift, across)}
    y_peer = {"y_hi": 1 - yh, "y_lo": 1 - low}
    c_peer = {"core": 1 - core}
    peers = [z_peer(s) for s in range(1, along)] + [x_peer(s) for s in range(1, across)]
    peers += [y_peer, c_peer]
    barrier = pltpu.get_barrier_semaphore()
    for peer in peers:
        pl.semaphore_signal(barrier, inc=1, device_id=peer, device_id_type=MESH)
    pl.semaphore_wait(barrier, len(peers))

    def block_of(z):
        return ((z // half * high + yh) * across + xx) * half + lax.rem(z, half)

    own = out_ref.at[pl.ds(block_of(zz), 1)]
    mine = zz // half == core

    @pl.when(mine)
    def _():
        local = pltpu.make_async_copy(x_ref, own, local_sem)
        local.start()
        local.wait()

    def remote(ref, peer, send_sem, recv_sem):
        return pltpu.make_async_remote_copy(
            src_ref=ref,
            dst_ref=ref,
            send_sem=send_sem,
            recv_sem=recv_sem,
            device_id=peer,
            device_id_type=MESH,
        )

    z_copies = [remote(own, z_peer(s), sems[0].at[s], sems[1].at[s]) for s in range(1, along)]

    @pl.when(mine)
    def _():
        for copy in z_copies:
            copy.start()
        for copy in z_copies:
            copy.wait_send()

    for s, copy in zip(range(1, along), z_copies):
        sender = lax.rem(zz + along - s, along)

        @pl.when(sender // half == core)
        def _():
            copy.wait_recv()

    def exchange(pairs, send_sem, recv_sem):
        copies = [remote(ref, peer, send_sem.at[i], recv_sem.at[i]) for i, (ref, peer) in enumerate(pairs)]
        for copy in copies:
            copy.start()
        for copy in copies:
            copy.wait()

    group = out_ref.at[pl.ds(((core * high + yh) * across + xx) * half, half)]
    exchange([(group, x_peer(s)) for s in range(1, across)], sems[2], sems[3])
    row = out_ref.at[pl.ds((core * high + yh) * across * half, across * half)]
    exchange([(row, y_peer)], sems[4], sems[5])
    whole = out_ref.at[pl.ds(core * high * across * half, high * across * half)]
    exchange([(whole, c_peer)], sems[6], sems[7])


def staged_gather(value, after):
    sizes = [lax.axis_size(axis) for axis in TM_PARTS]
    total = sizes[0] * sizes[1] * sizes[2]
    sems = []
    for count in (sizes[2], sizes[1], 1, 1):
        sems += [pltpu.SemaphoreType.DMA((count,))] * 2
    gathered = pl.pallas_call(
        functools.partial(staged_kernel, sizes),
        out_shape=jax.ShapeDtypeStruct((total,) + value.shape, value.dtype),
        in_specs=[pl.BlockSpec(memory_space=pl.ANY)] * 2,
        out_specs=pl.BlockSpec(memory_space=pl.ANY),
        scratch_shapes=[pltpu.SemaphoreType.DMA] + sems,
        compiler_params=pltpu.CompilerParams(collective_id=0, has_side_effects=True),
    )(value[None], after)
    return gathered.reshape((total * value.shape[0],) + value.shape[1:])


def extended(value, axis, dim, width):
    size = lax.axis_size(axis)
    length = value.shape[dim]
    up = [(i, i + 1) for i in range(size - 1)]
    down = [(j, i) for i, j in up]
    last = lax.slice_in_dim(value, length - width, length, axis=dim)
    initial = lax.slice_in_dim(value, 0, width, axis=dim)
    before = lax.ppermute(last, axis, up)
    after = lax.ppermute(initial, axis, down)
    return jnp.concatenate([before, value, after], axis=dim)


def attend_block(state, query_heads, keys, values, heads):
    top, total, summed = state
    length = keys.shape[0]
    key_heads = keys.reshape(length, heads, HD)
    value_heads = values.reshape(length, heads, HD)
    scores = jnp.einsum(
        "qhd,khd->hqk", query_heads, key_heads, preferred_element_type=jnp.float32
    )
    scores = scores * HD ** (-0.5)
    block_top = jnp.max(scores, axis=2)
    new_top = block_top if top is None else jnp.maximum(top, block_top)
    weights = jnp.exp(scores - new_top[..., None])
    block_total = jnp.sum(weights, axis=2)
    product = jnp.einsum(
        "hqk,khd->hqd",
        weights.astype(jnp.bfloat16),
        value_heads,
        preferred_element_type=jnp.float32,
    )
    if top is None:
        return (new_top, block_total, product)
    factor = jnp.exp(top - new_top)
    return (new_top, total * factor + block_total, summed * factor[..., None] + product)


def attention_kernel(heads, parts, *refs):
    bias_ref = refs[0]
    weights_in = refs[1:5]
    sources_in = refs[5 : 5 + parts]
    o_ref = refs[5 + parts]
    scratch = refs[6 + parts :]
    wq_ref, wk_ref, wv_ref, wo_ref = scratch[:4]
    sources = scratch[4 : 4 + parts]
    k_ref, v_ref, mixed_ref, q_ref, sems = scratch[4 + parts :]
    pairs = [(sources_in[0], sources[0])] + list(zip(weights_in[:3], (wq_ref, wk_ref, wv_ref)))
    pairs += list(zip(sources_in[1:], sources[1:])) + [(weights_in[3], wo_ref)]
    copies = []
    for index, (src_ref, dst_ref) in enumerate(pairs):
        copy = pltpu.make_async_copy(src_ref, dst_ref, sems.at[index])
        copy.start()
        copies.append(copy)
    for copy in copies[:4]:
        copy.wait()
    q_ref[...] = jnp.dot(
        sources[0][...], wq_ref[...], preferred_element_type=jnp.float32
    ).astype(q_ref.dtype)
    offset = 0
    for index, source in enumerate(sources):
        if index:
            copies[3 + index].wait()
        rows = source.shape[0]
        k_ref[:, offset : offset + rows] = lax.dot_general(
            wk_ref[...], source[...], (((0,), (1,)), ((), ())), preferred_element_type=jnp.float32
        ).astype(k_ref.dtype)
        v_ref[offset : offset + rows, :] = jnp.dot(
            source[...], wv_ref[...], preferred_element_type=jnp.float32
        ).astype(v_ref.dtype)
        offset += rows
    for head in range(heads):
        lanes = slice(head * HD, (head + 1) * HD)
        scores = jnp.dot(q_ref[:, lanes], k_ref[lanes, :], preferred_element_type=jnp.float32)
        scores = scores * HD ** (-0.5)
        top = jnp.max(scores, axis=1, keepdims=True)
        weights = jnp.exp(scores - top)
        total = jnp.sum(weights, axis=1, keepdims=True)
        summed = jnp.dot(
            weights.astype(jnp.bfloat16), v_ref[:, lanes], preferred_element_type=jnp.float32
        )
        mixed_ref[:, lanes] = (summed / total).astype(mixed_ref.dtype)
    copies[-1].wait()
    attended = jnp.dot(mixed_ref[...], wo_ref[...], preferred_element_type=jnp.float32)
    o_ref[...] = (attended + bias_ref[...]).astype(o_ref.dtype)


def attention(w_query, w_key, w_value, w_out, out_bias, sources, heads):
    tokens, channels = sources[0].shape
    length = sum(source.shape[0] for source in sources)
    weights = (w_query, w_key, w_value, w_out)
    operands = (out_bias.reshape(1, -1),) + weights + tuple(sources)
    anywhere = pl.BlockSpec(memory_space=pl.ANY)
    return pl.pallas_call(
        functools.partial(attention_kernel, heads, len(sources)),
        out_shape=jax.ShapeDtypeStruct((tokens, channels), jnp.bfloat16),
        grid=(1,),
        in_specs=[pl.BlockSpec((1, channels), lambda i: (0, 0))] + [anywhere] * (len(operands) - 1),
        out_specs=pl.BlockSpec((tokens, channels), lambda i: (0, 0)),
        scratch_shapes=[pltpu.VMEM(array.shape, array.dtype) for array in operands[1:]]
        + [
            pltpu.VMEM((channels, length), jnp.bfloat16),
            pltpu.VMEM((length, channels), jnp.bfloat16),
            pltpu.VMEM((tokens, channels), jnp.bfloat16),
            pltpu.VMEM((tokens, channels), jnp.bfloat16),
            pltpu.SemaphoreType.DMA((len(operands) - 1,)),
        ],
    )(*operands)


def doubling_gather(value, axis):
    size = lax.axis_size(axis)
    step = 1
    while step < size:
        pairs = [(j, j ^ step) for j in range(size)]
        value = jnp.concatenate([value, lax.ppermute(value, axis, pairs)], axis=0)
        step *= 2
    return value


def shards(frames, conv_weight, conv_bias, ref_features, w_query, w_key, w_value, w_out, out_bias):
    count, band_rows, width, channels = frames.shape
    heads = channels // HD
    band = band_rows * width
    activated = jax.nn.silu(frames.astype(jnp.float32)).astype(jnp.bfloat16)
    padded = extended(activated, ROW_PARTS, 1, 1)
    padded = jnp.pad(padded, ((0, 0), (0, 0), (1, 1), (0, 0)))
    convolved = jnp.zeros((count * band, channels), jnp.float32)
    for row_tap in range(3):
        for col_tap in range(3):
            window = padded[:, row_tap : row_tap + band_rows, col_tap : col_tap + width].reshape(
                count * band, channels
            )
            convolved = convolved + jnp.dot(
                window, conv_weight[row_tap, col_tap], preferred_element_type=jnp.float32
            )
    hidden = (
        frames.reshape(count * band, channels).astype(jnp.float32) + convolved + conv_bias
    ).astype(jnp.bfloat16)
    rows = lax.axis_size(ROW_PARTS)
    others = [
        lax.ppermute(hidden, ROW_PARTS, [(j, (j + shift) % rows) for j in range(rows)])
        for shift in range(1, rows)
    ]
    every_feature = staged_gather(ref_features, hidden)
    sources = [hidden] + others + [every_feature]
    attended = attention(w_query, w_key, w_value, w_out, out_bias, sources, heads)
    return (
        hidden.reshape(count, band_rows, width, channels),
        attended.reshape(count, band_rows, width, channels),
    )


def solution(mesh):
    fine = fine_mesh(mesh)
    blocks = P(TM_PARTS, ROW_PARTS, None, None)
    return jax.shard_map(
        shards,
        mesh=fine,
        in_specs=(blocks, P(), P(), P(TM_PARTS, None), P(), P(), P(), P(), P()),
        out_specs=(blocks, blocks),
        check_vma=False,
    )
```

```python
import functools

import jax
import jax.numpy as jnp
import numpy as np
from jax import lax
from jax.experimental import pallas as pl
from jax.experimental.pallas import tpu as pltpu
from jax.sharding import Mesh
from jax.sharding import PartitionSpec as P

HD = 80


MESH = pl.DeviceIdType.MESH
TM_PARTS = ("y_hi", "x", "z")
ROW_PARTS = ("y_lo", "core")


def distinct(values):
    return len(set(values))


def fine_mesh(mesh):
    devices = np.asarray(mesh.devices)
    tm, rows = devices.shape
    try:
        column = devices[:, 0]
        nx = distinct(d.coords[0] for d in column)
        nz = distinct(d.coords[2] for d in column)
        cores = distinct(d.core_on_chip for d in devices[0])
    except (AttributeError, IndexError, TypeError):
        nx, nz, cores = tm, 1, rows
    if tm % (nx * nz) or rows % cores:
        nx, nz, cores = tm, 1, rows
    shape = (tm // (nx * nz), nx, nz, rows // cores, cores)
    return Mesh(devices.reshape(shape), TM_PARTS + ROW_PARTS)


def staged_kernel(sizes, x_ref, after_ref, out_ref, local_sem, *sems):
    high, across, along = sizes
    half = along // 2
    yh, xx, zz = [lax.axis_index(axis) for axis in TM_PARTS]
    low, core = [lax.axis_index(axis) for axis in ROW_PARTS]
    z_peer = lambda shift: {"z": lax.rem(zz + shift, along)}
    x_peer = lambda shift: {"x": lax.rem(xx + shift, across)}
    y_peer = {"y_hi": 1 - yh, "y_lo": 1 - low}
    c_peer = {"core": 1 - core}
    peers = [z_peer(s) for s in range(1, along)] + [x_peer(s) for s in range(1, across)]
    peers += [y_peer, c_peer]
    barrier = pltpu.get_barrier_semaphore()
    for peer in peers:
        pl.semaphore_signal(barrier, inc=1, device_id=peer, device_id_type=MESH)
    pl.semaphore_wait(barrier, len(peers))

    def block_of(z):
        return ((z // half * high + yh) * across + xx) * half + lax.rem(z, half)

    own = out_ref.at[pl.ds(block_of(zz), 1)]
    mine = zz // half == core

    @pl.when(mine)
    def _():
        local = pltpu.make_async_copy(x_ref, own, local_sem)
        local.start()
        local.wait()

    def remote(ref, peer, send_sem, recv_sem):
        return pltpu.make_async_remote_copy(
            src_ref=ref,
            dst_ref=ref,
            send_sem=send_sem,
            recv_sem=recv_sem,
            device_id=peer,
            device_id_type=MESH,
        )

    z_copies = [remote(own, z_peer(s), sems[0].at[s], sems[1].at[s]) for s in range(1, along)]

    @pl.when(mine)
    def _():
        for copy in z_copies:
            copy.start()
        for copy in z_copies:
            copy.wait_send()

    for s, copy in zip(range(1, along), z_copies):
        sender = lax.rem(zz + along - s, along)

        @pl.when(sender // half == core)
        def _():
            copy.wait_recv()

    def exchange(pairs, send_sem, recv_sem):
        copies = [remote(ref, peer, send_sem.at[i], recv_sem.at[i]) for i, (ref, peer) in enumerate(pairs)]
        for copy in copies:
            copy.start()
        for copy in copies:
            copy.wait()

    group = out_ref.at[pl.ds(((core * high + yh) * across + xx) * half, half)]
    exchange([(group, x_peer(s)) for s in range(1, across)], sems[2], sems[3])
    row = out_ref.at[pl.ds((core * high + yh) * across * half, across * half)]
    exchange([(row, y_peer)], sems[4], sems[5])
    whole = out_ref.at[pl.ds(core * high * across * half, high * across * half)]
    exchange([(whole, c_peer)], sems[6], sems[7])


def staged_gather(value, after):
    sizes = [lax.axis_size(axis) for axis in TM_PARTS]
    total = sizes[0] * sizes[1] * sizes[2]
    sems = []
    for count in (sizes[2], sizes[1], 1, 1):
        sems += [pltpu.SemaphoreType.DMA((count,))] * 2
    gathered = pl.pallas_call(
        functools.partial(staged_kernel, sizes),
        out_shape=jax.ShapeDtypeStruct((total,) + value.shape, value.dtype),
        in_specs=[pl.BlockSpec(memory_space=pl.ANY)] * 2,
        out_specs=pl.BlockSpec(memory_space=pl.ANY),
        scratch_shapes=[pltpu.SemaphoreType.DMA] + sems,
        compiler_params=pltpu.CompilerParams(collective_id=0, has_side_effects=True),
    )(value[None], after)
    return gathered.reshape((total * value.shape[0],) + value.shape[1:])


def extended(value, axis, dim, width):
    size = lax.axis_size(axis)
    length = value.shape[dim]
    up = [(i, i + 1) for i in range(size - 1)]
    down = [(j, i) for i, j in up]
    last = lax.slice_in_dim(value, length - width, length, axis=dim)
    initial = lax.slice_in_dim(value, 0, width, axis=dim)
    before = lax.ppermute(last, axis, up)
    after = lax.ppermute(initial, axis, down)
    return jnp.concatenate([before, value, after], axis=dim)


def attend_block(state, query_heads, keys, values, heads):
    top, total, summed = state
    length = keys.shape[0]
    key_heads = keys.reshape(length, heads, HD)
    value_heads = values.reshape(length, heads, HD)
    scores = jnp.einsum(
        "qhd,khd->hqk", query_heads, key_heads, preferred_element_type=jnp.float32
    )
    scores = scores * HD ** (-0.5)
    block_top = jnp.max(scores, axis=2)
    new_top = block_top if top is None else jnp.maximum(top, block_top)
    weights = jnp.exp(scores - new_top[..., None])
    block_total = jnp.sum(weights, axis=2)
    product = jnp.einsum(
        "hqk,khd->hqd",
        weights.astype(jnp.bfloat16),
        value_heads,
        preferred_element_type=jnp.float32,
    )
    if top is None:
        return (new_top, block_total, product)
    factor = jnp.exp(top - new_top)
    return (new_top, total * factor + block_total, summed * factor[..., None] + product)


def attention_kernel(heads, parts, *refs):
    wq_ref, wk_ref, wv_ref, wo_ref, bias_ref = refs[:5]
    sources = refs[5 : 5 + parts]
    o_ref, k_ref, v_ref, mixed_ref, q_ref = refs[5 + parts :]
    q_ref[...] = jnp.dot(
        sources[0][...], wq_ref[...], preferred_element_type=jnp.float32
    ).astype(q_ref.dtype)
    offset = 0
    key_weight = jnp.transpose(wk_ref[...])
    for source in sources:
        rows = source.shape[0]
        k_ref[:, offset : offset + rows] = lax.dot_general(
            key_weight, source[...], (((1,), (1,)), ((), ())), preferred_element_type=jnp.float32
        ).astype(k_ref.dtype)
        v_ref[offset : offset + rows, :] = jnp.dot(
            source[...], wv_ref[...], preferred_element_type=jnp.float32
        ).astype(v_ref.dtype)
        offset += rows
    for head in range(heads):
        lanes = slice(head * HD, (head + 1) * HD)
        scores = jnp.dot(q_ref[:, lanes], k_ref[lanes, :], preferred_element_type=jnp.float32)
        scores = scores * HD ** (-0.5)
        top = jnp.max(scores, axis=1, keepdims=True)
        weights = jnp.exp(scores - top)
        total = jnp.sum(weights, axis=1, keepdims=True)
        summed = jnp.dot(
            weights.astype(jnp.bfloat16), v_ref[:, lanes], preferred_element_type=jnp.float32
        )
        mixed_ref[:, lanes] = (summed / total).astype(mixed_ref.dtype)
    attended = jnp.dot(mixed_ref[...], wo_ref[...], preferred_element_type=jnp.float32)
    o_ref[...] = (attended + bias_ref[...]).astype(o_ref.dtype)


def attention(w_query, w_key, w_value, w_out, out_bias, sources, heads):
    tokens, channels = sources[0].shape
    length = sum(source.shape[0] for source in sources)
    whole = lambda array: pl.BlockSpec(array.shape, lambda i: (0, 0))
    operands = (w_query, w_key, w_value, w_out, out_bias.reshape(1, -1)) + tuple(sources)
    return pl.pallas_call(
        functools.partial(attention_kernel, heads, len(sources)),
        out_shape=jax.ShapeDtypeStruct((tokens, channels), jnp.bfloat16),
        grid=(1,),
        in_specs=[whole(array) for array in operands],
        out_specs=pl.BlockSpec((tokens, channels), lambda i: (0, 0)),
        scratch_shapes=[
            pltpu.VMEM((channels, length), jnp.bfloat16),
            pltpu.VMEM((length, channels), jnp.bfloat16),
            pltpu.VMEM((tokens, channels), jnp.bfloat16),
            pltpu.VMEM((tokens, channels), jnp.bfloat16),
        ],
    )(*operands)


def doubling_gather(value, axis):
    size = lax.axis_size(axis)
    step = 1
    while step < size:
        pairs = [(j, j ^ step) for j in range(size)]
        value = jnp.concatenate([value, lax.ppermute(value, axis, pairs)], axis=0)
        step *= 2
    return value


def shards(frames, conv_weight, conv_bias, ref_features, w_query, w_key, w_value, w_out, out_bias):
    count, band_rows, width, channels = frames.shape
    heads = channels // HD
    band = band_rows * width
    activated = jax.nn.silu(frames.astype(jnp.float32)).astype(jnp.bfloat16)
    padded = extended(activated, ROW_PARTS, 1, 1)
    padded = jnp.pad(padded, ((0, 0), (0, 0), (1, 1), (0, 0)))
    convolved = jnp.zeros((count * band, channels), jnp.float32)
    for row_tap in range(3):
        for col_tap in range(3):
            window = padded[:, row_tap : row_tap + band_rows, col_tap : col_tap + width].reshape(
                count * band, channels
            )
            convolved = convolved + jnp.dot(
                window, conv_weight[row_tap, col_tap], preferred_element_type=jnp.float32
            )
    hidden = (
        frames.reshape(count * band, channels).astype(jnp.float32) + convolved + conv_bias
    ).astype(jnp.bfloat16)
    rows = lax.axis_size(ROW_PARTS)
    others = [
        lax.ppermute(hidden, ROW_PARTS, [(j, (j + shift) % rows) for j in range(rows)])
        for shift in range(1, rows)
    ]
    every_feature = staged_gather(ref_features, hidden)
    sources = [hidden] + others + [every_feature]
    attended = attention(w_query, w_key, w_value, w_out, out_bias, sources, heads)
    return (
        hidden.reshape(count, band_rows, width, channels),
        attended.reshape(count, band_rows, width, channels),
    )


def solution(mesh):
    fine = fine_mesh(mesh)
    blocks = P(TM_PARTS, ROW_PARTS, None, None)
    return jax.shard_map(
        shards,
        mesh=fine,
        in_specs=(blocks, P(), P(), P(TM_PARTS, None), P(), P(), P(), P(), P()),
        out_specs=(blocks, blocks),
        check_vma=False,
    )
```

```python
import functools

import jax
import jax.numpy as jnp
import numpy as np
from jax import lax
from jax.experimental import pallas as pl
from jax.experimental.pallas import tpu as pltpu
from jax.sharding import Mesh
from jax.sharding import PartitionSpec as P

HD = 80


MESH = pl.DeviceIdType.MESH
TM_PARTS = ("y_hi", "x", "z")
ROW_PARTS = ("y_lo", "core")


def distinct(values):
    return len(set(values))


def fine_mesh(mesh):
    devices = np.asarray(mesh.devices)
    tm, rows = devices.shape
    try:
        column = devices[:, 0]
        nx = distinct(d.coords[0] for d in column)
        nz = distinct(d.coords[2] for d in column)
        cores = distinct(d.core_on_chip for d in devices[0])
    except (AttributeError, IndexError, TypeError):
        nx, nz, cores = tm, 1, rows
    if tm % (nx * nz) or rows % cores:
        nx, nz, cores = tm, 1, rows
    shape = (tm // (nx * nz), nx, nz, rows // cores, cores)
    return Mesh(devices.reshape(shape), TM_PARTS + ROW_PARTS)


def staged_kernel(sizes, x_ref, after_ref, out_ref, local_sem, *sems):
    high, across, along = sizes
    half = along // 2
    yh, xx, zz = [lax.axis_index(axis) for axis in TM_PARTS]
    low, core = [lax.axis_index(axis) for axis in ROW_PARTS]
    z_peer = lambda shift: {"z": lax.rem(zz + shift, along)}
    x_peer = lambda shift: {"x": lax.rem(xx + shift, across)}
    y_peer = {"y_hi": 1 - yh, "y_lo": 1 - low}
    c_peer = {"core": 1 - core}
    peers = [z_peer(s) for s in range(1, along)] + [x_peer(s) for s in range(1, across)]
    peers += [y_peer, c_peer]
    barrier = pltpu.get_barrier_semaphore()
    for peer in peers:
        pl.semaphore_signal(barrier, inc=1, device_id=peer, device_id_type=MESH)
    pl.semaphore_wait(barrier, len(peers))

    def block_of(z):
        return ((z // half * high + yh) * across + xx) * half + lax.rem(z, half)

    own = out_ref.at[pl.ds(block_of(zz), 1)]
    mine = zz // half == core

    @pl.when(mine)
    def _():
        local = pltpu.make_async_copy(x_ref, own, local_sem)
        local.start()
        local.wait()

    def remote(ref, peer, send_sem, recv_sem):
        return pltpu.make_async_remote_copy(
            src_ref=ref,
            dst_ref=ref,
            send_sem=send_sem,
            recv_sem=recv_sem,
            device_id=peer,
            device_id_type=MESH,
        )

    z_copies = [remote(own, z_peer(s), sems[0].at[s], sems[1].at[s]) for s in range(1, along)]

    @pl.when(mine)
    def _():
        for copy in z_copies:
            copy.start()
        for copy in z_copies:
            copy.wait_send()

    for s, copy in zip(range(1, along), z_copies):
        sender = lax.rem(zz + along - s, along)

        @pl.when(sender // half == core)
        def _():
            copy.wait_recv()

    def exchange(pairs, send_sem, recv_sem):
        copies = [remote(ref, peer, send_sem.at[i], recv_sem.at[i]) for i, (ref, peer) in enumerate(pairs)]
        for copy in copies:
            copy.start()
        for copy in copies:
            copy.wait()

    group = out_ref.at[pl.ds(((core * high + yh) * across + xx) * half, half)]
    exchange([(group, x_peer(s)) for s in range(1, across)], sems[2], sems[3])
    row = out_ref.at[pl.ds((core * high + yh) * across * half, across * half)]
    exchange([(row, y_peer)], sems[4], sems[5])
    whole = out_ref.at[pl.ds(core * high * across * half, high * across * half)]
    exchange([(whole, c_peer)], sems[6], sems[7])


def staged_gather(value, after):
    sizes = [lax.axis_size(axis) for axis in TM_PARTS]
    total = sizes[0] * sizes[1] * sizes[2]
    sems = []
    for count in (sizes[2], sizes[1], 1, 1):
        sems += [pltpu.SemaphoreType.DMA((count,))] * 2
    gathered = pl.pallas_call(
        functools.partial(staged_kernel, sizes),
        out_shape=jax.ShapeDtypeStruct((total,) + value.shape, value.dtype),
        in_specs=[pl.BlockSpec(memory_space=pl.ANY)] * 2,
        out_specs=pl.BlockSpec(memory_space=pl.ANY),
        scratch_shapes=[pltpu.SemaphoreType.DMA] + sems,
        compiler_params=pltpu.CompilerParams(collective_id=0, has_side_effects=True),
    )(value[None], after)
    return gathered


def extended(value, axis, dim, width):
    size = lax.axis_size(axis)
    length = value.shape[dim]
    up = [(i, i + 1) for i in range(size - 1)]
    down = [(j, i) for i, j in up]
    last = lax.slice_in_dim(value, length - width, length, axis=dim)
    initial = lax.slice_in_dim(value, 0, width, axis=dim)
    before = lax.ppermute(last, axis, up)
    after = lax.ppermute(initial, axis, down)
    return jnp.concatenate([before, value, after], axis=dim)


def attend_block(state, query_heads, keys, values, heads):
    top, total, summed = state
    length = keys.shape[0]
    key_heads = keys.reshape(length, heads, HD)
    value_heads = values.reshape(length, heads, HD)
    scores = jnp.einsum(
        "qhd,khd->hqk", query_heads, key_heads, preferred_element_type=jnp.float32
    )
    scores = scores * HD ** (-0.5)
    block_top = jnp.max(scores, axis=2)
    new_top = block_top if top is None else jnp.maximum(top, block_top)
    weights = jnp.exp(scores - new_top[..., None])
    block_total = jnp.sum(weights, axis=2)
    product = jnp.einsum(
        "hqk,khd->hqd",
        weights.astype(jnp.bfloat16),
        value_heads,
        preferred_element_type=jnp.float32,
    )
    if top is None:
        return (new_top, block_total, product)
    factor = jnp.exp(top - new_top)
    return (new_top, total * factor + block_total, summed * factor[..., None] + product)


def attention_kernel(heads, parts, *refs):
    wq_ref, wk_ref, wv_ref, wo_ref, bias_ref = refs[:5]
    sources = refs[5 : 5 + parts]
    o_ref, k_ref, v_ref, mixed_ref, q_ref = refs[5 + parts :]
    q_ref[...] = jnp.dot(
        sources[0][...], wq_ref[...], preferred_element_type=jnp.float32
    ).astype(q_ref.dtype)
    offset = 0
    for source_ref in sources:
        source = source_ref[...]
        source = source.reshape(-1, source.shape[-1])
        rows = source.shape[0]
        k_ref[:, offset : offset + rows] = lax.dot_general(
            wk_ref[...], source, (((0,), (1,)), ((), ())), preferred_element_type=jnp.float32
        ).astype(k_ref.dtype)
        v_ref[offset : offset + rows, :] = jnp.dot(
            source, wv_ref[...], preferred_element_type=jnp.float32
        ).astype(v_ref.dtype)
        offset += rows
    for head in range(heads):
        lanes = slice(head * HD, (head + 1) * HD)
        scores = jnp.dot(q_ref[:, lanes], k_ref[lanes, :], preferred_element_type=jnp.float32)
        scores = scores * HD ** (-0.5)
        top = jnp.max(scores, axis=1, keepdims=True)
        weights = jnp.exp(scores - top)
        total = jnp.sum(weights, axis=1, keepdims=True)
        summed = jnp.dot(
            weights.astype(jnp.bfloat16), v_ref[:, lanes], preferred_element_type=jnp.float32
        )
        mixed_ref[:, lanes] = (summed / total).astype(mixed_ref.dtype)
    attended = jnp.dot(mixed_ref[...], wo_ref[...], preferred_element_type=jnp.float32)
    o_ref[...] = (attended + bias_ref[...]).astype(o_ref.dtype)


def attention(w_query, w_key, w_value, w_out, out_bias, sources, heads):
    tokens, channels = sources[0].shape
    length = sum(source.size // channels for source in sources)
    whole = lambda array: pl.BlockSpec(array.shape, lambda i: (0,) * array.ndim)
    operands = (w_query, w_key, w_value, w_out, out_bias.reshape(1, -1)) + tuple(sources)
    return pl.pallas_call(
        functools.partial(attention_kernel, heads, len(sources)),
        out_shape=jax.ShapeDtypeStruct((tokens, channels), jnp.bfloat16),
        grid=(1,),
        in_specs=[whole(array) for array in operands],
        out_specs=pl.BlockSpec((tokens, channels), lambda i: (0, 0)),
        scratch_shapes=[
            pltpu.VMEM((channels, length), jnp.bfloat16),
            pltpu.VMEM((length, channels), jnp.bfloat16),
            pltpu.VMEM((tokens, channels), jnp.bfloat16),
            pltpu.VMEM((tokens, channels), jnp.bfloat16),
        ],
    )(*operands)


def doubling_gather(value, axis):
    size = lax.axis_size(axis)
    step = 1
    while step < size:
        pairs = [(j, j ^ step) for j in range(size)]
        value = jnp.concatenate([value, lax.ppermute(value, axis, pairs)], axis=0)
        step *= 2
    return value


def shards(frames, conv_weight, conv_bias, ref_features, w_query, w_key, w_value, w_out, out_bias):
    count, band_rows, width, channels = frames.shape
    heads = channels // HD
    band = band_rows * width
    activated = jax.nn.silu(frames.astype(jnp.float32)).astype(jnp.bfloat16)
    padded = extended(activated, ROW_PARTS, 1, 1)
    padded = jnp.pad(padded, ((0, 0), (0, 0), (1, 1), (0, 0)))
    convolved = jnp.zeros((count * band, channels), jnp.float32)
    for row_tap in range(3):
        for col_tap in range(3):
            window = padded[:, row_tap : row_tap + band_rows, col_tap : col_tap + width].reshape(
                count * band, channels
            )
            convolved = convolved + jnp.dot(
                window, conv_weight[row_tap, col_tap], preferred_element_type=jnp.float32
            )
    hidden = (
        frames.reshape(count * band, channels).astype(jnp.float32) + convolved + conv_bias
    ).astype(jnp.bfloat16)
    rows = lax.axis_size(ROW_PARTS)
    others = [
        lax.ppermute(hidden, ROW_PARTS, [(j, (j + shift) % rows) for j in range(rows)])
        for shift in range(1, rows)
    ]
    every_feature = staged_gather(ref_features, hidden)
    sources = [hidden] + others + [every_feature]
    attended = attention(w_query, w_key, w_value, w_out, out_bias, sources, heads)
    return (
        hidden.reshape(count, band_rows, width, channels),
        attended.reshape(count, band_rows, width, channels),
    )


def solution(mesh):
    fine = fine_mesh(mesh)
    blocks = P(TM_PARTS, ROW_PARTS, None, None)
    return jax.shard_map(
        shards,
        mesh=fine,
        in_specs=(blocks, P(), P(), P(TM_PARTS, None), P(), P(), P(), P(), P()),
        out_specs=(blocks, blocks),
        check_vma=False,
    )
```

```python
import functools

import jax
import jax.numpy as jnp
import numpy as np
from jax import lax
from jax.experimental import pallas as pl
from jax.experimental.pallas import tpu as pltpu
from jax.sharding import Mesh
from jax.sharding import PartitionSpec as P

HD = 80


MESH = pl.DeviceIdType.MESH
TM_PARTS = ("y_hi", "x", "z")
ROW_PARTS = ("y_lo", "core")


def distinct(values):
    return len(set(values))


def fine_mesh(mesh):
    devices = np.asarray(mesh.devices)
    tm, rows = devices.shape
    try:
        column = devices[:, 0]
        nx = distinct(d.coords[0] for d in column)
        nz = distinct(d.coords[2] for d in column)
        cores = distinct(d.core_on_chip for d in devices[0])
    except (AttributeError, IndexError, TypeError):
        nx, nz, cores = tm, 1, rows
    if tm % (nx * nz) or rows % cores:
        nx, nz, cores = tm, 1, rows
    shape = (tm // (nx * nz), nx, nz, rows // cores, cores)
    return Mesh(devices.reshape(shape), TM_PARTS + ROW_PARTS)


def staged_kernel(sizes, x_ref, after_ref, out_ref, local_sem, *sems):
    high, across, along = sizes
    half = along // 2
    yh, xx, zz = [lax.axis_index(axis) for axis in TM_PARTS]
    low, core = [lax.axis_index(axis) for axis in ROW_PARTS]
    z_peer = lambda shift: {"z": lax.rem(zz + shift, along)}
    x_peer = lambda shift: {"x": lax.rem(xx + shift, across)}
    y_peer = {"y_hi": 1 - yh, "y_lo": 1 - low}
    c_peer = {"core": 1 - core}
    peers = [z_peer(s) for s in range(1, along)] + [x_peer(s) for s in range(1, across)]
    peers += [y_peer, c_peer]
    barrier = pltpu.get_barrier_semaphore()
    for peer in peers:
        pl.semaphore_signal(barrier, inc=1, device_id=peer, device_id_type=MESH)
    pl.semaphore_wait(barrier, len(peers))

    def block_of(z):
        return ((z // half * high + yh) * across + xx) * half + lax.rem(z, half)

    own = out_ref.at[pl.ds(block_of(zz), 1)]
    mine = zz // half == core

    local = pltpu.make_async_copy(x_ref, own, local_sem)

    def remote(ref, peer, send_sem, recv_sem, source=None):
        return pltpu.make_async_remote_copy(
            src_ref=ref if source is None else source,
            dst_ref=ref,
            send_sem=send_sem,
            recv_sem=recv_sem,
            device_id=peer,
            device_id_type=MESH,
        )

    z_copies = [
        remote(own, z_peer(s), sems[0].at[s], sems[1].at[s], x_ref) for s in range(1, along)
    ]

    @pl.when(mine)
    def _():
        for copy in z_copies:
            copy.start()
        local.start()
        local.wait()
        for copy in z_copies:
            copy.wait_send()

    for s, copy in zip(range(1, along), z_copies):
        sender = lax.rem(zz + along - s, along)

        @pl.when(sender // half == core)
        def _():
            copy.wait_recv()

    def exchange(pairs, send_sem, recv_sem):
        copies = [remote(ref, peer, send_sem.at[i], recv_sem.at[i]) for i, (ref, peer) in enumerate(pairs)]
        for copy in copies:
            copy.start()
        for copy in copies:
            copy.wait()

    group = out_ref.at[pl.ds(((core * high + yh) * across + xx) * half, half)]
    exchange([(group, x_peer(s)) for s in range(1, across)], sems[2], sems[3])
    row = out_ref.at[pl.ds((core * high + yh) * across * half, across * half)]
    exchange([(row, y_peer)], sems[4], sems[5])
    whole = out_ref.at[pl.ds(core * high * across * half, high * across * half)]
    exchange([(whole, c_peer)], sems[6], sems[7])


def staged_gather(value, after):
    sizes = [lax.axis_size(axis) for axis in TM_PARTS]
    total = sizes[0] * sizes[1] * sizes[2]
    sems = []
    for count in (sizes[2], sizes[1], 1, 1):
        sems += [pltpu.SemaphoreType.DMA((count,))] * 2
    gathered = pl.pallas_call(
        functools.partial(staged_kernel, sizes),
        out_shape=jax.ShapeDtypeStruct((total,) + value.shape, value.dtype),
        in_specs=[pl.BlockSpec(memory_space=pl.ANY)] * 2,
        out_specs=pl.BlockSpec(memory_space=pl.ANY),
        scratch_shapes=[pltpu.SemaphoreType.DMA] + sems,
        compiler_params=pltpu.CompilerParams(collective_id=0, has_side_effects=True),
    )(value[None], after)
    return gathered.reshape((total * value.shape[0],) + value.shape[1:])


def extended(value, axis, dim, width):
    size = lax.axis_size(axis)
    length = value.shape[dim]
    up = [(i, i + 1) for i in range(size - 1)]
    down = [(j, i) for i, j in up]
    last = lax.slice_in_dim(value, length - width, length, axis=dim)
    initial = lax.slice_in_dim(value, 0, width, axis=dim)
    before = lax.ppermute(last, axis, up)
    after = lax.ppermute(initial, axis, down)
    return jnp.concatenate([before, value, after], axis=dim)


def attend_block(state, query_heads, keys, values, heads):
    top, total, summed = state
    length = keys.shape[0]
    key_heads = keys.reshape(length, heads, HD)
    value_heads = values.reshape(length, heads, HD)
    scores = jnp.einsum(
        "qhd,khd->hqk", query_heads, key_heads, preferred_element_type=jnp.float32
    )
    scores = scores * HD ** (-0.5)
    block_top = jnp.max(scores, axis=2)
    new_top = block_top if top is None else jnp.maximum(top, block_top)
    weights = jnp.exp(scores - new_top[..., None])
    block_total = jnp.sum(weights, axis=2)
    product = jnp.einsum(
        "hqk,khd->hqd",
        weights.astype(jnp.bfloat16),
        value_heads,
        preferred_element_type=jnp.float32,
    )
    if top is None:
        return (new_top, block_total, product)
    factor = jnp.exp(top - new_top)
    return (new_top, total * factor + block_total, summed * factor[..., None] + product)


def attention_kernel(heads, parts, *refs):
    wq_ref, wk_ref, wv_ref, wo_ref, bias_ref = refs[:5]
    sources = refs[5 : 5 + parts]
    o_ref, k_ref, v_ref, mixed_ref, q_ref = refs[5 + parts :]
    q_ref[...] = jnp.dot(
        sources[0][...], wq_ref[...], preferred_element_type=jnp.float32
    ).astype(q_ref.dtype)
    offset = 0
    for source in sources:
        rows = source.shape[0]
        k_ref[:, offset : offset + rows] = lax.dot_general(
            wk_ref[...], source[...], (((0,), (1,)), ((), ())), preferred_element_type=jnp.float32
        ).astype(k_ref.dtype)
        v_ref[offset : offset + rows, :] = jnp.dot(
            source[...], wv_ref[...], preferred_element_type=jnp.float32
        ).astype(v_ref.dtype)
        offset += rows
    for head in range(heads):
        lanes = slice(head * HD, (head + 1) * HD)
        scores = jnp.dot(q_ref[:, lanes], k_ref[lanes, :], preferred_element_type=jnp.float32)
        scores = scores * HD ** (-0.5)
        top = jnp.max(scores, axis=1, keepdims=True)
        weights = jnp.exp(scores - top)
        total = jnp.sum(weights, axis=1, keepdims=True)
        summed = jnp.dot(
            weights.astype(jnp.bfloat16), v_ref[:, lanes], preferred_element_type=jnp.float32
        )
        mixed_ref[:, lanes] = (summed / total).astype(mixed_ref.dtype)
    attended = jnp.dot(mixed_ref[...], wo_ref[...], preferred_element_type=jnp.float32)
    o_ref[...] = (attended + bias_ref[...]).astype(o_ref.dtype)


def attention(w_query, w_key, w_value, w_out, out_bias, sources, heads):
    tokens, channels = sources[0].shape
    length = sum(source.shape[0] for source in sources)
    whole = lambda array: pl.BlockSpec(array.shape, lambda i: (0, 0))
    operands = (w_query, w_key, w_value, w_out, out_bias.reshape(1, -1)) + tuple(sources)
    return pl.pallas_call(
        functools.partial(attention_kernel, heads, len(sources)),
        out_shape=jax.ShapeDtypeStruct((tokens, channels), jnp.bfloat16),
        grid=(1,),
        in_specs=[whole(array) for array in operands],
        out_specs=pl.BlockSpec((tokens, channels), lambda i: (0, 0)),
        scratch_shapes=[
            pltpu.VMEM((channels, length), jnp.bfloat16),
            pltpu.VMEM((length, channels), jnp.bfloat16),
            pltpu.VMEM((tokens, channels), jnp.bfloat16),
            pltpu.VMEM((tokens, channels), jnp.bfloat16),
        ],
    )(*operands)


def doubling_gather(value, axis):
    size = lax.axis_size(axis)
    step = 1
    while step < size:
        pairs = [(j, j ^ step) for j in range(size)]
        value = jnp.concatenate([value, lax.ppermute(value, axis, pairs)], axis=0)
        step *= 2
    return value


def shards(frames, conv_weight, conv_bias, ref_features, w_query, w_key, w_value, w_out, out_bias):
    count, band_rows, width, channels = frames.shape
    heads = channels // HD
    band = band_rows * width
    activated = jax.nn.silu(frames.astype(jnp.float32)).astype(jnp.bfloat16)
    padded = extended(activated, ROW_PARTS, 1, 1)
    padded = jnp.pad(padded, ((0, 0), (0, 0), (1, 1), (0, 0)))
    convolved = jnp.zeros((count * band, channels), jnp.float32)
    for row_tap in range(3):
        for col_tap in range(3):
            window = padded[:, row_tap : row_tap + band_rows, col_tap : col_tap + width].reshape(
                count * band, channels
            )
            convolved = convolved + jnp.dot(
                window, conv_weight[row_tap, col_tap], preferred_element_type=jnp.float32
            )
    hidden = (
        frames.reshape(count * band, channels).astype(jnp.float32) + convolved + conv_bias
    ).astype(jnp.bfloat16)
    rows = lax.axis_size(ROW_PARTS)
    others = [
        lax.ppermute(hidden, ROW_PARTS, [(j, (j + shift) % rows) for j in range(rows)])
        for shift in range(1, rows)
    ]
    every_feature = staged_gather(ref_features, hidden)
    sources = [hidden] + others + [every_feature]
    attended = attention(w_query, w_key, w_value, w_out, out_bias, sources, heads)
    return (
        hidden.reshape(count, band_rows, width, channels),
        attended.reshape(count, band_rows, width, channels),
    )


def solution(mesh):
    fine = fine_mesh(mesh)
    blocks = P(TM_PARTS, ROW_PARTS, None, None)
    return jax.shard_map(
        shards,
        mesh=fine,
        in_specs=(blocks, P(), P(), P(TM_PARTS, None), P(), P(), P(), P(), P()),
        out_specs=(blocks, blocks),
        check_vma=False,
    )
```
